32 devices in a mesh: dp: 4 (over y, core), fsdp: 8 (over z, x).
Axes of the slice: x: 2, y: 2, z: 4, core: 2. Of those that a mesh axis runs over, the one named last changes fastest.
Arguments:
- tokens: bfloat16 [32, 1024, 512], P(('dp', 'fsdp')), may hold values from -6 to 6
- cotangent: bfloat16 [32, 1024, 512], P(('dp', 'fsdp')), may hold values from -6 to 6
- dataset_ids: int32 [32], P(('dp', 'fsdp')), may hold values from 0 to 7
- query_counts: int32 [32], P(('dp', 'fsdp')), may hold values from 1 to 128
- learn_rate: float32 [1], replicated, may hold values from 0.0002762136 to 0.00082864077
- momentum_coef: float32 [1], replicated, may hold values from 0.4 to 0.6
- average_decay: float32 [1], replicated, may hold values from 0.2 to 0.95
- step_count: int32 [1], replicated, may hold values from 2 to 20
- attend_weight: float32 [2, 512, 1536], P(None, ('dp', 'fsdp')), may hold values from -0.25 to 0.25
- attend_momentum: float32 [2, 512, 1536], P(None, ('dp', 'fsdp')), may hold values from -112 to 112
- attend_average: float32 [2, 512, 1536], P(None, ('dp', 'fsdp')), may hold values from -0.25 to 0.25
- output_weight: float32 [2, 512, 512], P(None, ('dp', 'fsdp')), may hold values from -1.5 to 1.5
- output_momentum: float32 [2, 512, 512], P(None, ('dp', 'fsdp')), may hold values from -20 to 20
- output_average: float32 [2, 512, 512], P(None, ('dp', 'fsdp')), may hold values from -1.5 to 1.5
- expand_weight: float32 [2, 512, 1024], P(None, ('dp', 'fsdp')), may hold values from -0.25 to 0.25
- expand_momentum: float32 [2, 512, 1024], P(None, ('dp', 'fsdp')), may hold values from -320 to 320
- expand_average: float32 [2, 512, 1024], P(None, ('dp', 'fsdp')), may hold values from -0.25 to 0.25
- shrink_weight: float32 [2, 1024, 512], P(None, ('dp', 'fsdp')), may hold values from -0.1875 to 0.1875
- shrink_momentum: float32 [2, 1024, 512], P(None, ('dp', 'fsdp')), may hold values from -320 to 320
- shrink_average: float32 [2, 1024, 512], P(None, ('dp', 'fsdp')), may hold values from -0.1875 to 0.1875
- norm_gains: float32 [2, 2, 512], P(None, None, ('dp', 'fsdp')), may hold values from 0.5 to 1.5
- gains_momentum: float32 [2, 2, 512], P(None, None, ('dp', 'fsdp')), may hold values from -320 to 320
- gains_average: float32 [2, 2, 512], P(None, None, ('dp', 'fsdp')), may hold values from 0.5 to 1.5
- bias_rows: float32 [2, 8, 512], P(None, None, ('dp', 'fsdp')), may hold values from -3 to 3
- bias_momentum: float32 [2, 8, 512], P(None, None, ('dp', 'fsdp')), may hold values from -320 to 320
- bias_average: float32 [2, 8, 512], P(None, None, ('dp', 'fsdp')), may hold values from -3 to 3
Outputs:
- layer_out: bfloat16 [32, 1024, 512], P(('dp', 'fsdp'))
- input_grad: float32 [32, 1024, 512], P(('dp', 'fsdp'))
- attend_velocity: float32 [2, 512, 1536], P(None, ('dp', 'fsdp'))
- attend_smoothed: float32 [2, 512, 1536], P(None, ('dp', 'fsdp'))
- attend_master: float32 [2, 512, 1536], P(None, ('dp', 'fsdp'))
- attend_copy: bfloat16 [2, 512, 1536], P(None, ('dp', 'fsdp'))
- output_velocity: float32 [2, 512, 512], P(None, ('dp', 'fsdp'))
- output_smoothed: float32 [2, 512, 512], P(None, ('dp', 'fsdp'))
- output_master: float32 [2, 512, 512], P(None, ('dp', 'fsdp'))
- output_copy: bfloat16 [2, 512, 512], P(None, ('dp', 'fsdp'))
- expand_velocity: float32 [2, 512, 1024], P(None, ('dp', 'fsdp'))
- expand_smoothed: float32 [2, 512, 1024], P(None, ('dp', 'fsdp'))
- expand_master: float32 [2, 512, 1024], P(None, ('dp', 'fsdp'))
- expand_copy: bfloat16 [2, 512, 1024], P(None, ('dp', 'fsdp'))
- shrink_velocity: float32 [2, 1024, 512], P(None, ('dp', 'fsdp'))
- shrink_smoothed: float32 [2, 1024, 512], P(None, ('dp', 'fsdp'))
- shrink_master: float32 [2, 1024, 512], P(None, ('dp', 'fsdp'))
- shrink_copy: bfloat16 [2, 1024, 512], P(None, ('dp', 'fsdp'))
- gains_velocity: float32 [2, 2, 512], P(None, None, ('dp', 'fsdp'))
- gains_smoothed: float32 [2, 2, 512], P(None, None, ('dp', 'fsdp'))
- gains_master: float32 [2, 2, 512], P(None, None, ('dp', 'fsdp'))
- gains_copy: bfloat16 [2, 2, 512], P(None, None, ('dp', 'fsdp'))
- bias_velocity: float32 [2, 8, 512], P(None, None, ('dp', 'fsdp'))
- bias_smoothed: float32 [2, 8, 512], P(None, None, ('dp', 'fsdp'))
- bias_master: float32 [2, 8, 512], P(None, None, ('dp', 'fsdp'))
- bias_copy: bfloat16 [2, 8, 512], P(None, None, ('dp', 'fsdp'))
The draws below stay inside these ranges and needn't reach their ends.
All inputs are finite; a program needn't handle non-finite values.
Results may differ from the reference program's by a relative error of at most 0.02.
The reference program's roundings to bfloat16 on the way count: a program that leaves them out, or rounds other values in their place, can miss the bound.
Values may be sent and summed in bfloat16 or wider, within the bound.
No kernel may reach another device: no remote copies, remote signals or barrier semaphores. Data moves between devices by JAX's collectives and lax.ppermute only.
A program may use at most 192 MiB of HBM per device.

```python
import math
import jax
import jax.numpy as jnp
import numpy as np
from jax import lax

D = 512
HEADS = 4
HD = 128
FF = 1024
CTX = 896
QMAX = 128
NDS = 8
LAYERS = 2
SLOT = 1024
NB_ALL = 32
TOKENS = 32768
BROWS = 8


def touch_ends(entries, rng, smallest, high):
    longest = entries.shape.index(max(entries.shape))
    spots = []
    for shift in (0, 1):
        where = [jax.random.randint(jax.random.fold_in(rng, axis), (), 0, length) for axis, length in enumerate(entries.shape)]
        where[longest] = (where[longest] + shift) % entries.shape[longest]
        spots.append(tuple(where))
    return entries.at[spots[0]].set(smallest).at[spots[1]].set(high)


def levels(key, shape, pieces, low, high):
    level = 1.0
    for axis_at, shards_of in pieces:
        heights = jax.random.uniform(jax.random.fold_in(jax.random.fold_in(key, 6), axis_at), (shards_of,), jnp.float32, low / len(pieces), high / len(pieces))
        level = level * jnp.repeat(jnp.exp(heights), shape[axis_at] // shards_of).reshape((-1,) + (1,) * (len(shape) - 1 - axis_at))
    return level


def rank_bounds(amount, lean):
    portions = [(1 << 20) // math.isqrt(standing ** lean) + 1 for standing in range(1, amount + 1)]
    scale = 1 + sum(portions) // (1 << 30)
    return np.cumsum(np.array([max(1, weight // scale) for weight in portions]))


def skewed_ids(key, shape, number_of, lean):
    listing = rank_bounds(number_of, lean)
    lot = jax.random.randint(jax.random.fold_in(key, 1), shape, 0, int(listing[number_of - 1]))
    rank = jnp.searchsorted(jnp.asarray(listing, jnp.int32), lot, side="right")
    return jax.random.permutation(jax.random.fold_in(key, 2), number_of)[rank].astype(jnp.int32)


def gaussian(key, shape, spread, most, cuts=(), kind=jnp.bfloat16):
    level = levels(key, shape, cuts, -0.22, 0.18) if cuts else 1.0
    drawn = jax.random.normal(key, shape, jnp.float32) * spread * level
    return jnp.minimum(jnp.maximum(drawn, -most), most).astype(kind)


def setup_inputs(seed: int = 0) -> dict:
    arg_keys = jax.random.split(jax.random.key(seed), 27)
    tokens = gaussian(arg_keys[0], (NB_ALL, SLOT, D), 1.0, 6.0, ((0, 32),))
    cotangent = gaussian(arg_keys[1], (NB_ALL, SLOT, D), 1.0, 6.0, ((0, 32),))
    dataset_ids = touch_ends(skewed_ids(arg_keys[2], (NB_ALL,), NDS, 2), jax.random.fold_in(arg_keys[2], 3), 0, NDS - 1).astype(jnp.int32)
    query_counts = touch_ends(jax.random.randint(arg_keys[3], (NB_ALL,), 1, QMAX + 1), jax.random.fold_in(arg_keys[3], 1), 1, QMAX).astype(jnp.int32)
    learn_rate = jnp.clip(jnp.exp(jax.random.uniform(arg_keys[4], (1,), jnp.float32, math.log(0.0002762136), math.log(0.00082864077))), 0.0002762136, 0.00082864077)
    momentum_coef = jnp.clip(jax.random.uniform(arg_keys[5], (1,), jnp.float32, 0.4, 0.6), 0.4, 0.6)
    average_decay = jnp.clip(jax.random.uniform(arg_keys[6], (1,), jnp.float32, 0.2, 0.95), 0.2, 0.95)
    step_count = jax.random.randint(arg_keys[7], (1,), 2, 21).astype(jnp.int32)
    attend_weight = gaussian(arg_keys[8], (LAYERS, D, 3 * D), D ** -0.5, 0.25, ((1, 32),), jnp.float32)
    attend_momentum = gaussian(arg_keys[9], (LAYERS, D, 3 * D), (0.1 * TOKENS ** 0.5), 112.0, ((1, 32),), jnp.float32)
    attend_average = gaussian(arg_keys[10], (LAYERS, D, 3 * D), D ** -0.5, 0.25, ((1, 32),), jnp.float32)
    output_weight = gaussian(arg_keys[11], (LAYERS, D, D), (D // 32) ** -0.5, 1.5, ((1, 32),), jnp.float32)
    output_momentum = gaussian(arg_keys[12], (LAYERS, D, D), (0.02 * TOKENS ** 0.5), 20.0, ((1, 32),), jnp.float32)
    output_average = gaussian(arg_keys[13], (LAYERS, D, D), (D // 32) ** -0.5, 1.5, ((1, 32),), jnp.float32)
    expand_weight = gaussian(arg_keys[14], (LAYERS, D, FF), D ** -0.5, 0.25, ((1, 32),), jnp.float32)
    expand_momentum = gaussian(arg_keys[15], (LAYERS, D, FF), (0.3 * TOKENS ** 0.5), 320.0, ((1, 32),), jnp.float32)
    expand_average = gaussian(arg_keys[16], (LAYERS, D, FF), D ** -0.5, 0.25, ((1, 32),), jnp.float32)
    shrink_weight = gaussian(arg_keys[17], (LAYERS, FF, D), FF ** -0.5, 0.1875, ((1, 32),), jnp.float32)
    shrink_momentum = gaussian(arg_keys[18], (LAYERS, FF, D), (0.3 * TOKENS ** 0.5), 320.0, ((1, 32),), jnp.float32)
    shrink_average = gaussian(arg_keys[19], (LAYERS, FF, D), FF ** -0.5, 0.1875, ((1, 32),), jnp.float32)
    norm_gains = jnp.clip(1.0 + 0.1 * jax.random.normal(arg_keys[20], (LAYERS, 2, D), jnp.float32), 0.5, 1.5)
    gains_momentum = gaussian(arg_keys[21], (LAYERS, 2, D), (0.3 * TOKENS ** 0.5), 320.0, ((2, 32),), jnp.float32)
    gains_average = jnp.clip(1.0 + 0.1 * jax.random.normal(arg_keys[22], (LAYERS, 2, D), jnp.float32), 0.5, 1.5)
    bias_rows = gaussian(arg_keys[23], (LAYERS, BROWS, D), 0.3, 3.0, ((2, 32),), jnp.float32)
    bias_momentum = gaussian(arg_keys[24], (LAYERS, BROWS, D), (0.3 * TOKENS ** 0.5), 320.0, ((2, 32),), jnp.float32)
    bias_average = gaussian(arg_keys[25], (LAYERS, BROWS, D), 0.3, 3.0, ((2, 32),), jnp.float32)
    return {"tokens": tokens, "cotangent": cotangent, "dataset_ids": dataset_ids, "query_counts": query_counts, "learn_rate": learn_rate, "momentum_coef": momentum_coef, "average_decay": average_decay, "step_count": step_count, "attend_weight": attend_weight, "attend_momentum": attend_momentum, "attend_average": attend_average, "output_weight": output_weight, "output_momentum": output_momentum, "output_average": output_average, "expand_weight": expand_weight, "expand_momentum": expand_momentum, "expand_average": expand_average, "shrink_weight": shrink_weight, "shrink_momentum": shrink_momentum, "shrink_average": shrink_average, "norm_gains": norm_gains, "gains_momentum": gains_momentum, "gains_average": gains_average, "bias_rows": bias_rows, "bias_momentum": bias_momentum, "bias_average": bias_average}


@jax.custom_vjp
def low(v):
    return lax.optimization_barrier(v.astype(jnp.bfloat16)).astype(jnp.float32)

@jax.custom_vjp
def low_back(v):
    return v

def low_keep(v):
    return (low(v), None)

def low_pass(kept, grad):
    return (grad,)

def back_keep(v):
    return (v, None)

def back_low(kept, grad):
    return (low(grad),)
low.defvjp(low_keep, low_pass)
low_back.defvjp(back_keep, back_low)
highest = lax.Precision.HIGHEST
EPS = 1e-05

def norm_rows(summed, gain, shift):
    row_mean = lax.optimization_barrier(jnp.mean(summed, axis=-1, keepdims=True))
    centred = summed - row_mean
    inv_std = lax.rsqrt(lax.optimization_barrier(jnp.mean(centred * centred, axis=-1, keepdims=True)) + EPS)
    return centred * inv_std * gain + shift

def attend_one(joint_rows):
    queries = joint_rows[:, :D].reshape(SLOT, HEADS, HD)
    key_rows = joint_rows[:CTX, D:2 * D].reshape(CTX, HEADS, HD)
    value_rows = joint_rows[:CTX, 2 * D:].reshape(CTX, HEADS, HD)
    scores = low_back(jnp.einsum('qhe,khe->hqk', queries, key_rows, precision=highest))
    softmax_rows = jax.nn.softmax(scores * HD ** (-0.5), axis=-1)
    mixed_sum = jnp.einsum('hqk,khe->qhe', low(softmax_rows), value_rows, precision=highest)
    return mixed_sum.reshape(SLOT, D)

def layer(inputs, params):
    attend_w, output_w, expand_w, shrink_w, gain_vals, biases = [low(item) for item in params]
    zeros_row = jnp.zeros((D,), jnp.float32)
    joint_sum = jnp.dot(inputs, attend_w, precision=highest) + jnp.concatenate([biases[0], zeros_row, biases[1]])
    joint_low = low_back(low(joint_sum))
    mixed_low = low_back(low(lax.map(jax.checkpoint(attend_one), joint_low)))
    attn_out = low_back(jnp.dot(mixed_low, output_w, precision=highest) + biases[2])
    first_norm = norm_rows(inputs + attn_out, gain_vals[0], biases[4])
    hidden = low_back(jnp.dot(low(first_norm), expand_w, precision=highest) + biases[6:].reshape(FF))
    act_low = low(jax.nn.gelu(hidden, approximate=False))
    branch = low_back(jnp.dot(act_low, shrink_w, precision=highest) + biases[3])
    return norm_rows(first_norm + branch, gain_vals[1], biases[5])

def advance(master, moment, average, grad, momentum, step_rate, decay_now):
    new_moment = momentum * moment + grad
    new_master = master - step_rate * (grad + momentum * new_moment)
    new_average = decay_now * average + (1.0 - decay_now) * new_master
    return (new_moment, new_average, new_master, new_master.astype(jnp.bfloat16))

def reference(tokens, cotangent, dataset_ids, query_counts, learn_rate, momentum_coef, average_decay, step_count, attend_weight, attend_momentum, attend_average, output_weight, output_momentum, output_average, expand_weight, expand_momentum, expand_average, shrink_weight, shrink_momentum, shrink_average, norm_gains, gains_momentum, gains_average, bias_rows, bias_momentum, bias_average):
    masters = (attend_weight, output_weight, expand_weight, shrink_weight, norm_gains, bias_rows)
    moments = (attend_momentum, output_momentum, expand_momentum, shrink_momentum, gains_momentum, bias_momentum)
    averages = (attend_average, output_average, expand_average, shrink_average, gains_average, bias_average)
    onehot = (dataset_ids[:, None] == jnp.arange(NDS, dtype=jnp.int32)[None, :]).astype(jnp.float32)
    counts = lax.optimization_barrier(jnp.sum(onehot, axis=0))
    own_count = lax.optimization_barrier(jnp.sum(onehot * counts[None, :], axis=1))
    row_weight = jnp.sum(counts) / (NDS * own_count)
    positions = jnp.arange(SLOT, dtype=jnp.int32)
    live_rows = ((positions[None, :] < CTX) | (positions[None, :] - CTX < query_counts[:, None])).astype(jnp.float32)
    effective = cotangent.astype(jnp.float32) * (live_rows * row_weight[:, None])[:, :, None]

    def run(inputs, params):
        current = inputs
        for layer_index in range(LAYERS):
            current = layer(current, tuple((item[layer_index] for item in params)))
            if layer_index + 1 < LAYERS:
                current = low(current)
        return current
    result, pullback = jax.vjp(run, tokens.astype(jnp.float32), masters)
    input_grad, grads = pullback(effective)
    step_value = step_count[0].astype(jnp.float32)
    decay_now = average_decay[0] * (1.0 + step_value) / (4.0 + step_value)
    outputs = [result.astype(jnp.bfloat16), input_grad]
    for group_index in range(6):
        outputs.extend(advance(masters[group_index], moments[group_index], averages[group_index], grads[group_index], momentum_coef[0], learn_rate[0], decay_now))
    return tuple(outputs)
```

```python
import jax
import jax.numpy as jnp
import numpy as np
from jax import lax
from jax.experimental import pallas as pl
from jax.experimental.pallas import tpu as pltpu
from jax.sharding import PartitionSpec as P

HEADS = 4
CTX = 896
NDS = 8


EPS = 1e-05


def norm_rows(summed, gain, shift):
    row_mean = jnp.mean(summed, axis=-1, keepdims=True)
    centred = summed - row_mean
    inv_std = lax.rsqrt(jnp.mean(centred * centred, axis=-1, keepdims=True) + EPS)
    unit_rows = centred * inv_std
    return (unit_rows * gain + shift, unit_rows, inv_std)


def norm_back(grad_rows, unit_rows, inv_std, gain):
    scaled = grad_rows * gain
    return inv_std * (
        scaled
        - jnp.mean(scaled, axis=-1, keepdims=True)
        - unit_rows * jnp.mean(scaled * unit_rows, axis=-1, keepdims=True)
    )


def gelu_slope(hidden):
    normal_cdf = 0.5 * (1.0 + jax.scipy.special.erf(hidden * 0.7071067811865476))
    normal_pdf = jnp.exp(-0.5 * hidden * hidden) * 0.3989422804014327
    return normal_cdf + hidden * normal_pdf


def attend_one(pieces):
    queries, key_rows, value_rows = pieces
    factor = queries.shape[-1] ** (-0.5)
    scaled = (
        jnp.einsum("qhe,khe->hqk", queries, key_rows, preferred_element_type=jnp.float32) * factor
    )
    row_top = jnp.max(scaled, axis=-1, keepdims=True)
    log_total = row_top + jnp.log(jnp.sum(jnp.exp(scaled - row_top), axis=-1, keepdims=True))
    softmax_low = jnp.exp(scaled - log_total).astype(jnp.bfloat16)
    mixed_sum = jnp.einsum(
        "hqk,khe->qhe", softmax_low, value_rows, preferred_element_type=jnp.float32
    )
    return (mixed_sum, log_total)


def attend_back(pieces):
    queries, key_rows, value_rows, log_total, grad_mixed = pieces
    factor = queries.shape[-1] ** (-0.5)
    scaled = (
        jnp.einsum("qhe,khe->hqk", queries, key_rows, preferred_element_type=jnp.float32) * factor
    )
    softmax_rows = jnp.exp(scaled - log_total)
    softmax_low = softmax_rows.astype(jnp.bfloat16)
    grad_values = jnp.einsum(
        "hqk,qhe->khe", softmax_low, grad_mixed, preferred_element_type=jnp.float32
    )
    grad_probs = jnp.einsum(
        "qhe,khe->hqk", grad_mixed, value_rows, preferred_element_type=jnp.float32
    )
    grad_scores = (
        factor
        * softmax_rows
        * (grad_probs - jnp.sum(softmax_rows * grad_probs, axis=-1, keepdims=True))
    ).astype(jnp.bfloat16)
    grad_query = jnp.einsum(
        "hqk,khe->qhe", grad_scores, key_rows, preferred_element_type=jnp.float32
    )
    grad_keys = jnp.einsum("hqk,qhe->khe", grad_scores, queries, preferred_element_type=jnp.float32)
    return (grad_query, grad_keys, grad_values)


def split_heads(joint_low, model_width):
    head_size = model_width // HEADS
    batch_rows = joint_low.shape[0]
    slot_rows = joint_low.shape[1]
    queries = joint_low[:, :, :model_width].reshape(batch_rows, slot_rows, HEADS, head_size)
    key_rows = joint_low[:, :CTX, model_width : 2 * model_width].reshape(
        batch_rows, CTX, HEADS, head_size
    )
    value_rows = joint_low[:, :CTX, 2 * model_width :].reshape(batch_rows, CTX, HEADS, head_size)
    return (queries, key_rows, value_rows)


def layer_forward(inputs_low, weights):
    attend_w, output_w, expand_w, shrink_w, gain_rows, bias_table = weights
    model_width = attend_w.shape[0]
    gain_vals = gain_rows.astype(jnp.float32)
    biases = bias_table.astype(jnp.float32)
    zeros_row = jnp.zeros((model_width,), jnp.float32)
    joint_sum = jnp.dot(inputs_low, attend_w, preferred_element_type=jnp.float32) + jnp.concatenate(
        [biases[0], zeros_row, biases[1]]
    )
    joint_low = joint_sum.astype(jnp.bfloat16)
    queries, key_rows, value_rows = split_heads(joint_low, model_width)
    mixed_sum, log_total = lax.map(attend_one, (queries, key_rows, value_rows))
    mixed_low = mixed_sum.reshape(inputs_low.shape[0], inputs_low.shape[1], model_width).astype(
        jnp.bfloat16
    )
    attn_out = jnp.dot(mixed_low, output_w, preferred_element_type=jnp.float32) + biases[2]
    first_norm, unit_one, inv_one = norm_rows(
        inputs_low.astype(jnp.float32) + attn_out, gain_vals[0], biases[4]
    )
    first_low = first_norm.astype(jnp.bfloat16)
    hidden = jnp.dot(first_low, expand_w, preferred_element_type=jnp.float32) + biases[6:].reshape(
        -1
    )
    act_low = jax.nn.gelu(hidden, approximate=False).astype(jnp.bfloat16)
    branch = jnp.dot(act_low, shrink_w, preferred_element_type=jnp.float32) + biases[3]
    result, unit_two, inv_two = norm_rows(first_norm + branch, gain_vals[1], biases[5])
    kept_values = (
        queries,
        key_rows,
        value_rows,
        log_total,
        mixed_low,
        unit_one,
        inv_one,
        first_low,
        hidden,
        act_low,
        unit_two,
        inv_two,
    )
    return (result, kept_values)


def layer_backward(inputs_low, weights, grad_out):
    attend_w, output_w, expand_w, shrink_w, gain_rows, bias_table = weights
    model_width = attend_w.shape[0]
    gain_vals = gain_rows.astype(jnp.float32)
    unused_result, kept_values = layer_forward(inputs_low, weights)
    (
        queries,
        key_rows,
        value_rows,
        log_total,
        mixed_low,
        unit_one,
        inv_one,
        first_low,
        hidden,
        act_low,
        unit_two,
        inv_two,
    ) = kept_values
    batch_rows = inputs_low.shape[0]
    slot_rows = inputs_low.shape[1]
    grad_two = norm_back(grad_out, unit_two, inv_two, gain_vals[1])
    gain_two = jnp.sum(grad_out * unit_two, axis=(0, 1))
    shift_two = jnp.sum(grad_out, axis=(0, 1))
    branch_low = grad_two.astype(jnp.bfloat16)
    grad_shrink = jnp.einsum("nsf,nsd->fd", act_low, branch_low, preferred_element_type=jnp.float32)
    bias_branch = jnp.sum(branch_low.astype(jnp.float32), axis=(0, 1))
    grad_hidden = (
        jnp.einsum("nsd,fd->nsf", branch_low, shrink_w, preferred_element_type=jnp.float32)
        * gelu_slope(hidden)
    ).astype(jnp.bfloat16)
    grad_expand = jnp.einsum(
        "nsd,nsf->df", first_low, grad_hidden, preferred_element_type=jnp.float32
    )
    bias_hidden = jnp.sum(grad_hidden.astype(jnp.float32), axis=(0, 1))
    grad_first = grad_two + jnp.einsum(
        "nsf,df->nsd", grad_hidden, expand_w, preferred_element_type=jnp.float32
    )
    grad_one = norm_back(grad_first, unit_one, inv_one, gain_vals[0])
    gain_one = jnp.sum(grad_first * unit_one, axis=(0, 1))
    shift_one = jnp.sum(grad_first, axis=(0, 1))
    attn_low = grad_one.astype(jnp.bfloat16)
    grad_output = jnp.einsum("nsd,nse->de", mixed_low, attn_low, preferred_element_type=jnp.float32)
    bias_attn = jnp.sum(attn_low.astype(jnp.float32), axis=(0, 1))
    grad_mixed = jnp.einsum(
        "nse,de->nsd", attn_low, output_w, preferred_element_type=jnp.float32
    ).astype(jnp.bfloat16)
    grad_heads = grad_mixed.reshape(batch_rows, slot_rows, HEADS, model_width // HEADS)
    grad_query, grad_keys, grad_values = lax.map(
        attend_back, (queries, key_rows, value_rows, log_total, grad_heads)
    )
    rim_pad = ((0, 0), (0, slot_rows - CTX), (0, 0))
    keys_full = jnp.pad(grad_keys.reshape(batch_rows, CTX, model_width), rim_pad)
    values_full = jnp.pad(grad_values.reshape(batch_rows, CTX, model_width), rim_pad)
    grad_joint = jnp.concatenate(
        [grad_query.reshape(batch_rows, slot_rows, model_width), keys_full, values_full], axis=-1
    ).astype(jnp.bfloat16)
    grad_attend = jnp.einsum(
        "nsd,nsj->dj", inputs_low, grad_joint, preferred_element_type=jnp.float32
    )
    joint_bias = jnp.sum(grad_joint.astype(jnp.float32), axis=(0, 1))
    grad_input = grad_one + jnp.einsum(
        "nsj,dj->nsd", grad_joint, attend_w, preferred_element_type=jnp.float32
    )
    grad_gains = jnp.stack([gain_one, gain_two])
    grad_biases = jnp.concatenate(
        [
            jnp.stack(
                [
                    joint_bias[:model_width],
                    joint_bias[2 * model_width :],
                    bias_attn,
                    bias_branch,
                    shift_one,
                    shift_two,
                ]
            ),
            bias_hidden.reshape(-1, model_width),
        ],
        axis=0,
    )
    return (
        (grad_attend, grad_output, grad_expand, grad_shrink, grad_gains, grad_biases),
        grad_input,
    )


class Route:
    def __init__(self, steps, inner_size):
        self.steps = steps
        masks = [bit * inner_size if axis == "dp" else bit for axis, size, bit in steps]
        self.count = 1 << len(steps)
        self.offset = [
            sum(mask for at, mask in enumerate(masks) if place >> at & 1)
            for place in range(self.count)
        ]

    def swap(self, at, payload):
        axis, size, bit = self.steps[at]
        return lax.ppermute(payload, axis, [(one, one ^ bit) for one in range(size)])


def routes(outer_size, inner_size):
    outer = [("dp", outer_size, 1 << at) for at in reversed(range(outer_size.bit_length() - 1))]
    inner = [("fsdp", inner_size, 1 << at) for at in reversed(range(inner_size.bit_length() - 1))]
    first = inner + outer
    second = inner[:-1] + outer[:-1] + inner[-1:] + outer[-1:]
    return (Route(first, inner_size), Route(second, inner_size))


def spread(route, block, shared=None):
    rows, width = block.shape
    for at in range(len(route.steps)):
        held = block.shape[0]
        payload = block if shared is None else jnp.concatenate([block, shared])
        got = route.swap(at, payload)
        block = jnp.concatenate([block, got[:held]])
        if shared is not None:
            shared = shared + got[held:]
    return (block.reshape(route.count, rows, width), shared)


def gather_sum(route, slots, shared=None):
    count, rows, width = slots.shape
    block = slots.reshape(count * rows, width)
    for at in reversed(range(len(route.steps))):
        half = block.shape[0] // 2
        payload = block[half:] if shared is None else jnp.concatenate([block[half:], shared])
        got = route.swap(at, payload)
        block = (block[:half].astype(jnp.float32) + got[:half].astype(jnp.float32)).astype(
            jnp.bfloat16
        )
        if shared is not None:
            shared = (shared.astype(jnp.float32) + got[half:].astype(jnp.float32)).astype(
                jnp.bfloat16
            )
    return (block, shared)


def in_order(route, slots, place):
    position = np.zeros((route.count,), np.int32)
    for at, off in enumerate(route.offset):
        position[off] = at
    table = jnp.asarray(position)
    owners = jnp.arange(route.count, dtype=jnp.int32)
    return jnp.take(slots, table[owners ^ place], axis=0)


def by_position(route, slots, place):
    return jnp.take(slots, jnp.asarray(route.offset, jnp.int32) ^ place, axis=0)


def wide_to_rows(shard, width):
    rows = shard.shape[0]
    return jnp.concatenate(
        [shard[:, at * width : (at + 1) * width] for at in range(shard.shape[1] // width)]
    )


def rows_to_wide(slots, pieces):
    owners, rows, width = slots.shape
    each = rows // pieces
    return (
        slots.reshape(owners, pieces, each, width)
        .transpose(0, 2, 1, 3)
        .reshape(owners * each, pieces * width)
    )


def wide_to_slots(grad, owners, width):
    rows, total = grad.shape
    pieces = total // width
    return (
        grad.reshape(owners, rows // owners, pieces, width)
        .transpose(0, 2, 1, 3)
        .reshape(owners, pieces * (rows // owners), width)
    )

def advance(master, moment, average, grad, momentum, step_rate, decay_now):
    new_moment = momentum * moment + grad
    new_master = master - step_rate * (grad + momentum * new_moment)
    new_average = decay_now * average + (1.0 - decay_now) * new_master
    return (new_moment, new_average, new_master, new_master.astype(jnp.bfloat16))


def shards(
    tokens,
    cotangent,
    dataset_ids,
    query_counts,
    learn_rate,
    momentum_coef,
    average_decay,
    step_count,
    attend_weight,
    attend_momentum,
    attend_average,
    output_weight,
    output_momentum,
    output_average,
    expand_weight,
    expand_momentum,
    expand_average,
    shrink_weight,
    shrink_momentum,
    shrink_average,
    norm_gains,
    gains_momentum,
    gains_average,
    bias_rows,
    bias_momentum,
    bias_average,
):
    masters = (attend_weight, output_weight, expand_weight, shrink_weight, norm_gains, bias_rows)
    moments = (
        attend_momentum,
        output_momentum,
        expand_momentum,
        shrink_momentum,
        gains_momentum,
        bias_momentum,
    )
    averages = (
        attend_average,
        output_average,
        expand_average,
        shrink_average,
        gains_average,
        bias_average,
    )
    layers = attend_weight.shape[0]
    model_width = attend_weight.shape[2] // 3
    each = attend_weight.shape[1]
    outer_size = lax.axis_size("dp")
    inner_size = lax.axis_size("fsdp")
    everyone = outer_size * inner_size
    place = lax.axis_index("dp") * inner_size + lax.axis_index("fsdp")
    first_route, second_route = routes(outer_size, inner_size)
    low = lambda item: item.astype(jnp.bfloat16)
    onehot = (dataset_ids[:, None] == jnp.arange(NDS, dtype=jnp.int32)[None, :]).astype(jnp.float32)
    mine = jnp.zeros((24, model_width), jnp.bfloat16)
    vectors = jnp.concatenate(
        [low(item[at]) for at in range(layers) for item in (norm_gains, bias_rows)]
    )
    mine = lax.dynamic_update_slice(mine, vectors, (0, place * vectors.shape[1]))
    mine = mine.at[20, :NDS].set(low(jnp.sum(onehot, axis=0)))
    gathered = []
    for at in range(layers):
        first = wide_to_rows(low(attend_weight[at]), model_width)
        second = jnp.concatenate(
            [
                low(output_weight[at]),
                wide_to_rows(low(expand_weight[at]), model_width),
                low(shrink_weight[at]),
            ]
        )
        first_all, mine_all = spread(first_route, first, mine if at == 0 else None)
        second_all, _ = spread(second_route, second)
        if at == 0:
            vectors_all = mine_all
        first_all = in_order(first_route, first_all, place)
        second_all = in_order(second_route, second_all, place)
        gathered.append(
            (
                rows_to_wide(first_all, 3),
                second_all[:, :each].reshape(model_width, model_width),
                rows_to_wide(second_all[:, each : 3 * each], 2),
                second_all[:, 3 * each :].reshape(2 * model_width, model_width),
                vectors_all[10 * at : 10 * at + 2],
                vectors_all[10 * at + 2 : 10 * at + 10],
            )
        )
    counts = vectors_all[20, :NDS].astype(jnp.float32)
    own_count = jnp.sum(onehot * counts[None, :], axis=1)
    row_weight = jnp.sum(counts) / (NDS * own_count)
    positions = jnp.arange(tokens.shape[1], dtype=jnp.int32)
    live_rows = (
        (positions[None, :] < CTX) | (positions[None, :] - CTX < query_counts[:, None])
    ).astype(jnp.float32)
    effective = cotangent.astype(jnp.float32) * (live_rows * row_weight[:, None])[:, :, None]
    current = tokens
    inputs_kept = []
    for layer_index in range(layers):
        inputs_kept.append(current)
        result, unused_kept = layer_forward(current, gathered[layer_index])
        current = result.astype(jnp.bfloat16)
    grad_rows = effective
    shard_grads = [None] * layers
    for layer_index in reversed(range(layers)):
        local, grad_rows = layer_backward(inputs_kept[layer_index], gathered[layer_index], grad_rows)
        first = by_position(first_route, wide_to_slots(low(local[0]), everyone, model_width), place)
        second = by_position(
            second_route,
            jnp.concatenate(
                [
                    low(local[1]).reshape(everyone, each, model_width),
                    wide_to_slots(low(local[2]), everyone, model_width),
                    low(local[3]).reshape(everyone, 2 * each, model_width),
                ],
                axis=1,
            ),
            place,
        )
        second_sum, _ = gather_sum(second_route, second)
        shared = jnp.pad(low(jnp.concatenate([local[4], local[5]])), ((0, 6), (0, 0)))
        first_sum, shared_sum = gather_sum(first_route, first, shared)
        wide = lambda rows, pieces: rows_to_wide(rows[None], pieces).astype(jnp.float32)
        own = lax.dynamic_slice(shared_sum, (0, place * each), (10, each)).astype(jnp.float32)
        shard_grads[layer_index] = (
            wide(first_sum, 3),
            second_sum[:each].astype(jnp.float32),
            wide(second_sum[each : 3 * each], 2),
            second_sum[3 * each :].astype(jnp.float32),
            own[:2],
            own[2:],
        )
    step_value = step_count[0].astype(jnp.float32)
    decay_now = average_decay[0] * (1.0 + step_value) / (4.0 + step_value)
    outputs = [current, grad_rows]
    for group_index in range(6):
        stacked = jnp.stack(
            [shard_grads[layer_index][group_index] for layer_index in range(layers)]
        )
        outputs.extend(
            advance(
                masters[group_index],
                moments[group_index],
                averages[group_index],
                stacked,
                momentum_coef[0],
                learn_rate[0],
                decay_now,
            )
        )
    return tuple(outputs)


def solution(mesh):
    return jax.shard_map(
        shards,
        mesh=mesh,
        in_specs=(
            P(("dp", "fsdp"), None, None),
            P(("dp", "fsdp"), None, None),
            P(("dp", "fsdp")),
            P(("dp", "fsdp")),
            P(),
            P(),
            P(),
            P(),
            P(None, ("dp", "fsdp"), None),
            P(None, ("dp", "fsdp"), None),
            P(None, ("dp", "fsdp"), None),
            P(None, ("dp", "fsdp"), None),
            P(None, ("dp", "fsdp"), None),
            P(None, ("dp", "fsdp"), None),
            P(None, ("dp", "fsdp"), None),
            P(None, ("dp", "fsdp"), None),
            P(None, ("dp", "fsdp"), None),
            P(None, ("dp", "fsdp"), None),
            P(None, ("dp", "fsdp"), None),
            P(None, ("dp", "fsdp"), None),
            P(None, None, ("dp", "fsdp")),
            P(None, None, ("dp", "fsdp")),
            P(None, None, ("dp", "fsdp")),
            P(None, None, ("dp", "fsdp")),
            P(None, None, ("dp", "fsdp")),
            P(None, None, ("dp", "fsdp")),
        ),
        out_specs=(
            P(("dp", "fsdp"), None, None),
            P(("dp", "fsdp"), None, None),
            P(None, ("dp", "fsdp"), None),
            P(None, ("dp", "fsdp"), None),
            P(None, ("dp", "fsdp"), None),
            P(None, ("dp", "fsdp"), None),
            P(None, ("dp", "fsdp"), None),
            P(None, ("dp", "fsdp"), None),
            P(None, ("dp", "fsdp"), None),
            P(None, ("dp", "fsdp"), None),
            P(None, ("dp", "fsdp"), None),
            P(None, ("dp", "fsdp"), None),
            P(None, ("dp", "fsdp"), None),
            P(None, ("dp", "fsdp"), None),
            P(None, ("dp", "fsdp"), None),
            P(None, ("dp", "fsdp"), None),
            P(None, ("dp", "fsdp"), None),
            P(None, ("dp", "fsdp"), None),
            P(None, None, ("dp", "fsdp")),
            P(None, None, ("dp", "fsdp")),
            P(None, None, ("dp", "fsdp")),
            P(None, None, ("dp", "fsdp")),
            P(None, None, ("dp", "fsdp")),
            P(None, None, ("dp", "fsdp")),
            P(None, None, ("dp", "fsdp")),
            P(None, None, ("dp", "fsdp")),
        ),
        check_vma=False,
    )
```

```python
import functools

import jax
import jax.numpy as jnp
import numpy as np
from jax import lax
from jax.experimental import pallas as pl
from jax.experimental.pallas import tpu as pltpu
from jax.sharding import PartitionSpec as P

HEADS = 4
CTX = 896
NDS = 8
EPS = 1e-05
OWNERS = 32
FIRST_PARTS = (16, 16, 16)
SECOND_PARTS = (16, 16, 16, 32)

SCORE_BLOCK = 256
ROW_BLOCK = 256
ROOT_HALF = 0.7071067811865476
PDF_PEAK = 0.3989422804014327
VMEM_LIMIT = 60 * 1024 * 1024
FLOAT = jnp.float32
HALF = jnp.bfloat16


def product(left, right, left_dim, right_dim):
    return lax.dot_general(
        left, right, (((left_dim,), (right_dim,)), ((), ())), preferred_element_type=FLOAT
    )


def owner_rows(offset, place, rows):
    return pl.ds(pl.multiple_of((offset ^ place) * rows, rows), rows)


def attend_kernel(offsets, place_ref, x_ref, near_ref, far_ref, vec_ref, joint_ref, probs_ref,
                  mixed_ref, weight_ref):
    head = pl.program_id(0)
    head_size = mixed_ref.shape[1]
    place = place_ref[0]

    half = len(offsets) // 2
    for at, offset in enumerate(offsets):
        slots = near_ref if at < half else far_ref
        rows = owner_rows(offset, place, 16)
        for piece in range(3):
            weight_ref[0, rows, piece * head_size : (piece + 1) * head_size] = slots[
                at % half, piece * 16 : (piece + 1) * 16, :
            ]
    zeros = jnp.zeros((1, head_size), FLOAT)
    shift = jnp.concatenate([vec_ref[2:3, :], zeros, vec_ref[3:4, :]], axis=1)
    joint_ref[0] = (product(x_ref[...], weight_ref[0], 1, 0) + shift).astype(HALF)
    keys = joint_ref[0, :CTX, head_size : 2 * head_size]
    values = joint_ref[0, :CTX, 2 * head_size :]
    values_turned = jnp.transpose(values)
    factor = head_size ** (-0.5) * 1.4426950408889634
    for start in range(0, x_ref.shape[0], SCORE_BLOCK):
        span = slice(start, start + SCORE_BLOCK)
        queries = joint_ref[0, span, :head_size]
        scores = product(keys, queries, 1, 1)
        top = jnp.max(scores, axis=0, keepdims=True)
        grown = jnp.exp2((scores - top) * factor)
        total = jnp.sum(grown, axis=0, keepdims=True)
        probs = (grown * (1.0 / total)).astype(HALF)
        probs_ref[0, :, span] = probs
        mixed_ref[span, :] = jnp.transpose(product(values_turned, probs, 1, 0)).astype(HALF)


def attend_call(offsets, place, x, near, far, vectors):
    rows, width = x.shape
    head_size = width // HEADS
    slots, high, _ = near.shape
    return pl.pallas_call(
        functools.partial(attend_kernel, offsets),
        grid_spec=pltpu.PrefetchScalarGridSpec(
            num_scalar_prefetch=1,
            grid=(HEADS,),
            in_specs=[
                pl.BlockSpec((rows, width), lambda h, p: (0, 0)),
                pl.BlockSpec((slots, high, head_size), lambda h, p: (0, 0, h)),
                pl.BlockSpec((slots, high, head_size), lambda h, p: (0, 0, h)),
                pl.BlockSpec((16, head_size), lambda h, p: (0, h)),
            ],
            out_specs=[
                pl.BlockSpec((1, rows, 3 * head_size), lambda h, p: (h, 0, 0)),
                pl.BlockSpec((1, CTX, rows), lambda h, p: (h, 0, 0)),
                pl.BlockSpec((rows, head_size), lambda h, p: (0, h)),
                pl.BlockSpec((1, width, 3 * head_size), lambda h, p: (h, 0, 0)),
            ],
        ),
        out_shape=[
            jax.ShapeDtypeStruct((HEADS, rows, 3 * head_size), HALF),
            jax.ShapeDtypeStruct((HEADS, CTX, rows), HALF),
            jax.ShapeDtypeStruct((rows, width), HALF),
            jax.ShapeDtypeStruct((HEADS, width, 3 * head_size), HALF),
        ],
        compiler_params=pltpu.CompilerParams(vmem_limit_bytes=VMEM_LIMIT),
        cost_estimate=pl.CostEstimate(
            flops=2 * rows * width * 3 * width + 4 * rows * CTX * width,
            bytes_accessed=16 * 1024 * 1024,
            transcendentals=HEADS * rows * CTX,
        ),
        name="attend",
    )(place, x, near, far, vectors)


def unpack_second(offsets, place, near_ref, far_ref, output_w, expand_w, shrink_w):
    half = len(offsets) // 2
    width = output_w.shape[1]
    for at, offset in enumerate(offsets):
        slots = near_ref if at < half else far_ref
        rows = owner_rows(offset, place, 16)
        output_w[rows, :] = slots[at % half, 0:16, :]
        expand_w[rows, :width] = slots[at % half, 16:32, :]
        expand_w[rows, width:] = slots[at % half, 32:48, :]
        shrink_w[owner_rows(offset, place, 32), :] = slots[at % half, 48:80, :]


def row_mean(rows):
    return jnp.mean(rows, axis=-1, keepdims=True)


def normalize(rows):
    centred = rows - row_mean(rows)
    inv_std = lax.rsqrt(row_mean(centred * centred) + EPS)
    return (centred * inv_std, inv_std)


def forward_rows(x_ref, mixed_ref, vec_ref, output_w, expand_w, shrink_w):
    attn_out = product(mixed_ref[...], output_w[...], 1, 0) + vec_ref[4:5, :]
    unit_one, inv_one = normalize(x_ref[...].astype(FLOAT) + attn_out)
    first_norm = unit_one * vec_ref[0:1, :] + vec_ref[6:7, :]
    first_low = first_norm.astype(HALF)
    shift = jnp.concatenate([vec_ref[8:9, :], vec_ref[9:10, :]], axis=1)
    hidden = product(first_low, expand_w[...], 1, 0) + shift
    normal_cdf = 0.5 * (1.0 + lax.erf(hidden * ROOT_HALF))
    act_low = (hidden * normal_cdf).astype(HALF)
    slope = normal_cdf + hidden * (jnp.exp(-0.5 * hidden * hidden) * PDF_PEAK)
    branch = product(act_low, shrink_w[...], 1, 0) + vec_ref[5:6, :]
    unit_two, inv_two = normalize(first_norm + branch)
    result = unit_two * vec_ref[1:2, :] + vec_ref[7:8, :]
    return (unit_one, inv_one, first_low, act_low, slope, unit_two, inv_two, result)


def column_sum(rows):
    return jnp.sum(rows, axis=0, keepdims=True)


def backward_rows(grad_rows, mixed_ref, vec_ref, kept, output_w, expand_w, shrink_w, grad_mixed_ref,
                  grad_one_ref, grad_output, grad_expand, grad_shrink, sums):
    unit_one, inv_one, first_low, act_low, slope, unit_two, inv_two = kept
    width = grad_rows.shape[1]

    def layer_norm_back(rows, unit_rows, inv_std, gain):
        scaled = rows * gain
        return inv_std * (scaled - row_mean(scaled) - unit_rows * row_mean(scaled * unit_rows))

    grad_two = layer_norm_back(grad_rows, unit_two, inv_two, vec_ref[1:2, :])
    branch_low = grad_two.astype(HALF)
    grad_shrink[...] += product(act_low, branch_low, 0, 0)
    grad_hidden = (product(branch_low, shrink_w[...], 1, 1) * slope).astype(HALF)
    grad_expand[...] += product(first_low, grad_hidden, 0, 0)
    grad_first = grad_two + product(grad_hidden, expand_w[...], 1, 1)
    grad_one = layer_norm_back(grad_first, unit_one, inv_one, vec_ref[0:1, :])
    attn_low = grad_one.astype(HALF)
    grad_output[...] += product(mixed_ref[...], attn_low, 0, 0)
    grad_mixed_ref[...] = product(attn_low, output_w[...], 1, 1).astype(HALF)
    grad_one_ref[...] = grad_one
    sums[0:1, :] += column_sum(grad_first * unit_one)
    sums[1:2, :] += column_sum(grad_rows * unit_two)
    sums[4:5, :] += column_sum(attn_low.astype(FLOAT))
    sums[5:6, :] += column_sum(branch_low.astype(FLOAT))
    sums[6:7, :] += column_sum(grad_first)
    sums[7:8, :] += column_sum(grad_rows)
    hidden_sum = column_sum(grad_hidden.astype(FLOAT))
    sums[8:9, :] += hidden_sum[:, :width]
    sums[9:10, :] += hidden_sum[:, width:]


def pack_second(offsets, place, slots_ref, grad_output, grad_expand, grad_shrink):
    width = grad_output.shape[1]
    for at, offset in enumerate(offsets):
        rows = owner_rows(offset, place, 16)
        slots_ref[at, 0:16, :] = grad_output[rows, :].astype(HALF)
        slots_ref[at, 16:32, :] = grad_expand[rows, :width].astype(HALF)
        slots_ref[at, 32:48, :] = grad_expand[rows, width:].astype(HALF)
        slots_ref[at, 48:80, :] = grad_shrink[owner_rows(offset, place, 32), :].astype(HALF)


def dense_kernel(offsets, place_ref, x_ref, mixed_ref, near_ref, far_ref, vec_ref, result_ref,
                 unit_one_ref, inv_one_ref, act_ref, slope_ref, unit_two_ref, inv_two_ref,
                 output_w, expand_w, shrink_w):
    @pl.when(pl.program_id(0) == 0)
    def _():
        unpack_second(offsets, place_ref[0], near_ref, far_ref, output_w, expand_w, shrink_w)

    unit_one, inv_one, _, act_low, slope, unit_two, inv_two, result = forward_rows(
        x_ref, mixed_ref, vec_ref, output_w, expand_w, shrink_w
    )
    result_ref[...] = result.astype(HALF)
    unit_one_ref[...] = unit_one
    inv_one_ref[...] = inv_one
    act_ref[...] = act_low
    slope_ref[...] = slope
    unit_two_ref[...] = unit_two
    inv_two_ref[...] = inv_two


def dense_back_kernel(offsets, place_ref, grad_ref, mixed_ref, vec_ref, unit_one_ref, inv_one_ref,
                      act_ref, slope_ref, unit_two_ref, inv_two_ref, output_w, expand_w, shrink_w,
                      grad_mixed_ref, grad_one_ref, slots_ref, sums, grad_output, grad_expand,
                      grad_shrink):
    @pl.when(pl.program_id(0) == 0)
    def _():
        for item in (sums, grad_output, grad_expand, grad_shrink):
            item[...] = jnp.zeros_like(item)

    unit_one = unit_one_ref[...]
    first_low = (unit_one * vec_ref[0:1, :] + vec_ref[6:7, :]).astype(HALF)
    kept = (unit_one, inv_one_ref[...], first_low, act_ref[...], slope_ref[...], unit_two_ref[...],
            inv_two_ref[...])
    backward_rows(grad_ref[...], mixed_ref, vec_ref, kept, output_w, expand_w, shrink_w,
                  grad_mixed_ref, grad_one_ref, grad_output, grad_expand, grad_shrink, sums)

    @pl.when(pl.program_id(0) == pl.num_programs(0) - 1)
    def _():
        pack_second(offsets, place_ref[0], slots_ref, grad_output, grad_expand, grad_shrink)


def dense_turn_kernel(offsets, place_ref, live_ref, weight_ref, x_ref, mixed_ref, near_ref, far_ref,
                      vec_ref, cot_ref, result_ref, grad_mixed_ref, grad_one_ref, slots_ref, sums,
                      output_w, expand_w, shrink_w, grad_output, grad_expand, grad_shrink):
    step = pl.program_id(0)

    @pl.when(step == 0)
    def _():
        unpack_second(offsets, place_ref[0], near_ref, far_ref, output_w, expand_w, shrink_w)
        for item in (sums, grad_output, grad_expand, grad_shrink):
            item[...] = jnp.zeros_like(item)

    *kept, result = forward_rows(x_ref, mixed_ref, vec_ref, output_w, expand_w, shrink_w)
    result_ref[...] = result.astype(HALF)
    rows = cot_ref.shape[0]
    slot = lax.broadcasted_iota(jnp.int32, (rows, 1), 0) + step * rows
    grad_rows = cot_ref[...].astype(FLOAT) * jnp.where(slot < live_ref[0], weight_ref[0], 0.0)
    backward_rows(grad_rows, mixed_ref, vec_ref, kept, output_w, expand_w, shrink_w,
                  grad_mixed_ref, grad_one_ref, grad_output, grad_expand, grad_shrink, sums)

    @pl.when(step == pl.num_programs(0) - 1)
    def _():
        pack_second(offsets, place_ref[0], slots_ref, grad_output, grad_expand, grad_shrink)


def by_rows(width):
    return pl.BlockSpec((ROW_BLOCK, width), lambda i, *p: (i, 0))


def fixed(*shape):
    return pl.BlockSpec(shape, lambda i, *p: (0,) * len(shape))


def dense_call(offsets, place, x, mixed, near, far, vectors):
    rows, width = x.shape
    like = jax.ShapeDtypeStruct
    return pl.pallas_call(
        functools.partial(dense_kernel, offsets),
        grid_spec=pltpu.PrefetchScalarGridSpec(
            num_scalar_prefetch=1,
            grid=(rows // ROW_BLOCK,),
            in_specs=[by_rows(width), by_rows(width), fixed(*near.shape), fixed(*far.shape),
                      fixed(16, width)],
            out_specs=[by_rows(width), by_rows(width), by_rows(1), by_rows(2 * width),
                       by_rows(2 * width), by_rows(width), by_rows(1), fixed(width, width),
                       fixed(width, 2 * width), fixed(2 * width, width)],
        ),
        out_shape=[like((rows, width), HALF), like((rows, width), FLOAT), like((rows, 1), FLOAT),
                   like((rows, 2 * width), HALF), like((rows, 2 * width), FLOAT),
                   like((rows, width), FLOAT), like((rows, 1), FLOAT), like((width, width), HALF),
                   like((width, 2 * width), HALF), like((2 * width, width), HALF)],
        compiler_params=pltpu.CompilerParams(vmem_limit_bytes=VMEM_LIMIT),
        cost_estimate=pl.CostEstimate(
            flops=10 * rows * width * width, bytes_accessed=16 * 1024 * 1024,
            transcendentals=4 * rows * width,
        ),
        name="dense",
    )(place, x, mixed, near, far, vectors)


def dense_back_call(offsets, place, grad_rows, mixed, vectors, kept, weights):
    rows, width = grad_rows.shape
    like = jax.ShapeDtypeStruct
    return pl.pallas_call(
        functools.partial(dense_back_kernel, offsets),
        grid_spec=pltpu.PrefetchScalarGridSpec(
            num_scalar_prefetch=1,
            grid=(rows // ROW_BLOCK,),
            in_specs=[by_rows(width), by_rows(width), fixed(16, width), by_rows(width), by_rows(1),
                      by_rows(2 * width), by_rows(2 * width), by_rows(width), by_rows(1),
                      fixed(width, width), fixed(width, 2 * width), fixed(2 * width, width)],
            out_specs=[by_rows(width), by_rows(width), fixed(32, 80, width), fixed(16, width)],
            scratch_shapes=[pltpu.VMEM((width, width), FLOAT), pltpu.VMEM((width, 2 * width), FLOAT),
                            pltpu.VMEM((2 * width, width), FLOAT)],
        ),
        out_shape=[like((rows, width), HALF), like((rows, width), FLOAT),
                   like((32, 80, width), HALF), like((16, width), FLOAT)],
        compiler_params=pltpu.CompilerParams(vmem_limit_bytes=VMEM_LIMIT),
        cost_estimate=pl.CostEstimate(
            flops=20 * rows * width * width, bytes_accessed=20 * 1024 * 1024, transcendentals=0
        ),
        name="dense_back",
    )(place, grad_rows, mixed, vectors, *kept, *weights)


def dense_turn_call(offsets, place, live, weight, x, mixed, near, far, vectors, cotangent):
    rows, width = x.shape
    like = jax.ShapeDtypeStruct
    return pl.pallas_call(
        functools.partial(dense_turn_kernel, offsets),
        grid_spec=pltpu.PrefetchScalarGridSpec(
            num_scalar_prefetch=3,
            grid=(rows // ROW_BLOCK,),
            in_specs=[by_rows(width), by_rows(width), fixed(*near.shape), fixed(*far.shape),
                      fixed(16, width), by_rows(width)],
            out_specs=[by_rows(width), by_rows(width), by_rows(width), fixed(32, 80, width),
                       fixed(16, width)],
            scratch_shapes=[pltpu.VMEM((width, width), HALF), pltpu.VMEM((width, 2 * width), HALF),
                            pltpu.VMEM((2 * width, width), HALF),
                            pltpu.VMEM((width, width), FLOAT), pltpu.VMEM((width, 2 * width), FLOAT),
                            pltpu.VMEM((2 * width, width), FLOAT)],
        ),
        out_shape=[like((rows, width), HALF), like((rows, width), HALF), like((rows, width), FLOAT),
                   like((32, 80, width), HALF), like((16, width), FLOAT)],
        compiler_params=pltpu.CompilerParams(vmem_limit_bytes=VMEM_LIMIT),
        cost_estimate=pl.CostEstimate(
            flops=30 * rows * width * width, bytes_accessed=16 * 1024 * 1024,
            transcendentals=4 * rows * width,
        ),
        name="dense_turn",
    )(place, live, weight, x, mixed, near, far, vectors, cotangent)


def attend_back_kernel(offsets, place_ref, x_ref, joint_ref, probs_ref, grad_mixed_ref, weight_ref,
                       grad_one_ref, slots_ref, grad_x_ref, sums_ref, x_turned, grad_scores,
                       grad_joint):
    head = pl.program_id(0)
    rows = x_ref.shape[0]
    head_size = grad_mixed_ref.shape[1]
    place = place_ref[0]

    @pl.when(head == 0)
    def _():
        x_turned[...] = jnp.transpose(x_ref[...])
        grad_x_ref[...] = grad_one_ref[...]
        grad_joint[CTX:, head_size:] = jnp.zeros((rows - CTX, 2 * head_size), HALF)

    keys = joint_ref[0, :CTX, head_size : 2 * head_size]
    values = joint_ref[0, :CTX, 2 * head_size :]
    keys_turned = jnp.transpose(keys)
    factor = head_size ** (-0.5)
    for start in range(0, rows, SCORE_BLOCK):
        span = slice(start, start + SCORE_BLOCK)
        grad_probs = product(values, grad_mixed_ref[span, :], 1, 1)
        probs = probs_ref[0, :, span].astype(FLOAT)
        weighted = probs * grad_probs
        grad_low = (factor * (weighted - probs * column_sum(weighted))).astype(HALF)
        grad_scores[:, span] = grad_low
        grad_joint[span, :head_size] = jnp.transpose(product(keys_turned, grad_low, 1, 0)).astype(
            HALF
        )
    grad_joint[:CTX, head_size : 2 * head_size] = product(
        grad_scores[...], joint_ref[0, :, :head_size], 1, 0
    ).astype(HALF)
    grad_joint[:CTX, 2 * head_size :] = product(probs_ref[0], grad_mixed_ref[...], 1, 0).astype(HALF)
    sums = column_sum(grad_joint[...].astype(FLOAT))
    sums_ref[0:1, :] = sums[:, :head_size]
    sums_ref[1:2, :] = sums[:, 2 * head_size :]
    grad_weight = product(x_turned[...], grad_joint[...], 1, 0)
    grad_low = grad_weight.astype(HALF)
    grad_x_ref[...] += product(grad_joint[...], weight_ref[0], 1, 1)
    holder = grad_scores
    holder[: grad_low.shape[0], : 3 * head_size] = grad_low
    for at, offset in enumerate(offsets):
        span = owner_rows(offset, place, 16)
        for piece in range(3):
            slots_ref[at, piece * 16 : (piece + 1) * 16, :] = holder[
                span, piece * head_size : (piece + 1) * head_size
            ]


def attend_back_call(offsets, place, x, joint, probs, grad_mixed, weight, grad_one):
    rows, width = x.shape
    head_size = width // HEADS
    like = jax.ShapeDtypeStruct
    return pl.pallas_call(
        functools.partial(attend_back_kernel, offsets),
        grid_spec=pltpu.PrefetchScalarGridSpec(
            num_scalar_prefetch=1,
            grid=(HEADS,),
            in_specs=[
                pl.BlockSpec((rows, width), lambda h, p: (0, 0)),
                pl.BlockSpec((1, rows, 3 * head_size), lambda h, p: (h, 0, 0)),
                pl.BlockSpec((1, CTX, rows), lambda h, p: (h, 0, 0)),
                pl.BlockSpec((rows, head_size), lambda h, p: (0, h)),
                pl.BlockSpec((1, width, 3 * head_size), lambda h, p: (h, 0, 0)),
                pl.BlockSpec((rows, width), lambda h, p: (0, 0)),
            ],
            out_specs=[
                pl.BlockSpec((32, 48, head_size), lambda h, p: (0, 0, h)),
                pl.BlockSpec((rows, width), lambda h, p: (0, 0)),
                pl.BlockSpec((8, head_size), lambda h, p: (0, h)),
            ],
            scratch_shapes=[pltpu.VMEM((width, rows), HALF), pltpu.VMEM((CTX, rows), HALF),
                            pltpu.VMEM((rows, 3 * head_size), HALF)],
        ),
        out_shape=[like((32, 48, width), HALF), like((rows, width), FLOAT),
                   like((8, width), FLOAT)],
        compiler_params=pltpu.CompilerParams(vmem_limit_bytes=VMEM_LIMIT),
        cost_estimate=pl.CostEstimate(
            flops=12 * rows * width * width + 8 * rows * CTX * width,
            bytes_accessed=20 * 1024 * 1024, transcendentals=0,
        ),
        name="attend_back",
    )(place, x, joint, probs, grad_mixed, weight, grad_one)


class Route:
    def __init__(self, steps, inner_size):
        self.steps = steps
        masks = [bit * inner_size if axis == "dp" else bit for axis, size, bit in steps]
        self.count = 1 << len(steps)
        self.offset = [
            sum(mask for at, mask in enumerate(masks) if place >> at & 1)
            for place in range(self.count)
        ]

    def swap(self, at, payload):
        axis, size, bit = self.steps[at]
        return lax.ppermute(payload, axis, [(one, one ^ bit) for one in range(size)])


def routes(outer_size, inner_size):
    outer = [("dp", outer_size, 1 << at) for at in reversed(range(outer_size.bit_length() - 1))]
    inner = [("fsdp", inner_size, 1 << at) for at in reversed(range(inner_size.bit_length() - 1))]
    first = inner + outer
    second = inner[:-1] + outer[:-1] + inner[-1:] + outer[-1:]
    return (Route(first, inner_size), Route(second, inner_size))


def spread(route, block, shared=None):
    rows, width = block.shape
    last = len(route.steps) - 1
    for at in range(last + 1):
        held = block.shape[0]
        payload = block if shared is None else jnp.concatenate([block, shared])
        got = route.swap(at, payload)
        if shared is not None:
            shared = shared + got[held:]
        if at == last:
            far = got[:held].reshape(route.count // 2, rows, width)
            return (block.reshape(route.count // 2, rows, width), far, shared)
        block = jnp.concatenate([block, got[:held]])


def gather_sum(route, slots, shared=None):
    count, rows, width = slots.shape
    block = slots.reshape(count * rows, width)
    for at in reversed(range(len(route.steps))):
        half = block.shape[0] // 2
        payload = block[half:] if shared is None else jnp.concatenate([block[half:], shared])
        got = route.swap(at, payload)
        block = (block[:half].astype(FLOAT) + got[:half].astype(FLOAT)).astype(HALF)
        if shared is not None:
            shared = (shared.astype(FLOAT) + got[half:].astype(FLOAT)).astype(HALF)
    return (block, shared)


def split_parts(slots, parts):
    ends = np.cumsum((0,) + parts)
    return [slots[:, ends[at] : ends[at + 1]] for at in range(len(parts))]


def coarse(route, near, far, place, parts):
    position = np.zeros((route.count,), np.int32)
    for at, off in enumerate(route.offset):
        position[off] = at
    owners = jnp.arange(route.count, dtype=jnp.int32)
    slots = jnp.take(jnp.concatenate([near, far]), jnp.asarray(position)[owners ^ place], axis=0)
    fine = tuple(part * OWNERS // route.count for part in parts)
    slots = jnp.concatenate(
        [
            piece.reshape(OWNERS, part, piece.shape[2])
            for part, piece in zip(parts, split_parts(slots, fine), strict=True)
        ],
        axis=1,
    )
    return (slots[: OWNERS // 2], slots[OWNERS // 2 :])


def fine(route, slots, place, parts):
    each = [part * OWNERS // route.count for part in parts]
    slots = jnp.concatenate(
        [
            piece.reshape(route.count, rows, piece.shape[2])
            for rows, piece in zip(each, split_parts(slots, parts), strict=True)
        ],
        axis=1,
    )
    return jnp.take(slots, jnp.asarray(route.offset, jnp.int32) ^ place, axis=0)


def wide_to_rows(shard, width):
    return jnp.concatenate(
        [shard[:, at * width : (at + 1) * width] for at in range(shard.shape[1] // width)]
    )


def rows_to_wide(rows, pieces):
    each = rows.shape[0] // pieces
    return jnp.concatenate([rows[at * each : (at + 1) * each] for at in range(pieces)], axis=1)


def advance(master, moment, average, grad, momentum, step_rate, decay_now):
    new_moment = momentum * moment + grad
    new_master = master - step_rate * (grad + momentum * new_moment)
    new_average = decay_now * average + (1.0 - decay_now) * new_master
    return (new_moment, new_average, new_master, new_master.astype(jnp.bfloat16))


def shards(
    tokens,
    cotangent,
    dataset_ids,
    query_counts,
    learn_rate,
    momentum_coef,
    average_decay,
    step_count,
    attend_weight,
    attend_momentum,
    attend_average,
    output_weight,
    output_momentum,
    output_average,
    expand_weight,
    expand_momentum,
    expand_average,
    shrink_weight,
    shrink_momentum,
    shrink_average,
    norm_gains,
    gains_momentum,
    gains_average,
    bias_rows,
    bias_momentum,
    bias_average,
):
    masters = (attend_weight, output_weight, expand_weight, shrink_weight, norm_gains, bias_rows)
    moments = (
        attend_momentum,
        output_momentum,
        expand_momentum,
        shrink_momentum,
        gains_momentum,
        bias_momentum,
    )
    averages = (
        attend_average,
        output_average,
        expand_average,
        shrink_average,
        gains_average,
        bias_average,
    )
    layers = attend_weight.shape[0]
    width = attend_weight.shape[2] // 3
    each = attend_weight.shape[1]
    outer_size = lax.axis_size("dp")
    inner_size = lax.axis_size("fsdp")
    everyone = outer_size * inner_size
    place = lax.axis_index("dp") * inner_size + lax.axis_index("fsdp")
    first_route, second_route = routes(outer_size, inner_size)
    direct = everyone == OWNERS
    plain = tuple(range(OWNERS))
    first_order = tuple(first_route.offset) if direct else plain
    second_order = tuple(second_route.offset) if direct else plain
    where = (place if direct else jnp.zeros_like(place)).astype(jnp.int32).reshape(1)
    low = lambda item: item.astype(HALF)

    onehot = (dataset_ids[:, None] == jnp.arange(NDS, dtype=jnp.int32)[None, :]).astype(FLOAT)
    own = jnp.concatenate(
        [low(item[at]) for at in range(layers) for item in (norm_gains, bias_rows)]
    )
    shared = lax.dynamic_update_slice(
        jnp.zeros((24, width), HALF), own, (0, place * own.shape[1])
    )
    shared = shared.at[20, :NDS].set(low(jnp.sum(onehot, axis=0)))

    weights = []
    for at in range(layers):
        first = wide_to_rows(low(attend_weight[at]), width)
        second = jnp.concatenate(
            [
                low(output_weight[at]),
                wide_to_rows(low(expand_weight[at]), width),
                low(shrink_weight[at]),
            ]
        )
        if at == 0:
            first_near, first_far, shared = spread(first_route, first, shared)
        else:
            first_near, first_far, _ = spread(first_route, first)
        second_near, second_far, _ = spread(second_route, second)
        if not direct:
            first_near, first_far = coarse(first_route, first_near, first_far, place, FIRST_PARTS)
            second_near, second_far = coarse(
                second_route, second_near, second_far, place, SECOND_PARTS
            )
        weights.append((first_near, first_far, second_near, second_far))
    shared = shared.astype(FLOAT)
    vectors = [jnp.pad(shared[10 * at : 10 * at + 10], ((0, 6), (0, 0))) for at in range(layers)]
    counts = shared[20, :NDS]
    own_count = jnp.sum(onehot * counts[None, :], axis=1)
    row_weight = jnp.sum(counts) / (NDS * own_count)

    current = tokens[0]
    kept = []
    for at in range(layers):
        first_near, first_far, second_near, second_far = weights[at]
        joint, probs, mixed, attend_w = attend_call(
            first_order, where, current, first_near, first_far, vectors[at]
        )
        kept.append([current, joint, probs, mixed, attend_w])
        if at + 1 < layers:
            current, *rest = dense_call(
                second_order, where, current, mixed, second_near, second_far, vectors[at]
            )
            kept[at].extend([rest[:6], rest[6:]])
    shard_grads = [None] * layers
    for at in reversed(range(layers)):
        start, joint, probs, mixed, attend_w = kept[at][:5]
        if at + 1 == layers:
            result, grad_mixed, grad_one, second_slots, sums = dense_turn_call(
                second_order,
                where,
                query_counts + CTX,
                row_weight,
                start,
                mixed,
                weights[at][2],
                weights[at][3],
                vectors[at],
                cotangent[0],
            )
        else:
            grad_mixed, grad_one, second_slots, sums = dense_back_call(
                second_order, where, grad_rows, mixed, vectors[at], kept[at][5], kept[at][6]
            )
        first_slots, grad_rows, joint_sums = attend_back_call(
            first_order, where, start, joint, probs, grad_mixed, attend_w, grad_one
        )
        if not direct:
            second_slots = fine(second_route, second_slots, place, SECOND_PARTS)
            first_slots = fine(first_route, first_slots, place, FIRST_PARTS)
        second_sum, _ = gather_sum(second_route, second_slots)
        small = low(jnp.concatenate([sums[:2], joint_sums[:2], sums[4:]]))
        first_sum, small_sum = gather_sum(first_route, first_slots, small)
        own_small = lax.dynamic_slice(small_sum, (0, place * each), (10, each)).astype(FLOAT)
        shard_grads[at] = (
            rows_to_wide(first_sum, 3).astype(FLOAT),
            second_sum[:each].astype(FLOAT),
            rows_to_wide(second_sum[each : 3 * each], 2).astype(FLOAT),
            second_sum[3 * each :].astype(FLOAT),
            own_small[:2],
            own_small[2:],
        )
    step_value = step_count[0].astype(jnp.float32)
    decay_now = average_decay[0] * (1.0 + step_value) / (4.0 + step_value)
    outputs = [result[None], grad_rows[None]]
    for group_index in range(6):
        stacked = jnp.stack(
            [shard_grads[at][group_index] for at in range(layers)]
        )
        outputs.extend(
            advance(
                masters[group_index],
                moments[group_index],
                averages[group_index],
                stacked,
                momentum_coef[0],
                learn_rate[0],
                decay_now,
            )
        )
    return tuple(outputs)


def solution(mesh):
    return jax.shard_map(
        shards,
        mesh=mesh,
        in_specs=(
            P(("dp", "fsdp"), None, None),
            P(("dp", "fsdp"), None, None),
            P(("dp", "fsdp")),
            P(("dp", "fsdp")),
            P(),
            P(),
            P(),
            P(),
            P(None, ("dp", "fsdp"), None),
            P(None, ("dp", "fsdp"), None),
            P(None, ("dp", "fsdp"), None),
            P(None, ("dp", "fsdp"), None),
            P(None, ("dp", "fsdp"), None),
            P(None, ("dp", "fsdp"), None),
            P(None, ("dp", "fsdp"), None),
            P(None, ("dp", "fsdp"), None),
            P(None, ("dp", "fsdp"), None),
            P(None, ("dp", "fsdp"), None),
            P(None, ("dp", "fsdp"), None),
            P(None, ("dp", "fsdp"), None),
            P(None, None, ("dp", "fsdp")),
            P(None, None, ("dp", "fsdp")),
            P(None, None, ("dp", "fsdp")),
            P(None, None, ("dp", "fsdp")),
            P(None, None, ("dp", "fsdp")),
            P(None, None, ("dp", "fsdp")),
        ),
        out_specs=(
            P(("dp", "fsdp"), None, None),
            P(("dp", "fsdp"), None, None),
            P(None, ("dp", "fsdp"), None),
            P(None, ("dp", "fsdp"), None),
            P(None, ("dp", "fsdp"), None),
            P(None, ("dp", "fsdp"), None),
            P(None, ("dp", "fsdp"), None),
            P(None, ("dp", "fsdp"), None),
            P(None, ("dp", "fsdp"), None),
            P(None, ("dp", "fsdp"), None),
            P(None, ("dp", "fsdp"), None),
            P(None, ("dp", "fsdp"), None),
            P(None, ("dp", "fsdp"), None),
            P(None, ("dp", "fsdp"), None),
            P(None, ("dp", "fsdp"), None),
            P(None, ("dp", "fsdp"), None),
            P(None, ("dp", "fsdp"), None),
            P(None, ("dp", "fsdp"), None),
            P(None, None, ("dp", "fsdp")),
            P(None, None, ("dp", "fsdp")),
            P(None, None, ("dp", "fsdp")),
            P(None, None, ("dp", "fsdp")),
            P(None, None, ("dp", "fsdp")),
            P(None, None, ("dp", "fsdp")),
            P(None, None, ("dp", "fsdp")),
            P(None, None, ("dp", "fsdp")),
        ),
        check_vma=False,
    )
```

```python
import functools

import jax
import jax.numpy as jnp
import numpy as np
from jax import lax
from jax.experimental import pallas as pl
from jax.experimental.pallas import tpu as pltpu
from jax.sharding import PartitionSpec as P

HEADS = 4
CTX = 896
NDS = 8
EPS = 1e-05
OWNERS = 32
AXES = ("dp", "fsdp")

CHAIN = (0, 2, 4, 6)
SQUARE = (0, 1, 16, 17)
CORE = 8
ORDER = tuple(core ^ side ^ link for core in (0, CORE) for side in SQUARE for link in CHAIN)

FIRST_ROWS = 64
SECOND_ROWS = 96

SCORE_BLOCK = 256
ROW_BLOCK = 256
ROOT_HALF = 0.7071067811865476
PDF_PEAK = 0.3989422804014327
VMEM_LIMIT = 60 * 1024 * 1024
FLOAT = jnp.float32
HALF = jnp.bfloat16
LIKE = jax.ShapeDtypeStruct


def product(left, right, left_dim, right_dim):
    return lax.dot_general(
        left, right, (((left_dim,), (right_dim,)), ((), ())), preferred_element_type=FLOAT
    )


def owner_rows(offset, place, rows):
    return pl.ds(pl.multiple_of((offset ^ place) * rows, rows), rows)


def params(limit=VMEM_LIMIT):
    return pltpu.CompilerParams(vmem_limit_bytes=limit)


def pack_kernel(place_ref, ids_ref, attend_ref, output_ref, expand_ref, shrink_ref, gains_ref,
                bias_ref, near_first_ref, near_second_ref, late_ref, small):
    width = near_first_ref.shape[1]
    each = gains_ref.shape[2]
    lane = lax.broadcasted_iota(jnp.int32, (each, width), 1)
    own = lax.broadcasted_iota(jnp.int32, (each, width), 0) + place_ref[0] * each
    pick = (lane == own).astype(HALF)
    lanes = lax.broadcasted_iota(jnp.int32, (1, width), 1)

    for layer in range(attend_ref.shape[0]):
        first, second, start = (
            (near_first_ref, near_second_ref, 0) if layer == 0 else (late_ref, late_ref, FIRST_ROWS)
        )
        gains = product(gains_ref[layer].astype(HALF), pick, 1, 0)
        biases = product(bias_ref[layer].astype(HALF), pick, 1, 0)
        for piece in range(3):
            first[piece * 16 : (piece + 1) * 16, :] = attend_ref[
                layer, :, piece * width : (piece + 1) * width
            ].astype(HALF)
        small[...] = jnp.zeros_like(small)
        small[0:2, :] = biases[0:2, :]
        first[48:64, :] = small[...].astype(HALF)
        second[start : start + 16, :] = output_ref[layer].astype(HALF)
        for piece in range(2):
            second[start + (piece + 1) * 16 : start + (piece + 2) * 16, :] = expand_ref[
                layer, :, piece * width : (piece + 1) * width
            ].astype(HALF)
        second[start + 48 : start + 80, :] = shrink_ref[layer].astype(HALF)
        small[0:2, :] = gains
        small[2:8, :] = biases[2:8, :]
        small[8:9, :] = (lanes == ids_ref[0]).astype(FLOAT)
        second[start + 80 : start + 96, :] = small[...].astype(HALF)


def pack_call(place, ids, masters):
    width = masters[1].shape[2]
    rows = (FIRST_ROWS, SECOND_ROWS, FIRST_ROWS + SECOND_ROWS)
    return pl.pallas_call(
        pack_kernel,
        in_specs=[pl.BlockSpec(memory_space=pltpu.SMEM)] * 2
        + [pl.BlockSpec(memory_space=pltpu.VMEM)] * 6,
        out_specs=[pl.BlockSpec(memory_space=pltpu.VMEM)] * 3,
        out_shape=[LIKE((count, width), HALF) for count in rows],
        scratch_shapes=[pltpu.VMEM((16, width), FLOAT)],
        cost_estimate=pl.CostEstimate(flops=0, bytes_accessed=1 << 20, transcendentals=0),
        name="pack",
    )(place, ids, *masters)


def join_kernel(cuts, count, *refs):
    sources, targets, sems = refs[:count], refs[count:-1], refs[-1]
    copies = []
    for at, source in enumerate(sources):
        for to, (start, rows) in enumerate(cuts):
            if len(source.shape) == 2:
                piece = (source.at[pl.ds(start, rows)], targets[to].at[at])
            else:
                piece = (source, targets[to].at[pl.ds(at * source.shape[0], source.shape[0])])
            copies.append(pltpu.make_async_copy(*piece, sems.at[at, to]))
    for piece in copies:
        piece.start()
    for piece in copies:
        piece.wait()


def join_call(blocks, cuts):
    head, width = blocks[0].shape[:-2], blocks[0].shape[-1]
    slots = len(blocks) * (head[0] if head else 1)
    anywhere = pl.BlockSpec(memory_space=pl.ANY)
    return pl.pallas_call(
        functools.partial(join_kernel, cuts, len(blocks)),
        in_specs=[anywhere] * len(blocks),
        out_specs=[anywhere] * len(cuts),
        out_shape=[LIKE((slots, rows, width), HALF) for _, rows in cuts],
        scratch_shapes=[pltpu.SemaphoreType.DMA((len(blocks), len(cuts)))],
        cost_estimate=pl.CostEstimate(flops=0, bytes_accessed=1 << 20, transcendentals=0),
        name="join",
    )(*blocks)


def block_sum(refs):
    total = refs[0][...].astype(FLOAT)
    for ref in refs[1:]:
        total = total + ref[...].astype(FLOAT)
    return total


def core_sum_kernel(*refs):
    for at in range(4):
        refs[8 + at][...] = (refs[at][...].astype(FLOAT) + refs[4 + at][...].astype(FLOAT)).astype(
            HALF
        )


def core_sum_call(kept, got):
    _, rows, width = kept.shape

    def view(at):
        return pl.BlockSpec((1, rows, width), lambda i: (4 * at + i, 0, 0))

    return pl.pallas_call(
        core_sum_kernel,
        grid=(4,),
        in_specs=[view(at) for at in range(4)] * 2,
        out_specs=[pl.BlockSpec((1, rows, width), lambda i: (i, 0, 0))] * 4,
        out_shape=[LIKE((4, rows, width), HALF)] * 4,
        cost_estimate=pl.CostEstimate(flops=0, bytes_accessed=1 << 22, transcendentals=0),
        name="core_sum",
    )(*[kept] * 4, *[got] * 4)


def square_sum_kernel(rows, *refs):
    outs = refs[-4:]
    start = 0
    for at, count in enumerate(rows):
        total = block_sum(refs[4 * at : 4 * at + 4])
        for to, out in enumerate(outs):
            out[start : start + count, :] = total[to].astype(HALF)
        start += count


def square_sum_call(*pieces):
    rows = tuple(stacks[0].shape[1] for stacks in pieces)
    shape = LIKE((sum(rows), pieces[0][0].shape[2]), HALF)
    return pl.pallas_call(
        functools.partial(square_sum_kernel, rows),
        out_shape=[shape] * 4,
        compiler_params=params(32 * 1024 * 1024),
        cost_estimate=pl.CostEstimate(flops=0, bytes_accessed=1 << 21, transcendentals=0),
        name="square_sum",
    )(*[stack for stacks in pieces for stack in stacks])


def swap(block, offset):
    return lax.ppermute(block, AXES, [(one, one ^ offset) for one in range(OWNERS)])


def swaps(block, offsets):
    return [swap(block, offset) for offset in offsets]


def slot_places(slot_refs):
    for at, offset in enumerate(ORDER):
        yield slot_refs[min(at // 4, 4)], at % 4 if at < 16 else at - 16, offset


def small_rows(slot_refs, start):
    total = None
    for slots in slot_refs:
        for at in range(slots.shape[0]):
            block = slots[at, start : start + 16, :].astype(FLOAT)
            total = block if total is None else total + block
    return total


def attend_kernel(place_ref, x_ref, *refs):
    slot_refs = refs[:5]
    joint_ref, probs_ref, mixed_ref, weight_ref = refs[5:]
    head_size = mixed_ref.shape[1]
    place = place_ref[0]

    for slots, at, offset in slot_places(slot_refs):
        rows = owner_rows(offset, place, 16)
        for piece in range(3):
            weight_ref[0, rows, piece * head_size : (piece + 1) * head_size] = slots[
                at, piece * 16 : (piece + 1) * 16, :
            ]
    zeros = jnp.zeros((1, head_size), FLOAT)
    small = small_rows(slot_refs, 48)
    shift = jnp.concatenate([small[0:1, :], zeros, small[1:2, :]], axis=1)
    joint_ref[0] = (product(x_ref[...], weight_ref[0], 1, 0) + shift).astype(HALF)
    keys = joint_ref[0, :CTX, head_size : 2 * head_size]
    values = joint_ref[0, :CTX, 2 * head_size :]
    values_turned = jnp.transpose(values)
    factor = head_size ** (-0.5) * 1.4426950408889634
    for start in range(0, x_ref.shape[0], SCORE_BLOCK):
        span = slice(start, start + SCORE_BLOCK)
        queries = joint_ref[0, span, :head_size]
        scores = product(keys, queries, 1, 1)
        top = jnp.max(scores, axis=0, keepdims=True)
        grown = jnp.exp2((scores - top) * factor)
        total = jnp.sum(grown, axis=0, keepdims=True)
        probs = (grown * (1.0 / total)).astype(HALF)
        probs_ref[0, :, span] = probs
        mixed_ref[span, :] = jnp.transpose(product(values_turned, probs, 1, 0)).astype(HALF)


def attend_call(place, x, slots, base, heads):
    rows, width = x.shape
    head_size = width // HEADS
    return pl.pallas_call(
        attend_kernel,
        grid_spec=pltpu.PrefetchScalarGridSpec(
            num_scalar_prefetch=1,
            grid=(heads,),
            in_specs=[pl.BlockSpec((rows, width), lambda h, p: (0, 0))]
            + [pl.BlockSpec((part.shape[0], FIRST_ROWS, head_size), lambda h, p: (0, 0, h + base))
               for part in slots],
            out_specs=[
                pl.BlockSpec((1, rows, 3 * head_size), lambda h, p: (h, 0, 0)),
                pl.BlockSpec((1, CTX, rows), lambda h, p: (h, 0, 0)),
                pl.BlockSpec((rows, head_size), lambda h, p: (0, h)),
                pl.BlockSpec((1, width, 3 * head_size), lambda h, p: (h, 0, 0)),
            ],
        ),
        out_shape=[
            LIKE((heads, rows, 3 * head_size), HALF),
            LIKE((heads, CTX, rows), HALF),
            LIKE((rows, heads * head_size), HALF),
            LIKE((heads, width, 3 * head_size), HALF),
        ],
        compiler_params=params(),
        cost_estimate=pl.CostEstimate(
            flops=heads * (2 * rows * width * 3 * head_size + 4 * rows * CTX * head_size),
            bytes_accessed=heads * 4 * 1024 * 1024,
            transcendentals=heads * rows * CTX,
        ),
        name="attend",
    )(place, x, *slots)


def unpack_second(place, slot_refs, output_w, expand_w, shrink_w, vec_ref):
    width = output_w.shape[1]
    for slots, at, offset in slot_places(slot_refs):
        rows = owner_rows(offset, place, 16)
        output_w[rows, :] = slots[at, 0:16, :]
        expand_w[rows, :width] = slots[at, 16:32, :]
        expand_w[rows, width:] = slots[at, 32:48, :]
        shrink_w[owner_rows(offset, place, 32), :] = slots[at, 48:80, :]
    vec_ref[...] = small_rows(slot_refs, 80)


def row_mean(rows):
    return jnp.mean(rows, axis=-1, keepdims=True)


def normalize(rows):
    centred = rows - row_mean(rows)
    inv_std = lax.rsqrt(row_mean(centred * centred) + EPS)
    return (centred * inv_std, inv_std)


def column_spans(refs):
    start = 0
    for ref in refs:
        yield ref, slice(start, start + ref.shape[1])
        start += ref.shape[1]


def forward_rows(x_ref, mixed_refs, vec_ref, output_w, expand_w, shrink_w):
    attn_out = vec_ref[2:3, :]
    for mixed_ref, span in column_spans(mixed_refs):
        attn_out = attn_out + product(mixed_ref[...], output_w[span, :], 1, 0)
    unit_one, inv_one = normalize(x_ref[...].astype(FLOAT) + attn_out)
    first_norm = unit_one * vec_ref[0:1, :] + vec_ref[4:5, :]
    first_low = first_norm.astype(HALF)
    shift = jnp.concatenate([vec_ref[6:7, :], vec_ref[7:8, :]], axis=1)
    hidden = product(first_low, expand_w[...], 1, 0) + shift
    normal_cdf = 0.5 * (1.0 + lax.erf(hidden * ROOT_HALF))
    act_low = (hidden * normal_cdf).astype(HALF)
    slope = normal_cdf + hidden * (jnp.exp(-0.5 * hidden * hidden) * PDF_PEAK)
    branch = product(act_low, shrink_w[...], 1, 0) + vec_ref[3:4, :]
    unit_two, inv_two = normalize(first_norm + branch)
    result = unit_two * vec_ref[1:2, :] + vec_ref[5:6, :]
    return (unit_one, inv_one, first_low, act_low, slope, unit_two, inv_two, result)


def column_sum(rows):
    return jnp.sum(rows, axis=0, keepdims=True)


def backward_rows(grad_rows, mixed_refs, vec_ref, kept, output_w, expand_w, shrink_w,
                  grad_mixed_ref, grad_one_ref, grad_output, grad_expand, grad_shrink, sums):
    unit_one, inv_one, first_low, act_low, slope, unit_two, inv_two = kept
    width = grad_rows.shape[1]

    def layer_norm_back(rows, unit_rows, inv_std, gain):
        scaled = rows * gain
        return inv_std * (scaled - row_mean(scaled) - unit_rows * row_mean(scaled * unit_rows))

    grad_two = layer_norm_back(grad_rows, unit_two, inv_two, vec_ref[1:2, :])
    branch_low = grad_two.astype(HALF)
    grad_shrink[...] += product(act_low, branch_low, 0, 0)
    grad_hidden = (product(branch_low, shrink_w[...], 1, 1) * slope).astype(HALF)
    grad_expand[...] += product(first_low, grad_hidden, 0, 0)
    grad_first = grad_two + product(grad_hidden, expand_w[...], 1, 1)
    grad_one = layer_norm_back(grad_first, unit_one, inv_one, vec_ref[0:1, :])
    attn_low = grad_one.astype(HALF)
    for mixed_ref, span in column_spans(mixed_refs):
        grad_output[span, :] += product(mixed_ref[...], attn_low, 0, 0)
    grad_mixed_ref[...] = product(attn_low, output_w[...], 1, 1).astype(HALF)
    grad_one_ref[...] = grad_one
    sums[0:1, :] += column_sum(grad_first * unit_one)
    sums[1:2, :] += column_sum(grad_rows * unit_two)
    sums[2:3, :] += column_sum(attn_low.astype(FLOAT))
    sums[3:4, :] += column_sum(branch_low.astype(FLOAT))
    sums[4:5, :] += column_sum(grad_first)
    sums[5:6, :] += column_sum(grad_rows)
    hidden_sum = column_sum(grad_hidden.astype(FLOAT))
    sums[6:7, :] += hidden_sum[:, :width]
    sums[7:8, :] += hidden_sum[:, width:]


def pack_second(place, kept_ref, sent_ref, grad_output, grad_expand, grad_shrink, sums):
    width = grad_output.shape[1]
    small = sums[...].astype(HALF)
    for at, offset in enumerate(ORDER):
        slots_ref = kept_ref if at < 16 else sent_ref
        at = at % 16
        rows = owner_rows(offset, place, 16)
        slots_ref[at, 0:16, :] = grad_output[rows, :].astype(HALF)
        slots_ref[at, 16:32, :] = grad_expand[rows, :width].astype(HALF)
        slots_ref[at, 32:48, :] = grad_expand[rows, width:].astype(HALF)
        slots_ref[at, 48:80, :] = grad_shrink[owner_rows(offset, place, 32), :].astype(HALF)
        slots_ref[at, 80:96, :] = small


def dense_kernel(count, place_ref, x_ref, *refs):
    mixed_refs, slot_refs = refs[:count], refs[count : count + 5]
    (result_ref, unit_one_ref, inv_one_ref, act_ref, slope_ref, unit_two_ref, inv_two_ref, output_w,
     expand_w, shrink_w, vec_ref) = refs[count + 5 :]

    @pl.when(pl.program_id(0) == 0)
    def _():
        unpack_second(place_ref[0], slot_refs, output_w, expand_w, shrink_w, vec_ref)

    unit_one, inv_one, _, act_low, slope, unit_two, inv_two, result = forward_rows(
        x_ref, mixed_refs, vec_ref, output_w, expand_w, shrink_w
    )
    result_ref[...] = result.astype(HALF)
    unit_one_ref[...] = unit_one
    inv_one_ref[...] = inv_one
    act_ref[...] = act_low
    slope_ref[...] = slope
    unit_two_ref[...] = unit_two
    inv_two_ref[...] = inv_two


def clear(*items):
    for item in items:
        item[...] = jnp.zeros_like(item)


def dense_back_kernel(count, place_ref, grad_ref, *refs):
    mixed_refs = refs[:count]
    (unit_one_ref, inv_one_ref, act_ref, slope_ref, unit_two_ref, inv_two_ref, output_w, expand_w,
     shrink_w, vec_ref, grad_mixed_ref, grad_one_ref, kept_ref, sent_ref, sums, grad_output,
     grad_expand, grad_shrink) = refs[count:]

    @pl.when(pl.program_id(0) == 0)
    def _():
        clear(sums, grad_output, grad_expand, grad_shrink)

    unit_one = unit_one_ref[...]
    first_low = (unit_one * vec_ref[0:1, :] + vec_ref[4:5, :]).astype(HALF)
    kept = (unit_one, inv_one_ref[...], first_low, act_ref[...], slope_ref[...], unit_two_ref[...],
            inv_two_ref[...])
    backward_rows(grad_ref[...], mixed_refs, vec_ref, kept, output_w, expand_w, shrink_w,
                  grad_mixed_ref, grad_one_ref, grad_output, grad_expand, grad_shrink, sums)

    @pl.when(pl.program_id(0) == pl.num_programs(0) - 1)
    def _():
        pack_second(place_ref[0], kept_ref, sent_ref, grad_output, grad_expand, grad_shrink, sums)


def dense_turn_kernel(count, place_ref, live_ref, ids_ref, x_ref, *refs):
    mixed_refs, slot_refs = refs[:count], refs[count : count + 5]
    (cot_ref, result_ref, grad_mixed_ref, grad_one_ref, kept_ref, sent_ref, output_w, expand_w,
     shrink_w, vec_ref, grad_output, grad_expand, grad_shrink, sums) = refs[count + 5 :]
    step = pl.program_id(0)

    @pl.when(step == 0)
    def _():
        unpack_second(place_ref[0], slot_refs, output_w, expand_w, shrink_w, vec_ref)
        clear(sums, grad_output, grad_expand, grad_shrink)

    *kept, result = forward_rows(x_ref, mixed_refs, vec_ref, output_w, expand_w, shrink_w)
    result_ref[...] = result.astype(HALF)
    counts = vec_ref[8:9, :]
    lanes = lax.broadcasted_iota(jnp.int32, counts.shape, 1)
    own_count = jnp.sum(jnp.where(lanes == ids_ref[0], counts, 0.0), axis=1, keepdims=True)
    row_weight = jnp.sum(counts, axis=1, keepdims=True) / (NDS * own_count)
    rows = cot_ref.shape[0]
    slot = lax.broadcasted_iota(jnp.int32, (rows, 1), 0) + step * rows
    grad_rows = cot_ref[...].astype(FLOAT) * jnp.where(slot < live_ref[0], row_weight, 0.0)
    backward_rows(grad_rows, mixed_refs, vec_ref, kept, output_w, expand_w, shrink_w,
                  grad_mixed_ref, grad_one_ref, grad_output, grad_expand, grad_shrink, sums)

    @pl.when(step == pl.num_programs(0) - 1)
    def _():
        pack_second(place_ref[0], kept_ref, sent_ref, grad_output, grad_expand, grad_shrink, sums)


def by_rows(width):
    return pl.BlockSpec((ROW_BLOCK, width), lambda i, *p: (i, 0))


def fixed(*shape):
    return pl.BlockSpec(shape, lambda i, *p: (0,) * len(shape))


def weight_shapes(width):
    return [(width, width), (width, 2 * width), (2 * width, width)]


def dense_call(place, x, mixed, slots):
    rows, width = x.shape
    weights = weight_shapes(width)
    return pl.pallas_call(
        functools.partial(dense_kernel, len(mixed)),
        grid_spec=pltpu.PrefetchScalarGridSpec(
            num_scalar_prefetch=1,
            grid=(rows // ROW_BLOCK,),
            in_specs=[by_rows(width)]
            + [by_rows(part.shape[1]) for part in mixed]
            + [fixed(*part.shape) for part in slots],
            out_specs=[by_rows(width), by_rows(width), by_rows(1), by_rows(2 * width),
                       by_rows(2 * width), by_rows(width), by_rows(1)]
            + [fixed(*shape) for shape in weights]
            + [fixed(16, width)],
        ),
        out_shape=[LIKE((rows, width), HALF), LIKE((rows, width), FLOAT), LIKE((rows, 1), FLOAT),
                   LIKE((rows, 2 * width), HALF), LIKE((rows, 2 * width), FLOAT),
                   LIKE((rows, width), FLOAT), LIKE((rows, 1), FLOAT)]
        + [LIKE(shape, HALF) for shape in weights]
        + [LIKE((16, width), FLOAT)],
        compiler_params=params(),
        cost_estimate=pl.CostEstimate(
            flops=10 * rows * width * width, bytes_accessed=16 * 1024 * 1024,
            transcendentals=4 * rows * width,
        ),
        name="dense",
    )(place, x, *mixed, *slots)


def dense_back_call(place, grad_rows, mixed, kept):
    rows, width = grad_rows.shape
    weights = weight_shapes(width)
    return pl.pallas_call(
        functools.partial(dense_back_kernel, len(mixed)),
        grid_spec=pltpu.PrefetchScalarGridSpec(
            num_scalar_prefetch=1,
            grid=(rows // ROW_BLOCK,),
            in_specs=[by_rows(width)]
            + [by_rows(part.shape[1]) for part in mixed]
            + [by_rows(width), by_rows(1), by_rows(2 * width), by_rows(2 * width), by_rows(width),
               by_rows(1)]
            + [fixed(*shape) for shape in weights]
            + [fixed(16, width)],
            out_specs=[by_rows(width), by_rows(width)] + [fixed(16, SECOND_ROWS, width)] * 2,
            scratch_shapes=[pltpu.VMEM((16, width), FLOAT)]
            + [pltpu.VMEM(shape, FLOAT) for shape in weights],
        ),
        out_shape=[LIKE((rows, width), HALF), LIKE((rows, width), FLOAT)]
        + [LIKE((16, SECOND_ROWS, width), HALF)] * 2,
        compiler_params=params(),
        cost_estimate=pl.CostEstimate(
            flops=20 * rows * width * width, bytes_accessed=20 * 1024 * 1024, transcendentals=0
        ),
        name="dense_back",
    )(place, grad_rows, *mixed, *kept)


def dense_turn_call(place, live, ids, x, mixed, slots, cotangent):
    rows, width = x.shape
    weights = weight_shapes(width)
    return pl.pallas_call(
        functools.partial(dense_turn_kernel, len(mixed)),
        grid_spec=pltpu.PrefetchScalarGridSpec(
            num_scalar_prefetch=3,
            grid=(rows // ROW_BLOCK,),
            in_specs=[by_rows(width)]
            + [by_rows(part.shape[1]) for part in mixed]
            + [fixed(*part.shape) for part in slots]
            + [by_rows(width)],
            out_specs=[by_rows(width)] * 3 + [fixed(16, SECOND_ROWS, width)] * 2,
            scratch_shapes=[pltpu.VMEM(shape, HALF) for shape in weights]
            + [pltpu.VMEM((16, width), FLOAT)]
            + [pltpu.VMEM(shape, FLOAT) for shape in weights]
            + [pltpu.VMEM((16, width), FLOAT)],
        ),
        out_shape=[LIKE((rows, width), HALF), LIKE((rows, width), HALF), LIKE((rows, width), FLOAT)]
        + [LIKE((16, SECOND_ROWS, width), HALF)] * 2,
        compiler_params=params(),
        cost_estimate=pl.CostEstimate(
            flops=30 * rows * width * width, bytes_accessed=16 * 1024 * 1024,
            transcendentals=4 * rows * width,
        ),
        name="dense_turn",
    )(place, live, ids, x, *mixed, *slots, cotangent)


def attend_back_kernel(place_ref, x_ref, joint_ref, probs_ref, grad_mixed_ref, weight_ref,
                       grad_one_ref, *refs):
    kept_ref, sent_ref, grad_x_ref, x_turned, grad_scores, grad_joint, small = refs[-7:]
    head = pl.program_id(0)
    rows = x_ref.shape[0]
    head_size = grad_mixed_ref.shape[1]
    place = place_ref[0]

    @pl.when(head == 0)
    def _():
        x_turned[...] = jnp.transpose(x_ref[...])
        grad_x_ref[...] = grad_one_ref[...]
        grad_joint[CTX:, head_size:] = jnp.zeros((rows - CTX, 2 * head_size), HALF)
        clear(small)

    keys = joint_ref[0, :CTX, head_size : 2 * head_size]
    values = joint_ref[0, :CTX, 2 * head_size :]
    keys_turned = jnp.transpose(keys)
    factor = head_size ** (-0.5)
    for start in range(0, rows, SCORE_BLOCK):
        span = slice(start, start + SCORE_BLOCK)
        grad_probs = product(values, grad_mixed_ref[span, :], 1, 1)
        probs = probs_ref[0, :, span].astype(FLOAT)
        weighted = probs * grad_probs
        grad_low = (factor * (weighted - probs * column_sum(weighted))).astype(HALF)
        grad_scores[:, span] = grad_low
        grad_joint[span, :head_size] = jnp.transpose(product(keys_turned, grad_low, 1, 0)).astype(
            HALF
        )
    grad_joint[:CTX, head_size : 2 * head_size] = product(
        grad_scores[...], joint_ref[0, :, :head_size], 1, 0
    ).astype(HALF)
    grad_joint[:CTX, 2 * head_size :] = product(probs_ref[0], grad_mixed_ref[...], 1, 0).astype(HALF)
    sums = column_sum(grad_joint[...].astype(FLOAT))
    small[0:1, :] = sums[:, :head_size]
    small[1:2, :] = sums[:, 2 * head_size :]
    small_low = small[...].astype(HALF)
    grad_weight = product(x_turned[...], grad_joint[...], 1, 0)
    grad_low = grad_weight.astype(HALF)
    grad_x_ref[...] += product(grad_joint[...], weight_ref[0], 1, 1)
    holder = grad_scores
    holder[: grad_low.shape[0], : 3 * head_size] = grad_low
    for at, offset in enumerate(ORDER):
        slots_ref = kept_ref if at < 16 else sent_ref
        at = at % 16
        span = owner_rows(offset, place, 16)
        for piece in range(3):
            slots_ref[at, piece * 16 : (piece + 1) * 16, :] = holder[
                span, piece * head_size : (piece + 1) * head_size
            ]
        slots_ref[at, 48:64, :] = small_low


def attend_back_call(place, base, x, joint, probs, grad_mixed, weight, grad_one, slots=()):
    rows, width = x.shape
    head_size = width // HEADS
    heads = joint.shape[0]
    return pl.pallas_call(
        attend_back_kernel,
        grid_spec=pltpu.PrefetchScalarGridSpec(
            num_scalar_prefetch=1,
            grid=(heads,),
            in_specs=[
                pl.BlockSpec((rows, width), lambda h, p: (0, 0)),
                pl.BlockSpec((1, rows, 3 * head_size), lambda h, p: (h, 0, 0)),
                pl.BlockSpec((1, CTX, rows), lambda h, p: (h, 0, 0)),
                pl.BlockSpec((rows, head_size), lambda h, p: (0, h + base)),
                pl.BlockSpec((1, width, 3 * head_size), lambda h, p: (h, 0, 0)),
                pl.BlockSpec((rows, width), lambda h, p: (0, 0)),
            ]
            + [pl.BlockSpec(memory_space=pl.ANY)] * len(slots),
            out_specs=[pl.BlockSpec((16, FIRST_ROWS, head_size), lambda h, p: (0, 0, h + base))] * 2
            + [pl.BlockSpec((rows, width), lambda h, p: (0, 0))],
            scratch_shapes=[pltpu.VMEM((width, rows), HALF), pltpu.VMEM((CTX, rows), HALF),
                            pltpu.VMEM((rows, 3 * head_size), HALF),
                            pltpu.VMEM((16, head_size), FLOAT)],
        ),
        out_shape=[LIKE((16, FIRST_ROWS, width), HALF)] * 2 + [LIKE((rows, width), FLOAT)],
        input_output_aliases={7 + at: at for at in range(len(slots))},
        compiler_params=params(),
        cost_estimate=pl.CostEstimate(
            flops=heads * (12 * rows * width * head_size + 8 * rows * CTX * head_size),
            bytes_accessed=heads * 5 * 1024 * 1024, transcendentals=0,
        ),
        name="attend_back",
    )(place, x, joint, probs, grad_mixed, weight, grad_one, *slots)


def advance(master, moment, average, grad, momentum, step_rate, decay_now):
    new_moment = momentum * moment + grad
    new_master = master - step_rate * (grad + momentum * new_moment)
    new_average = decay_now * average + (1.0 - decay_now) * new_master
    return (new_moment, new_average, new_master, new_master.astype(HALF))


def stepper(rates_ref, state_refs, out_refs):
    rates = [rates_ref[at] for at in range(3)]

    def step(weight, where, grad):
        state = [ref[where] for ref in state_refs[3 * weight : 3 * weight + 3]]
        for ref, item in zip(out_refs[4 * weight : 4 * weight + 4], advance(*state, grad, *rates)):
            ref[where] = item

    return step


def second_step_kernel(starts, rates_ref, *refs):
    blocks, state_refs, out_refs, (first_ref, small_ref) = refs[:4], refs[4:13], refs[13:25], refs[25:]
    width = small_ref.shape[2]
    step = stepper(rates_ref, state_refs, out_refs)
    total = block_sum(blocks)
    for layer, start in enumerate(starts):
        piece = total[start : start + SECOND_ROWS]
        step(0, (layer,), piece[0:16])
        step(1, (layer, slice(None), slice(0, width)), piece[16:32])
        step(1, (layer, slice(None), slice(width, 2 * width)), piece[32:48])
        step(2, (layer,), piece[48:80])
        small_ref[layer] = piece[80:96]
    first_ref[...] = total[SECOND_ROWS : SECOND_ROWS + FIRST_ROWS]


def step_shapes(masters):
    return [
        LIKE(master.shape, kind) for master in masters for kind in (FLOAT, FLOAT, FLOAT, HALF)
    ]


def step_call(kernel, rates, inputs, out_shape, name):
    return pl.pallas_call(
        kernel,
        in_specs=[pl.BlockSpec(memory_space=pltpu.SMEM)] * len(rates)
        + [pl.BlockSpec(memory_space=pltpu.VMEM)] * len(inputs),
        out_specs=[pl.BlockSpec(memory_space=pltpu.VMEM)] * len(out_shape),
        out_shape=out_shape,
        compiler_params=params(32 * 1024 * 1024),
        cost_estimate=pl.CostEstimate(flops=0, bytes_accessed=1 << 22, transcendentals=0),
        name=name,
    )(*rates, *inputs)


def first_step_kernel(place_ref, rates_ref, small_ref, late_ref, *refs):
    blocks, state_refs, out_refs = refs[:4], refs[4:13], refs[13:]
    width = small_ref.shape[2]
    each = out_refs[4].shape[2]
    step = stepper(rates_ref, state_refs, out_refs)
    turn = width - place_ref[0] * each
    for layer, total in enumerate((block_sum(blocks), late_ref[...])):
        for piece in range(3):
            columns = slice(piece * width, (piece + 1) * width)
            step(0, (layer, slice(None), columns), total[piece * 16 : (piece + 1) * 16])
        own_first = pltpu.roll(total[48:64], turn, 1)[:, :each]
        own_second = pltpu.roll(small_ref[layer], turn, 1)[:, :each]
        step(1, (layer,), own_second[0:2])
        step(2, (layer, slice(0, 2)), own_first[0:2])
        step(2, (layer, slice(2, 8)), own_second[2:8])


def wide_to_rows(shard, width):
    return jnp.concatenate(
        [shard[:, at * width : (at + 1) * width] for at in range(shard.shape[1] // width)]
    )


def rows_to_wide(rows, pieces):
    each = rows.shape[0] // pieces
    return jnp.concatenate([rows[at * each : (at + 1) * each] for at in range(pieces)], axis=1)


def gather_rows(shards_by_part, small):
    width = small.shape[1]
    parts = []
    for shard in shards_by_part:
        whole = lax.all_gather(shard, AXES, axis=0, tiled=False)
        parts.append(whole.reshape(OWNERS, -1, width))
    smalls = jnp.broadcast_to(small[None] * (jnp.arange(OWNERS) == 0)[:, None, None].astype(HALF),
                              (OWNERS, *small.shape))
    slots = jnp.concatenate([*parts, smalls], axis=1)[np.array(ORDER)]
    return [*[slots[4 * at : 4 * at + 4] for at in range(4)], slots[16:]]


def scatter_rows(kept, sent, parts):
    slots = jnp.concatenate([kept, sent])[np.argsort(np.array(ORDER))]
    everyone = lax.axis_size(AXES)
    own, start = [], 0
    for rows in parts:
        piece = slots[:, start : start + rows].reshape(everyone, -1, slots.shape[2])
        own.append(lax.psum_scatter(piece, AXES, scatter_dimension=0, tiled=False).astype(FLOAT))
        start += rows
    return own, lax.psum(slots[0, start:].astype(FLOAT), AXES)


def sync(*items):
    return lax.optimization_barrier(items)


def any_size(place, x, cotangent, dataset_ids, live, masters, moments, averages, rates):
    layers = masters[0].shape[0]
    width = x.shape[1]
    position = lax.axis_index(AXES)
    low = lambda item: item.astype(HALF)
    own = low(jnp.concatenate([masters[4], masters[5]], axis=1))
    wide = lax.all_gather(own, AXES, axis=2, tiled=True)
    onehot = (dataset_ids[0] == jnp.arange(width, dtype=jnp.int32)).astype(FLOAT)
    counts = low(lax.psum(onehot, AXES))[None]
    first, second = [], []
    for at in range(layers):
        pad = lambda rows: jnp.pad(rows, ((0, 16 - rows.shape[0]), (0, 0)))
        attend_w = masters[0][at]
        first.append(gather_rows(
            [low(attend_w[:, piece * width : (piece + 1) * width]) for piece in range(3)],
            pad(wide[at, 2:4]),
        ))
        expand_w = masters[2][at]
        second.append(gather_rows(
            [low(masters[1][at]), low(expand_w[:, :width]), low(expand_w[:, width:]),
             low(masters[3][at])],
            pad(jnp.concatenate([wide[at, 0:2], wide[at, 4:10], counts])),
        ))
    current = x
    saved = []
    for at in range(layers):
        joint, probs, mixed, weight = attend_call(place, current, first[at], 0, HEADS)
        keep = (current, joint, probs, [mixed], weight)
        if at + 1 < layers:
            current, *rest = dense_call(place, current, [mixed], second[at])
            keep = (*keep, rest)
        saved.append(keep)
    first_grads, second_grads = [None] * layers, [None] * layers
    for at in reversed(range(layers)):
        start, joint, probs, mixed, weight = saved[at][:5]
        if at + 1 == layers:
            result, grad_mixed, grad_rows, *slots = dense_turn_call(
                place, live, dataset_ids, start, mixed, second[at], cotangent
            )
        else:
            grad_mixed, grad_rows, *slots = dense_back_call(place, grad_rows, mixed, saved[at][5])
        second_grads[at] = slots
        *slots, grad_rows = attend_back_call(
            place, 0, start, joint, probs, grad_mixed, weight, grad_rows
        )
        first_grads[at] = slots
    grads = [[] for _ in range(6)]
    for at in range(layers):
        kept, sent = first_grads[at]
        own, first_small = scatter_rows(kept, sent, (16, 16, 16))
        grads[0].append(jnp.concatenate(own, axis=1))
        own, small = scatter_rows(*second_grads[at], (16, 16, 16, 32))
        grads[1].append(own[0])
        grads[2].append(jnp.concatenate(own[1:3], axis=1))
        grads[3].append(own[3])
        rows = jnp.concatenate([small[0:2], first_small[0:2], small[2:8]])
        lanes = masters[4].shape[2]
        own_rows = lax.dynamic_slice(rows, (0, position * lanes), (10, lanes))
        grads[4].append(own_rows[:2])
        grads[5].append(own_rows[2:])
    outputs = []
    for master, moment, average, grad in zip(masters, moments, averages, grads):
        outputs.extend(
            advance(master, moment, average, jnp.stack(grad), rates[0], rates[1], rates[2])
        )
    return (result, grad_rows, *outputs)


def one_per_owner(place, x, cotangent, dataset_ids, live, masters, moments, averages, rates):
    width = x.shape[1]
    pair = HEADS // 2

    def stack(block, got, *cuts):
        return join_call([block, *got], cuts or ((0, block.shape[0]),))

    def to_core(stacks):
        (all_stacks,) = join_call(stacks, ((0, stacks[0].shape[1]),))
        return swap(all_stacks, CORE)

    def square(block):
        return swaps(block, SQUARE[1:])

    near_first, near_second, late = pack_call(place, dataset_ids, masters)
    got = swaps(near_first, CHAIN[1:])
    (first_own,) = stack(near_first, got)

    first_own, near_second = sync(first_own, near_second)
    got = square(first_own)
    chain_second = swaps(near_second, CHAIN[1:3])
    first_near = [first_own, *got]

    first_near, chain_second, near_second, late = sync(first_near, chain_second, near_second, late)
    first_far = to_core(first_near)
    chain_second.append(swap(near_second, CHAIN[3]))
    chain_late = swaps(late, CHAIN[1:3])
    (second_own,) = stack(near_second, chain_second)

    first_far, second_own, x = sync(first_far, second_own, x)
    first_slots = [*first_near, first_far]
    second_got = square(second_own)
    low_call = attend_call(place, x, first_slots, 0, pair)

    low_call, chain_late, late, x = sync(low_call, chain_late, late, x)
    chain_late.append(swap(late, CHAIN[3]))
    high_call = attend_call(place, x, first_slots, pair, pair)

    high_call, chain_late, second_got = sync(high_call, chain_late, second_got)
    second_near = [second_own, *second_got]
    second_far = to_core(second_near)
    late_first, late_second = stack(
        late, chain_late, (0, FIRST_ROWS), (FIRST_ROWS, SECOND_ROWS)
    )
    late_got = square(late_first)

    second_far, late_first, high_call = sync(second_far, late_first, high_call)
    mixed = [low_call[2], high_call[2]]
    middle, *dense_kept = dense_call(place, x, mixed, [*second_near, second_far])

    middle, late_got, late_second = sync(middle, late_got, late_second)
    late_near = [late_first, *late_got]
    late_far = to_core(late_near)
    second_got = square(late_second)

    late_far, middle, late_second = sync(late_far, middle, late_second)
    first_slots = [*late_near, late_far]
    late_low = attend_call(place, middle, first_slots, 0, pair)

    late_low, second_got, middle = sync(late_low, second_got, middle)
    second_near = [late_second, *second_got]
    second_far = to_core(second_near)
    late_high = attend_call(place, middle, first_slots, pair, pair)

    second_far, late_high, middle = sync(second_far, late_high, middle)
    result, grad_mixed, grad_rows, kept, sent = dense_turn_call(
        place, live, dataset_ids, middle, [late_low[2], late_high[2]], [*second_near, second_far],
        cotangent,
    )

    def back(base, start, call, grad_mixed, grad_rows, slots=()):
        joint, probs, _, weight = call
        *slots, grad_rows = attend_back_call(
            place, base, start, joint, probs, grad_mixed, weight, grad_rows, slots
        )
        return slots, grad_rows

    def square_back(stacks):
        return [swap(one, offset) for one, offset in zip(stacks[1:], SQUARE[1:])]

    def chain_back(blocks):
        return [swap(one, offset) for one, offset in zip(blocks[1:], CHAIN[1:])]

    sent, grad_rows, grad_mixed = sync(sent, grad_rows, grad_mixed)
    got = swap(sent, CORE)
    slots, grad_rows = back(0, middle, late_low, grad_mixed, grad_rows)

    got, slots, grad_rows, grad_mixed = sync(got, slots, grad_rows, grad_mixed)
    late_stacks = core_sum_call(kept, got)
    late_stacks, grad_rows, slots = sync(late_stacks, grad_rows, slots)
    late_got = square_back(late_stacks)
    (kept, sent), grad_rows = back(pair, middle, late_high, grad_mixed, grad_rows, slots)

    sent, grad_rows = sync(sent, grad_rows)
    got = swap(sent, CORE)
    grad_mixed, grad_rows, next_kept, next_sent = dense_back_call(
        place, grad_rows, mixed, dense_kept
    )

    got, late_got, next_sent, grad_mixed, grad_rows = sync(
        got, late_got, next_sent, grad_mixed, grad_rows
    )
    first_stacks = core_sum_call(kept, got)
    first_stacks, next_sent, grad_mixed, grad_rows = sync(
        first_stacks, next_sent, grad_mixed, grad_rows
    )
    got = swap(next_sent, CORE)
    first_got = square_back(first_stacks)
    slots, grad_rows = back(0, x, low_call, grad_mixed, grad_rows)

    got, first_got, slots, grad_rows, grad_mixed = sync(got, first_got, slots, grad_rows, grad_mixed)
    second_stacks = core_sum_call(next_kept, got)
    second_stacks, slots, grad_rows, grad_mixed = sync(second_stacks, slots, grad_rows, grad_mixed)
    second_got = square_back(second_stacks)
    (kept, sent), grad_rows = back(pair, x, high_call, grad_mixed, grad_rows, slots)

    second_got, sent, grad_rows = sync(second_got, sent, grad_rows)
    got = swap(sent, CORE)
    blocks = square_sum_call(
        [late_stacks[0], *late_got], [first_stacks[0], *first_got], [second_stacks[0], *second_got]
    )

    got, blocks = sync(got, blocks)
    stacks = core_sum_call(kept, got)
    got = square_back(stacks)
    chain_got = chain_back(blocks)

    def state_of(*which):
        return [item for at in which for item in (masters[at], moments[at], averages[at])]

    *stepped, late_first, small = step_call(
        functools.partial(second_step_kernel, (SECOND_ROWS + FIRST_ROWS, 0)),
        [rates],
        [blocks[0], *chain_got, *state_of(1, 2, 3)],
        [*step_shapes(masters[1:4]), LIKE((FIRST_ROWS, width), FLOAT),
         LIKE((2, 16, width), FLOAT)],
        "second_step",
    )
    blocks = square_sum_call([stacks[0], *got])
    chain_got = chain_back(blocks)
    rest = step_call(
        first_step_kernel,
        [place, rates],
        [small, late_first, blocks[0], *chain_got, *state_of(0, 4, 5)],
        step_shapes((masters[0], masters[4], masters[5])),
        "first_step",
    )
    return (result, grad_rows, *rest[:4], *stepped, *rest[4:])


def shards(
    tokens,
    cotangent,
    dataset_ids,
    query_counts,
    learn_rate,
    momentum_coef,
    average_decay,
    step_count,
    *state,
):
    masters, moments, averages = state[0::3], state[1::3], state[2::3]
    position = lax.axis_index(AXES)
    direct = lax.axis_size(AXES) == OWNERS
    place = (position if direct else jnp.zeros_like(position)).astype(jnp.int32).reshape(1)
    step_value = step_count[0].astype(FLOAT)
    decay_now = average_decay[0] * (1.0 + step_value) / (4.0 + step_value)
    rates = jnp.stack([momentum_coef[0], learn_rate[0], decay_now])
    run = one_per_owner if direct else any_size
    result, grad_rows, *outputs = run(
        place, tokens[0], cotangent[0], dataset_ids, query_counts + CTX, masters, moments, averages,
        rates,
    )
    return (result[None], grad_rows[None], *outputs)


def solution(mesh):
    rows = P(AXES, None, None)
    weight = P(None, AXES, None)
    vector = P(None, None, AXES)
    scalar = P()
    return jax.shard_map(
        shards,
        mesh=mesh,
        in_specs=(rows, rows, P(AXES), P(AXES), *[scalar] * 4, *[weight] * 12, *[vector] * 6),
        out_specs=(rows, rows, *[weight] * 16, *[vector] * 8),
        check_vma=False,
    )
```

```python
import functools

import jax
import jax.numpy as jnp
import numpy as np
from jax import lax
from jax.experimental import pallas as pl
from jax.experimental.pallas import tpu as pltpu
from jax.sharding import PartitionSpec as P

HEADS = 4
CTX = 896
NDS = 8
EPS = 1e-05
OWNERS = 32
AXES = ("dp", "fsdp")

CHAIN = (0, 4, 2, 6)
SQUARE = (0, 1, 16, 17)
CORE = 8
ORDER = tuple(core ^ side ^ link for core in (0, CORE) for side in SQUARE for link in CHAIN)

FIRST_ROWS = 64
SECOND_ROWS = 96

SCORE_BLOCK = 256
ROW_BLOCK = 256
ROOT_HALF = 0.7071067811865476
PDF_PEAK = 0.3989422804014327
VMEM_LIMIT = 60 * 1024 * 1024
SMALL_LIMIT = 12 * 1024 * 1024
FLOAT = jnp.float32
HALF = jnp.bfloat16
LIKE = jax.ShapeDtypeStruct


def product(left, right, left_dim, right_dim):
    return lax.dot_general(
        left, right, (((left_dim,), (right_dim,)), ((), ())), preferred_element_type=FLOAT
    )


def owner_rows(offset, place, rows):
    return pl.ds(pl.multiple_of((offset ^ place) * rows, rows), rows)


def params(limit=VMEM_LIMIT):
    return pltpu.CompilerParams(vmem_limit_bytes=limit)


def pack_kernel(place_ref, ids_ref, attend_ref, output_ref, expand_ref, shrink_ref, gains_ref,
                bias_ref, near_ref, next_ref, late_ref, small):
    width = near_ref.shape[1]
    each = gains_ref.shape[2]
    lane = lax.broadcasted_iota(jnp.int32, (each, width), 1)
    own = lax.broadcasted_iota(jnp.int32, (each, width), 0) + place_ref[0] * each
    pick = (lane == own).astype(HALF)
    lanes = lax.broadcasted_iota(jnp.int32, (1, width), 1)

    for layer in range(attend_ref.shape[0]):
        first, second, top = (
            (near_ref, next_ref, 0) if layer == 0 else (late_ref, late_ref, FIRST_ROWS)
        )
        gains = product(gains_ref[layer].astype(HALF), pick, 1, 0)
        biases = product(bias_ref[layer].astype(HALF), pick, 1, 0)
        for piece in range(3):
            first[piece * 16 : (piece + 1) * 16, :] = attend_ref[
                layer, :, piece * width : (piece + 1) * width
            ].astype(HALF)
        small[...] = jnp.zeros_like(small)
        small[0:2, :] = biases[0:2, :]
        first[48:64, :] = small[...].astype(HALF)
        second[top : top + 16, :] = output_ref[layer].astype(HALF)
        for piece in range(2):
            second[top + (piece + 1) * 16 : top + (piece + 2) * 16, :] = expand_ref[
                layer, :, piece * width : (piece + 1) * width
            ].astype(HALF)
        second[top + 48 : top + 80, :] = shrink_ref[layer].astype(HALF)
        small[0:2, :] = gains
        small[2:8, :] = biases[2:8, :]
        small[8:9, :] = (lanes == ids_ref[0]).astype(FLOAT)
        second[top + 80 : top + 96, :] = small[...].astype(HALF)


def pack_call(place, ids, masters):
    width = masters[1].shape[2]
    rows = (FIRST_ROWS, SECOND_ROWS, FIRST_ROWS + SECOND_ROWS)
    return pl.pallas_call(
        pack_kernel,
        in_specs=[pl.BlockSpec(memory_space=pltpu.SMEM)] * 2
        + [pl.BlockSpec(memory_space=pltpu.VMEM)] * 6,
        out_specs=[pl.BlockSpec(memory_space=pltpu.VMEM)] * 3,
        out_shape=[LIKE((count, width), HALF) for count in rows],
        scratch_shapes=[pltpu.VMEM((16, width), FLOAT)],
        compiler_params=params(),
        cost_estimate=pl.CostEstimate(flops=0, bytes_accessed=1 << 20, transcendentals=0),
        name="pack",
    )(place, ids, *masters)


def join_kernel(cuts, count, *refs):
    each = refs[count].shape[0] // count
    for at in range(count):
        for to, (start, rows) in enumerate(cuts):
            target = refs[count + to]
            if len(refs[at].shape) == 2:
                target[at] = refs[at][start : start + rows, :]
            else:
                target[at * each : (at + 1) * each] = refs[at][:, start : start + rows, :]


def join_call(blocks, *cuts):
    *head, rows, width = blocks[0].shape
    slots = len(blocks) * (head[0] if head else 1)
    cuts = cuts or ((0, rows),)
    return pl.pallas_call(
        functools.partial(join_kernel, cuts, len(blocks)),
        out_shape=[LIKE((slots, rows, width), HALF) for _, rows in cuts],
        compiler_params=params(SMALL_LIMIT),
        cost_estimate=pl.CostEstimate(flops=0, bytes_accessed=1 << 20, transcendentals=0),
        name="join",
    )(*blocks)


def block_sum(refs):
    total = refs[0][...].astype(FLOAT)
    for ref in refs[1:]:
        total = total + ref[...].astype(FLOAT)
    return total


def core_sum(kept, got):
    return [
        (kept[at : at + 4].astype(FLOAT) + got[at : at + 4].astype(FLOAT)).astype(HALF)
        for at in range(0, 16, 4)
    ]


def square_sum_kernel(rows, *refs):
    outs = refs[4 * len(rows) :]
    start = 0
    for at, count in enumerate(rows):
        total = block_sum(refs[4 * at : 4 * at + 4]).astype(HALF)
        for to in range(4):
            each = 4 // len(outs)
            if each == 1:
                outs[to][start : start + count, :] = total[to]
            else:
                outs[to // each][to % each, start : start + count, :] = total[to]
        start += count


def square_sum_call(*pieces, halves=True):
    rows = tuple(stacks[0].shape[1] for stacks in pieces)
    shape = (sum(rows), pieces[0][0].shape[2])
    return pl.pallas_call(
        functools.partial(square_sum_kernel, rows),
        out_shape=[LIKE((2, *shape), HALF)] * 2 if halves else [LIKE(shape, HALF)] * 4,
        compiler_params=params(SMALL_LIMIT),
        cost_estimate=pl.CostEstimate(flops=0, bytes_accessed=1 << 21, transcendentals=0),
        name="square_sum",
    )(*[stack for stacks in pieces for stack in stacks])


def pair_sum(kept, got):
    return [(kept[at].astype(FLOAT) + got[at].astype(FLOAT)).astype(HALF) for at in range(2)]


def swap(block, offset):
    return lax.ppermute(block, AXES, [(one, one ^ offset) for one in range(OWNERS)])


def swaps(block, offsets):
    return [swap(block, offset) for offset in offsets]


def slot_places(slot_refs):
    for at, offset in enumerate(ORDER):
        yield slot_refs[at // 4], at % 4, offset


def small_rows(slot_refs, start):
    total = None
    for slots in slot_refs:
        for at in range(slots.shape[0]):
            block = slots[at, start : start + 16, :].astype(FLOAT)
            total = block if total is None else total + block
    return total


def attend_kernel(place_ref, x_ref, *refs):
    slot_refs = refs[:8]
    joint_ref, probs_ref, mixed_ref, weight_ref = refs[8:]
    head_size = mixed_ref.shape[1]
    place = place_ref[0]

    for slots, at, offset in slot_places(slot_refs):
        rows = owner_rows(offset, place, 16)
        for piece in range(3):
            weight_ref[0, rows, piece * head_size : (piece + 1) * head_size] = slots[
                at, piece * 16 : (piece + 1) * 16, :
            ]
    zeros = jnp.zeros((1, head_size), FLOAT)
    small = small_rows(slot_refs, 48)
    shift = jnp.concatenate([small[0:1, :], zeros, small[1:2, :]], axis=1)
    joint_ref[0] = (product(x_ref[...], weight_ref[0], 1, 0) + shift).astype(HALF)
    keys = joint_ref[0, :CTX, head_size : 2 * head_size]
    values = joint_ref[0, :CTX, 2 * head_size :]
    values_turned = jnp.transpose(values)
    factor = head_size ** (-0.5) * 1.4426950408889634
    for start in range(0, x_ref.shape[0], SCORE_BLOCK):
        span = slice(start, start + SCORE_BLOCK)
        queries = joint_ref[0, span, :head_size]
        scores = product(keys, queries, 1, 1)
        top = jnp.max(scores, axis=0, keepdims=True)
        grown = jnp.exp2((scores - top) * factor)
        total = jnp.sum(grown, axis=0, keepdims=True)
        probs = (grown * (1.0 / total)).astype(HALF)
        probs_ref[0, :, span] = probs
        mixed_ref[span, :] = jnp.transpose(product(values_turned, probs, 1, 0)).astype(HALF)


def attend_call(place, x, slots):
    rows, width = x.shape
    head_size = width // HEADS
    return pl.pallas_call(
        attend_kernel,
        grid_spec=pltpu.PrefetchScalarGridSpec(
            num_scalar_prefetch=1,
            grid=(HEADS,),
            in_specs=[pl.BlockSpec((rows, width), lambda h, p: (0, 0))]
            + [pl.BlockSpec((part.shape[0], FIRST_ROWS, head_size), lambda h, p: (0, 0, h))
               for part in slots],
            out_specs=[
                pl.BlockSpec((1, rows, 3 * head_size), lambda h, p: (h, 0, 0)),
                pl.BlockSpec((1, CTX, rows), lambda h, p: (h, 0, 0)),
                pl.BlockSpec((rows, head_size), lambda h, p: (0, h)),
                pl.BlockSpec((1, width, 3 * head_size), lambda h, p: (h, 0, 0)),
            ],
        ),
        out_shape=[
            LIKE((HEADS, rows, 3 * head_size), HALF),
            LIKE((HEADS, CTX, rows), HALF),
            LIKE((rows, HEADS * head_size), HALF),
            LIKE((HEADS, width, 3 * head_size), HALF),
        ],
        compiler_params=params(),
        cost_estimate=pl.CostEstimate(
            flops=HEADS * (2 * rows * width * 3 * head_size + 4 * rows * CTX * head_size),
            bytes_accessed=HEADS * 4 * 1024 * 1024,
            transcendentals=HEADS * rows * CTX,
        ),
        name="attend",
    )(place, x, *slots)


def unpack_second(place, slot_refs, output_w, expand_w, shrink_w, vec_ref):
    width = output_w.shape[1]
    for slots, at, offset in slot_places(slot_refs):
        rows = owner_rows(offset, place, 16)
        output_w[rows, :] = slots[at, 0:16, :]
        expand_w[rows, :width] = slots[at, 16:32, :]
        expand_w[rows, width:] = slots[at, 32:48, :]
        shrink_w[owner_rows(offset, place, 32), :] = slots[at, 48:80, :]
    vec_ref[...] = small_rows(slot_refs, 80)


def row_mean(rows):
    return jnp.mean(rows, axis=-1, keepdims=True)


def normalize(rows):
    centred = rows - row_mean(rows)
    inv_std = lax.rsqrt(row_mean(centred * centred) + EPS)
    return (centred * inv_std, inv_std)


def forward_rows(x_ref, mixed_ref, vec_ref, output_w, expand_w, shrink_w):
    attn_out = product(mixed_ref[...], output_w[...], 1, 0) + vec_ref[2:3, :]
    unit_one, inv_one = normalize(x_ref[...].astype(FLOAT) + attn_out)
    first_norm = unit_one * vec_ref[0:1, :] + vec_ref[4:5, :]
    first_low = first_norm.astype(HALF)
    shift = jnp.concatenate([vec_ref[6:7, :], vec_ref[7:8, :]], axis=1)
    hidden = product(first_low, expand_w[...], 1, 0) + shift
    normal_cdf = 0.5 * (1.0 + lax.erf(hidden * ROOT_HALF))
    act_low = (hidden * normal_cdf).astype(HALF)
    slope = normal_cdf + hidden * (jnp.exp(-0.5 * hidden * hidden) * PDF_PEAK)
    branch = product(act_low, shrink_w[...], 1, 0) + vec_ref[3:4, :]
    unit_two, inv_two = normalize(first_norm + branch)
    result = unit_two * vec_ref[1:2, :] + vec_ref[5:6, :]
    return (unit_one, inv_one, first_low, act_low, slope, unit_two, inv_two, result)


def column_sum(rows):
    return jnp.sum(rows, axis=0, keepdims=True)


def backward_rows(grad_rows, mixed_ref, vec_ref, kept, output_w, expand_w, shrink_w,
                  grad_mixed_ref, grad_one_ref, grad_output, grad_expand, grad_shrink, sums):
    unit_one, inv_one, first_low, act_low, slope, unit_two, inv_two = kept
    width = grad_rows.shape[1]

    def layer_norm_back(rows, unit_rows, inv_std, gain):
        scaled = rows * gain
        return inv_std * (scaled - row_mean(scaled) - unit_rows * row_mean(scaled * unit_rows))

    grad_two = layer_norm_back(grad_rows, unit_two, inv_two, vec_ref[1:2, :])
    branch_low = grad_two.astype(HALF)
    grad_shrink[...] += product(act_low, branch_low, 0, 0)
    grad_hidden = (product(branch_low, shrink_w[...], 1, 1) * slope).astype(HALF)
    grad_expand[...] += product(first_low, grad_hidden, 0, 0)
    grad_first = grad_two + product(grad_hidden, expand_w[...], 1, 1)
    grad_one = layer_norm_back(grad_first, unit_one, inv_one, vec_ref[0:1, :])
    attn_low = grad_one.astype(HALF)
    grad_output[...] += product(mixed_ref[...], attn_low, 0, 0)
    grad_mixed_ref[...] = product(attn_low, output_w[...], 1, 1).astype(HALF)
    grad_one_ref[...] = grad_one
    sums[0:1, :] += column_sum(grad_first * unit_one)
    sums[1:2, :] += column_sum(grad_rows * unit_two)
    sums[2:3, :] += column_sum(attn_low.astype(FLOAT))
    sums[3:4, :] += column_sum(branch_low.astype(FLOAT))
    sums[4:5, :] += column_sum(grad_first)
    sums[5:6, :] += column_sum(grad_rows)
    hidden_sum = column_sum(grad_hidden.astype(FLOAT))
    sums[6:7, :] += hidden_sum[:, :width]
    sums[7:8, :] += hidden_sum[:, width:]


def pack_second(place, kept_ref, sent_ref, grad_output, grad_expand, grad_shrink, sums):
    width = grad_output.shape[1]
    small = sums[...].astype(HALF)
    for at, offset in enumerate(ORDER):
        slots_ref = kept_ref if at < 16 else sent_ref
        at = at % 16
        rows = owner_rows(offset, place, 16)
        slots_ref[at, 0:16, :] = grad_output[rows, :].astype(HALF)
        slots_ref[at, 16:32, :] = grad_expand[rows, :width].astype(HALF)
        slots_ref[at, 32:48, :] = grad_expand[rows, width:].astype(HALF)
        slots_ref[at, 48:80, :] = grad_shrink[owner_rows(offset, place, 32), :].astype(HALF)
        slots_ref[at, 80:96, :] = small


def dense_kernel(place_ref, x_ref, mixed_ref, *refs):
    slot_refs = refs[:8]
    (result_ref, unit_one_ref, inv_one_ref, act_ref, slope_ref, unit_two_ref, inv_two_ref, output_w,
     expand_w, shrink_w, vec_ref) = refs[8:]

    @pl.when(pl.program_id(0) == 0)
    def _():
        unpack_second(place_ref[0], slot_refs, output_w, expand_w, shrink_w, vec_ref)

    unit_one, inv_one, _, act_low, slope, unit_two, inv_two, result = forward_rows(
        x_ref, mixed_ref, vec_ref, output_w, expand_w, shrink_w
    )
    result_ref[...] = result.astype(HALF)
    unit_one_ref[...] = unit_one
    inv_one_ref[...] = inv_one
    act_ref[...] = act_low
    slope_ref[...] = slope
    unit_two_ref[...] = unit_two
    inv_two_ref[...] = inv_two


def grad_x_rows(grad_one_ref, grad_joint_ref, weight_ref):
    total = grad_one_ref[...]
    for head in range(weight_ref.shape[0]):
        total = total + product(grad_joint_ref[head], weight_ref[head], 1, 1)
    return total


def clear(*items):
    for item in items:
        item[...] = jnp.zeros_like(item)


def dense_back_kernel(place_ref, grad_one_next, grad_joint_next, weight_next, mixed_ref, *refs):
    (unit_one_ref, inv_one_ref, act_ref, slope_ref, unit_two_ref, inv_two_ref, output_w, expand_w,
     shrink_w, vec_ref, grad_mixed_ref, grad_one_ref, kept_ref, sent_ref, sums, grad_output,
     grad_expand, grad_shrink) = refs

    @pl.when(pl.program_id(0) == 0)
    def _():
        clear(sums, grad_output, grad_expand, grad_shrink)

    unit_one = unit_one_ref[...]
    first_low = (unit_one * vec_ref[0:1, :] + vec_ref[4:5, :]).astype(HALF)
    kept = (unit_one, inv_one_ref[...], first_low, act_ref[...], slope_ref[...], unit_two_ref[...],
            inv_two_ref[...])
    grad_rows = grad_x_rows(grad_one_next, grad_joint_next, weight_next)
    backward_rows(grad_rows, mixed_ref, vec_ref, kept, output_w, expand_w, shrink_w,
                  grad_mixed_ref, grad_one_ref, grad_output, grad_expand, grad_shrink, sums)

    @pl.when(pl.program_id(0) == pl.num_programs(0) - 1)
    def _():
        pack_second(place_ref[0], kept_ref, sent_ref, grad_output, grad_expand, grad_shrink, sums)


def dense_turn_kernel(place_ref, live_ref, ids_ref, x_ref, mixed_ref, *refs):
    slot_refs = refs[:8]
    (cot_ref, result_ref, grad_mixed_ref, grad_one_ref, kept_ref, sent_ref, output_w, expand_w,
     shrink_w, vec_ref, grad_output, grad_expand, grad_shrink, sums) = refs[8:]
    step = pl.program_id(0)

    @pl.when(step == 0)
    def _():
        unpack_second(place_ref[0], slot_refs, output_w, expand_w, shrink_w, vec_ref)
        clear(sums, grad_output, grad_expand, grad_shrink)

    *kept, result = forward_rows(x_ref, mixed_ref, vec_ref, output_w, expand_w, shrink_w)
    result_ref[...] = result.astype(HALF)
    counts = vec_ref[8:9, :]
    lanes = lax.broadcasted_iota(jnp.int32, counts.shape, 1)
    own_count = jnp.sum(jnp.where(lanes == ids_ref[0], counts, 0.0), axis=1, keepdims=True)
    row_weight = jnp.sum(counts, axis=1, keepdims=True) / (NDS * own_count)
    rows = cot_ref.shape[0]
    slot = lax.broadcasted_iota(jnp.int32, (rows, 1), 0) + step * rows
    grad_rows = cot_ref[...].astype(FLOAT) * jnp.where(slot < live_ref[0], row_weight, 0.0)
    backward_rows(grad_rows, mixed_ref, vec_ref, kept, output_w, expand_w, shrink_w,
                  grad_mixed_ref, grad_one_ref, grad_output, grad_expand, grad_shrink, sums)

    @pl.when(step == pl.num_programs(0) - 1)
    def _():
        pack_second(place_ref[0], kept_ref, sent_ref, grad_output, grad_expand, grad_shrink, sums)


def by_rows(width):
    return pl.BlockSpec((ROW_BLOCK, width), lambda i, *p: (i, 0))


def fixed(*shape):
    return pl.BlockSpec(shape, lambda i, *p: (0,) * len(shape))


def joint_rows(grad_joint):
    heads, _, width = grad_joint.shape
    return pl.BlockSpec((heads, ROW_BLOCK, width), lambda i, *p: (0, i, 0))


def weight_shapes(width):
    return [(width, width), (width, 2 * width), (2 * width, width)]


def dense_call(place, x, mixed, slots):
    rows, width = x.shape
    weights = weight_shapes(width)
    return pl.pallas_call(
        dense_kernel,
        grid_spec=pltpu.PrefetchScalarGridSpec(
            num_scalar_prefetch=1,
            grid=(rows // ROW_BLOCK,),
            in_specs=[by_rows(width)] * 2
            + [fixed(*part.shape) for part in slots],
            out_specs=[by_rows(width), by_rows(width), by_rows(1), by_rows(2 * width),
                       by_rows(2 * width), by_rows(width), by_rows(1)]
            + [fixed(*shape) for shape in weights]
            + [fixed(16, width)],
        ),
        out_shape=[LIKE((rows, width), HALF), LIKE((rows, width), FLOAT), LIKE((rows, 1), FLOAT),
                   LIKE((rows, 2 * width), HALF), LIKE((rows, 2 * width), FLOAT),
                   LIKE((rows, width), FLOAT), LIKE((rows, 1), FLOAT)]
        + [LIKE(shape, HALF) for shape in weights]
        + [LIKE((16, width), FLOAT)],
        compiler_params=params(),
        cost_estimate=pl.CostEstimate(
            flops=10 * rows * width * width, bytes_accessed=16 * 1024 * 1024,
            transcendentals=4 * rows * width,
        ),
        name="dense",
    )(place, x, mixed, *slots)


def dense_back_call(place, grad_one, grad_joint, weight, mixed, kept):
    rows, width = grad_one.shape
    weights = weight_shapes(width)
    return pl.pallas_call(
        dense_back_kernel,
        grid_spec=pltpu.PrefetchScalarGridSpec(
            num_scalar_prefetch=1,
            grid=(rows // ROW_BLOCK,),
            in_specs=[by_rows(width), joint_rows(grad_joint), fixed(*weight.shape), by_rows(width)]
            + [by_rows(width), by_rows(1), by_rows(2 * width), by_rows(2 * width), by_rows(width),
               by_rows(1)]
            + [fixed(*shape) for shape in weights]
            + [fixed(16, width)],
            out_specs=[by_rows(width), by_rows(width)] + [fixed(16, SECOND_ROWS, width)] * 2,
            scratch_shapes=[pltpu.VMEM((16, width), FLOAT)]
            + [pltpu.VMEM(shape, FLOAT) for shape in weights],
        ),
        out_shape=[LIKE((rows, width), HALF), LIKE((rows, width), FLOAT)]
        + [LIKE((16, SECOND_ROWS, width), HALF)] * 2,
        compiler_params=params(),
        cost_estimate=pl.CostEstimate(
            flops=26 * rows * width * width, bytes_accessed=20 * 1024 * 1024, transcendentals=0
        ),
        name="dense_back",
    )(place, grad_one, grad_joint, weight, mixed, *kept)


def dense_turn_call(place, live, ids, x, mixed, slots, cotangent):
    rows, width = x.shape
    weights = weight_shapes(width)
    return pl.pallas_call(
        dense_turn_kernel,
        grid_spec=pltpu.PrefetchScalarGridSpec(
            num_scalar_prefetch=3,
            grid=(rows // ROW_BLOCK,),
            in_specs=[by_rows(width)] * 2
            + [fixed(*part.shape) for part in slots]
            + [by_rows(width)],
            out_specs=[by_rows(width)] * 3 + [fixed(16, SECOND_ROWS, width)] * 2,
            scratch_shapes=[pltpu.VMEM(shape, HALF) for shape in weights]
            + [pltpu.VMEM((16, width), FLOAT)]
            + [pltpu.VMEM(shape, FLOAT) for shape in weights]
            + [pltpu.VMEM((16, width), FLOAT)],
        ),
        out_shape=[LIKE((rows, width), HALF), LIKE((rows, width), HALF), LIKE((rows, width), FLOAT)]
        + [LIKE((16, SECOND_ROWS, width), HALF)] * 2,
        compiler_params=params(),
        cost_estimate=pl.CostEstimate(
            flops=30 * rows * width * width, bytes_accessed=16 * 1024 * 1024,
            transcendentals=4 * rows * width,
        ),
        name="dense_turn",
    )(place, live, ids, x, mixed, *slots, cotangent)


def attend_back_kernel(place_ref, x_ref, joint_ref, probs_ref, grad_mixed_ref, *refs):
    kept_ref, sent_ref, grad_joint_ref, x_turned, grad_scores, small = refs[-6:]
    grad_joint = grad_joint_ref.at[0]
    rows = x_ref.shape[0]
    head_size = grad_mixed_ref.shape[1]
    place = place_ref[0]

    @pl.when(pl.program_id(0) == 0)
    def _():
        x_turned[...] = jnp.transpose(x_ref[...])
        clear(small)

    grad_joint[CTX:, head_size:] = jnp.zeros((rows - CTX, 2 * head_size), HALF)
    keys = joint_ref[0, :CTX, head_size : 2 * head_size]
    values = joint_ref[0, :CTX, 2 * head_size :]
    keys_turned = jnp.transpose(keys)
    factor = head_size ** (-0.5)
    for start in range(0, rows, SCORE_BLOCK):
        span = slice(start, start + SCORE_BLOCK)
        grad_probs = product(values, grad_mixed_ref[span, :], 1, 1)
        probs = probs_ref[0, :, span].astype(FLOAT)
        weighted = probs * grad_probs
        grad_low = (factor * (weighted - probs * column_sum(weighted))).astype(HALF)
        grad_scores[:, span] = grad_low
        grad_joint[span, :head_size] = jnp.transpose(product(keys_turned, grad_low, 1, 0)).astype(
            HALF
        )
    grad_joint[:CTX, head_size : 2 * head_size] = product(
        grad_scores[...], joint_ref[0, :, :head_size], 1, 0
    ).astype(HALF)
    grad_joint[:CTX, 2 * head_size :] = product(probs_ref[0], grad_mixed_ref[...], 1, 0).astype(HALF)
    sums = column_sum(grad_joint[...].astype(FLOAT))
    small[0:1, :] = sums[:, :head_size]
    small[1:2, :] = sums[:, 2 * head_size :]
    small_low = small[...].astype(HALF)
    grad_low = product(x_turned[...], grad_joint[...], 1, 0).astype(HALF)
    holder = grad_scores
    holder[: grad_low.shape[0], : 3 * head_size] = grad_low
    for at, offset in enumerate(ORDER):
        slots_ref = kept_ref if at < 16 else sent_ref
        at = at % 16
        span = owner_rows(offset, place, 16)
        for piece in range(3):
            slots_ref[at, piece * 16 : (piece + 1) * 16, :] = holder[
                span, piece * head_size : (piece + 1) * head_size
            ]
        slots_ref[at, 48:64, :] = small_low


def attend_back_call(place, x, joint, probs, grad_mixed, base=0, heads=HEADS, before=()):
    rows, width = x.shape
    head_size = width // HEADS
    return pl.pallas_call(
        attend_back_kernel,
        grid_spec=pltpu.PrefetchScalarGridSpec(
            num_scalar_prefetch=1,
            grid=(heads,),
            in_specs=[
                pl.BlockSpec((rows, width), lambda h, p: (0, 0)),
                pl.BlockSpec((1, rows, 3 * head_size), lambda h, p: (h + base, 0, 0)),
                pl.BlockSpec((1, CTX, rows), lambda h, p: (h + base, 0, 0)),
                pl.BlockSpec((rows, head_size), lambda h, p: (0, h + base)),
            ]
            + [pl.BlockSpec(memory_space=pl.ANY)] * len(before),
            out_specs=[pl.BlockSpec((16, FIRST_ROWS, head_size), lambda h, p: (0, 0, h + base))] * 2
            + [pl.BlockSpec((1, rows, 3 * head_size), lambda h, p: (h + base, 0, 0))],
            scratch_shapes=[pltpu.VMEM((width, rows), HALF), pltpu.VMEM((CTX, rows), HALF),
                            pltpu.VMEM((16, head_size), FLOAT)],
        ),
        out_shape=[LIKE((16, FIRST_ROWS, width), HALF)] * 2
        + [LIKE((HEADS, rows, 3 * head_size), HALF)],
        input_output_aliases={5 + at: at for at in range(len(before))},
        compiler_params=params(),
        cost_estimate=pl.CostEstimate(
            flops=heads * (6 * rows * width * head_size + 8 * rows * CTX * head_size),
            bytes_accessed=heads * 4 * 1024 * 1024, transcendentals=0,
        ),
        name="attend_back",
    )(place, x, joint, probs, grad_mixed, *before)


def grad_x_kernel(grad_one_ref, grad_joint_ref, weight_ref, grad_x_ref):
    grad_x_ref[...] = grad_x_rows(grad_one_ref, grad_joint_ref, weight_ref)


def grad_x_call(grad_one, grad_joint, weight):
    rows, width = grad_one.shape
    return pl.pallas_call(
        grad_x_kernel,
        grid=(rows // ROW_BLOCK,),
        in_specs=[
            by_rows(width),
            joint_rows(grad_joint),
            fixed(*weight.shape),
        ],
        out_specs=by_rows(width),
        out_shape=LIKE((rows, width), FLOAT),
        compiler_params=params(),
        cost_estimate=pl.CostEstimate(
            flops=6 * rows * width * width, bytes_accessed=10 * 1024 * 1024, transcendentals=0
        ),
        name="grad_x",
    )(grad_one, grad_joint, weight)


def advance(master, moment, average, grad, momentum, step_rate, decay_now):
    new_moment = momentum * moment + grad
    new_master = master - step_rate * (grad + momentum * new_moment)
    new_average = decay_now * average + (1.0 - decay_now) * new_master
    return (new_moment, new_average, new_master, new_master.astype(HALF))


def stepper(rates_ref, state_refs, out_refs):
    rates = [rates_ref[at] for at in range(3)]

    def step(weight, where, grad):
        state = [ref[where] for ref in state_refs[3 * weight : 3 * weight + 3]]
        for ref, item in zip(out_refs[4 * weight : 4 * weight + 4], advance(*state, grad, *rates)):
            ref[where] = item

    return step


def second_step_kernel(rates_ref, *refs):
    middle, late = block_sum(refs[:2]), block_sum(refs[2:4])
    state_refs, out_refs, (first_ref, small_ref) = refs[4:13], refs[13:25], refs[25:]
    width = small_ref.shape[2]
    step = stepper(rates_ref, state_refs, out_refs)
    for layer, piece in enumerate((middle[FIRST_ROWS:], late)):
        step(0, (layer,), piece[0:16])
        step(1, (layer, slice(None), slice(0, width)), piece[16:32])
        step(1, (layer, slice(None), slice(width, 2 * width)), piece[32:48])
        step(2, (layer,), piece[48:80])
        small_ref[layer] = piece[80:96]
    first_ref[...] = middle[:FIRST_ROWS]


def step_shapes(masters):
    return [
        LIKE(master.shape, kind) for master in masters for kind in (FLOAT, FLOAT, FLOAT, HALF)
    ]


def step_call(kernel, rates, inputs, out_shape, name):
    return pl.pallas_call(
        kernel,
        in_specs=[pl.BlockSpec(memory_space=pltpu.SMEM)] * len(rates)
        + [pl.BlockSpec(memory_space=pltpu.VMEM)] * len(inputs),
        out_specs=[pl.BlockSpec(memory_space=pltpu.VMEM)] * len(out_shape),
        out_shape=out_shape,
        compiler_params=params(SMALL_LIMIT),
        cost_estimate=pl.CostEstimate(flops=0, bytes_accessed=1 << 22, transcendentals=0),
        name=name,
    )(*rates, *inputs)


def first_step_kernel(place_ref, rates_ref, small_ref, late_ref, *refs):
    blocks, state_refs, out_refs = refs[:4], refs[4:13], refs[13:]
    width = small_ref.shape[2]
    each = out_refs[4].shape[2]
    step = stepper(rates_ref, state_refs, out_refs)
    turn = width - place_ref[0] * each
    for layer, total in enumerate((block_sum(blocks), late_ref[...])):
        for piece in range(3):
            columns = slice(piece * width, (piece + 1) * width)
            step(0, (layer, slice(None), columns), total[piece * 16 : (piece + 1) * 16])
        own_first = pltpu.roll(total[48:64], turn, 1)[:, :each]
        own_second = pltpu.roll(small_ref[layer], turn, 1)[:, :each]
        step(1, (layer,), own_second[0:2])
        step(2, (layer, slice(0, 2)), own_first[0:2])
        step(2, (layer, slice(2, 8)), own_second[2:8])


def wide_to_rows(shard, width):
    return jnp.concatenate(
        [shard[:, at * width : (at + 1) * width] for at in range(shard.shape[1] // width)]
    )


def rows_to_wide(rows, pieces):
    each = rows.shape[0] // pieces
    return jnp.concatenate([rows[at * each : (at + 1) * each] for at in range(pieces)], axis=1)


def gather_rows(shards_by_part, small):
    width = small.shape[1]
    parts = []
    for shard in shards_by_part:
        whole = lax.all_gather(shard, AXES, axis=0, tiled=False)
        parts.append(whole.reshape(OWNERS, -1, width))
    smalls = jnp.broadcast_to(small[None] * (jnp.arange(OWNERS) == 0)[:, None, None].astype(HALF),
                              (OWNERS, *small.shape))
    slots = jnp.concatenate([*parts, smalls], axis=1)[np.array(ORDER)]
    return [slots[4 * at : 4 * at + 4] for at in range(8)]


def scatter_rows(kept, sent, parts):
    slots = jnp.concatenate([kept, sent])[np.argsort(np.array(ORDER))]
    everyone = lax.axis_size(AXES)
    own, start = [], 0
    for rows in parts:
        piece = slots[:, start : start + rows].reshape(everyone, -1, slots.shape[2])
        own.append(lax.psum_scatter(piece, AXES, scatter_dimension=0, tiled=False).astype(FLOAT))
        start += rows
    return own, lax.psum(slots[0, start:].astype(FLOAT), AXES)


def sync(*items):
    return lax.optimization_barrier(items)


def any_size(place, x, cotangent, dataset_ids, live, masters, moments, averages, rates):
    layers = masters[0].shape[0]
    width = x.shape[1]
    position = lax.axis_index(AXES)
    low = lambda item: item.astype(HALF)
    own = low(jnp.concatenate([masters[4], masters[5]], axis=1))
    wide = lax.all_gather(own, AXES, axis=2, tiled=True)
    onehot = (dataset_ids[0] == jnp.arange(width, dtype=jnp.int32)).astype(FLOAT)
    counts = low(lax.psum(onehot, AXES))[None]
    first, second = [], []
    for at in range(layers):
        pad = lambda rows: jnp.pad(rows, ((0, 16 - rows.shape[0]), (0, 0)))
        attend_w = masters[0][at]
        first.append(gather_rows(
            [low(attend_w[:, piece * width : (piece + 1) * width]) for piece in range(3)],
            pad(wide[at, 2:4]),
        ))
        expand_w = masters[2][at]
        second.append(gather_rows(
            [low(masters[1][at]), low(expand_w[:, :width]), low(expand_w[:, width:]),
             low(masters[3][at])],
            pad(jnp.concatenate([wide[at, 0:2], wide[at, 4:10], counts])),
        ))
    current = x
    saved = []
    for at in range(layers):
        joint, probs, mixed, weight = attend_call(place, current, first[at])
        keep = (current, joint, probs, mixed, weight)
        if at + 1 < layers:
            current, *rest = dense_call(place, current, mixed, second[at])
            keep = (*keep, rest)
        saved.append(keep)
    first_grads, second_grads = [None] * layers, [None] * layers
    for at in reversed(range(layers)):
        start, joint, probs, mixed, weight = saved[at][:5]
        if at + 1 == layers:
            result, grad_mixed, grad_one, *slots = dense_turn_call(
                place, live, dataset_ids, start, mixed, second[at], cotangent
            )
        else:
            grad_mixed, grad_one, *slots = dense_back_call(
                place, grad_one, grad_joint, saved[at + 1][4], mixed, saved[at][5]
            )
        second_grads[at] = slots
        *slots, grad_joint = attend_back_call(place, start, joint, probs, grad_mixed)
        first_grads[at] = slots
    grad_rows = grad_x_call(grad_one, grad_joint, weight)
    grads = [[] for _ in range(6)]
    for at in range(layers):
        kept, sent = first_grads[at]
        own, first_small = scatter_rows(kept, sent, (16, 16, 16))
        grads[0].append(jnp.concatenate(own, axis=1))
        own, small = scatter_rows(*second_grads[at], (16, 16, 16, 32))
        grads[1].append(own[0])
        grads[2].append(jnp.concatenate(own[1:3], axis=1))
        grads[3].append(own[3])
        rows = jnp.concatenate([small[0:2], first_small[0:2], small[2:8]])
        lanes = masters[4].shape[2]
        own_rows = lax.dynamic_slice(rows, (0, position * lanes), (10, lanes))
        grads[4].append(own_rows[:2])
        grads[5].append(own_rows[2:])
    outputs = []
    for master, moment, average, grad in zip(masters, moments, averages, grads):
        outputs.extend(
            advance(master, moment, average, jnp.stack(grad), rates[0], rates[1], rates[2])
        )
    return (result, grad_rows, *outputs)


def one_per_owner(place, x, cotangent, dataset_ids, live, masters, moments, averages, rates):
    width = x.shape[1]
    pair = HEADS // 2

    def to_core(stacks):
        return [swap(one, CORE) for one in stacks]

    def square(block):
        return swaps(block, SQUARE[1:])

    def square_back(stacks):
        return [swap(one, offset) for one, offset in zip(stacks[1:], SQUARE[1:])]

    def chain_back(blocks):
        return [swap(one, offset) for one, offset in zip(blocks[1:], CHAIN[1:])]

    near, following, late = pack_call(place, dataset_ids, masters)
    (first_own,) = join_call([near, *swaps(near, CHAIN[1:])])

    first_own, following, late = sync(first_own, following, late)
    first_near = [first_own, *square(first_own)]
    (following_two,) = join_call([following, swap(following, CHAIN[1])])
    (late_two,) = join_call([late, swap(late, CHAIN[1])])
    (second_own,) = join_call([following_two, swap(following_two, CHAIN[2])])
    first_far = to_core(first_near)

    first_far, second_own, x, late_two = sync(first_far, second_own, x, late_two)
    second_near = [second_own, *square(second_own)]
    late_got = swap(late_two, CHAIN[2])
    joint, probs, mixed, weight = attend_call(place, x, [*first_near, *first_far])

    mixed, second_near, late_two, late_got = sync(mixed, second_near, late_two, late_got)
    third_own, late_own = join_call(
        [late_two, late_got], (0, FIRST_ROWS), (FIRST_ROWS, SECOND_ROWS)
    )
    second_far = to_core(second_near)
    second_far, third_own, mixed = sync(second_far, third_own, mixed)
    third_near = [third_own, *square(third_own)]
    third_far = [swap(third_own, CORE)]
    middle, *dense_kept = dense_call(place, x, mixed, [*second_near, *second_far])

    middle, third_near, third_far, late_own = sync(middle, third_near, third_far, late_own)
    third_far += to_core(third_near[1:])
    third_far, late_own, middle = sync(third_far, late_own, middle)
    late_near = [late_own, *square(late_own)]
    late_far = [swap(late_own, CORE)]
    late_joint, late_probs, late_mixed, late_weight = attend_call(
        place, middle, [*third_near, *third_far]
    )

    late_mixed, late_near, late_far = sync(late_mixed, late_near, late_far)
    late_far += to_core(late_near[1:])
    result, grad_mixed, grad_one, kept, sent = dense_turn_call(
        place, live, dataset_ids, middle, late_mixed, [*late_near, *late_far], cotangent
    )

    sent, grad_mixed = sync(sent, grad_mixed)
    got = swap(sent, CORE)
    next_kept, next_sent, grad_joint = attend_back_call(
        place, middle, late_joint, late_probs, grad_mixed
    )

    got, next_sent, grad_joint = sync(got, next_sent, grad_joint)
    late_stacks = core_sum(kept, got)
    late_stacks, next_sent, grad_joint = sync(late_stacks, next_sent, grad_joint)
    late_got = square_back(late_stacks)
    got = swap(next_sent, CORE)
    grad_mixed, grad_one, kept, sent = dense_back_call(
        place, grad_one, grad_joint, late_weight, mixed, dense_kept
    )

    got, late_got, sent, grad_mixed = sync(got, late_got, sent, grad_mixed)
    first_stacks = core_sum(next_kept, got)
    late_kept, late_sent = square_sum_call([late_stacks[0], *late_got])
    first_stacks, late_kept, late_sent, sent, grad_mixed = sync(
        first_stacks, late_kept, late_sent, sent, grad_mixed
    )
    first_got = square_back(first_stacks)
    got = swap(sent, CORE)
    late_got = swap(late_sent, CHAIN[2])
    before = attend_back_call(place, x, joint, probs, grad_mixed, 0, pair)

    got, first_got, late_got, before = sync(got, first_got, late_got, before)
    second_stacks = core_sum(kept, got)
    late_own, late_sent = pair_sum(late_kept, late_got)
    second_stacks, before, late_sent = sync(second_stacks, before, late_sent)
    second_got = square_back(second_stacks)
    late_got = swap(late_sent, CHAIN[1])
    kept, sent, grad_joint = attend_back_call(
        place, x, joint, probs, grad_mixed, pair, HEADS - pair, before
    )

    second_got, sent, grad_joint, late_got = sync(second_got, sent, grad_joint, late_got)
    got = swap(sent, CORE)
    middle_kept, middle_sent = square_sum_call(
        [first_stacks[0], *first_got], [second_stacks[0], *second_got]
    )
    got, middle_sent = sync(got, middle_sent)
    stacks = core_sum(kept, got)
    stacks, middle_sent, grad_joint = sync(stacks, middle_sent, grad_joint)
    got = square_back(stacks)
    middle_got = swap(middle_sent, CHAIN[2])
    grad_rows = grad_x_call(grad_one, grad_joint, weight)

    middle_got, grad_rows = sync(middle_got, grad_rows)
    middle_own, middle_sent = pair_sum(middle_kept, middle_got)
    middle_got = swap(middle_sent, CHAIN[1])

    def state_of(*which):
        return [item for at in which for item in (masters[at], moments[at], averages[at])]

    last_blocks = square_sum_call([stacks[0], *got], halves=False)
    last_got = chain_back(last_blocks)
    *stepped, late_first, small = step_call(
        second_step_kernel,
        [rates],
        [middle_own, middle_got, late_own, late_got, *state_of(1, 2, 3)],
        [*step_shapes(masters[1:4]), LIKE((FIRST_ROWS, width), FLOAT),
         LIKE((2, 16, width), FLOAT)],
        "second_step",
    )
    rest = step_call(
        first_step_kernel,
        [place, rates],
        [small, late_first, last_blocks[0], *last_got, *state_of(0, 4, 5)],
        step_shapes((masters[0], masters[4], masters[5])),
        "first_step",
    )
    return (result, grad_rows, *rest[:4], *stepped, *rest[4:])


def shards(
    tokens,
    cotangent,
    dataset_ids,
    query_counts,
    learn_rate,
    momentum_coef,
    average_decay,
    step_count,
    *state,
):
    masters, moments, averages = state[0::3], state[1::3], state[2::3]
    position = lax.axis_index(AXES)
    direct = lax.axis_size(AXES) == OWNERS
    place = (position if direct else jnp.zeros_like(position)).astype(jnp.int32).reshape(1)
    step_value = step_count[0].astype(FLOAT)
    decay_now = average_decay[0] * (1.0 + step_value) / (4.0 + step_value)
    rates = jnp.stack([momentum_coef[0], learn_rate[0], decay_now])
    run = one_per_owner if direct else any_size
    result, grad_rows, *outputs = run(
        place, tokens[0], cotangent[0], dataset_ids, query_counts + CTX, masters, moments, averages,
        rates,
    )
    return (result[None], grad_rows[None], *outputs)


def solution(mesh):
    rows = P(AXES, None, None)
    weight = P(None, AXES, None)
    vector = P(None, None, AXES)
    scalar = P()
    return jax.shard_map(
        shards,
        mesh=mesh,
        in_specs=(rows, rows, P(AXES), P(AXES), *[scalar] * 4, *[weight] * 12, *[vector] * 6),
        out_specs=(rows, rows, *[weight] * 16, *[vector] * 8),
        check_vma=False,
    )
```

```python
import functools

import jax
import jax.numpy as jnp
import numpy as np
from jax import lax
from jax.experimental import pallas as pl
from jax.experimental.pallas import tpu as pltpu
from jax.sharding import PartitionSpec as P

HEADS = 4
CTX = 896
NDS = 8
EPS = 1e-05
OWNERS = 32
AXES = ("dp", "fsdp")

CHAIN = (0, 4, 2, 6)
SQUARE = (0, 1, 16, 17)
CORE = 8
ORDER = tuple(core ^ side ^ link for core in (0, CORE) for side in SQUARE for link in CHAIN)

FIRST_ROWS = 56
SECOND_ROWS = 88

ROW_BLOCK = 512
BACK_BLOCK = 256
ROOT_HALF = 0.7071067811865476
PDF_PEAK = 0.3989422804014327
VMEM_LIMIT = 60 * 1024 * 1024
SMALL_LIMIT = 12 * 1024 * 1024
FLOAT = jnp.float32
HALF = jnp.bfloat16
LIKE = jax.ShapeDtypeStruct


def product(left, right, left_dim, right_dim):
    return lax.dot_general(
        left, right, (((left_dim,), (right_dim,)), ((), ())), preferred_element_type=FLOAT
    )


def owner_rows(offset, place, rows):
    return pl.ds(pl.multiple_of((offset ^ place) * rows, rows), rows)


def params(limit=VMEM_LIMIT):
    return pltpu.CompilerParams(vmem_limit_bytes=limit)


def pack_kernel(place_ref, ids_ref, attend_ref, output_ref, expand_ref, shrink_ref, gains_ref,
                bias_ref, near_ref, next_ref, late_ref, small):
    width = near_ref.shape[1]
    each = gains_ref.shape[2]
    lane = lax.broadcasted_iota(jnp.int32, (each, width), 1)
    own = lax.broadcasted_iota(jnp.int32, (each, width), 0) + place_ref[0] * each
    pick = (lane == own).astype(HALF)
    lanes = lax.broadcasted_iota(jnp.int32, (1, width), 1)

    for layer in range(attend_ref.shape[0]):
        first, second, top = (
            (near_ref, next_ref, 0) if layer == 0 else (late_ref, late_ref, FIRST_ROWS)
        )
        gains = product(gains_ref[layer].astype(HALF), pick, 1, 0)
        biases = product(bias_ref[layer].astype(HALF), pick, 1, 0)
        for piece in range(3):
            first[piece * 16 : (piece + 1) * 16, :] = attend_ref[
                layer, :, piece * width : (piece + 1) * width
            ].astype(HALF)
        small[...] = jnp.zeros_like(small)
        small[0:2, :] = biases[0:2, :]
        small[2:3, :] = (lanes == ids_ref[0]).astype(FLOAT)
        first[48:56, :] = small[...].astype(HALF)
        second[top : top + 16, :] = output_ref[layer].astype(HALF)
        for piece in range(2):
            second[top + (piece + 1) * 16 : top + (piece + 2) * 16, :] = expand_ref[
                layer, :, piece * width : (piece + 1) * width
            ].astype(HALF)
        second[top + 48 : top + 80, :] = shrink_ref[layer].astype(HALF)
        small[0:2, :] = gains
        small[2:8, :] = biases[2:8, :]
        second[top + 80 : top + 88, :] = small[...].astype(HALF)


def pack_call(place, ids, masters):
    width = masters[1].shape[2]
    rows = (FIRST_ROWS, SECOND_ROWS, FIRST_ROWS + SECOND_ROWS)
    return pl.pallas_call(
        pack_kernel,
        in_specs=[pl.BlockSpec(memory_space=pltpu.SMEM)] * 2
        + [pl.BlockSpec(memory_space=pltpu.VMEM)] * 6,
        out_specs=[pl.BlockSpec(memory_space=pltpu.VMEM)] * 3,
        out_shape=[LIKE((count, width), HALF) for count in rows],
        scratch_shapes=[pltpu.VMEM((8, width), FLOAT)],
        compiler_params=params(),
        cost_estimate=pl.CostEstimate(flops=0, bytes_accessed=1 << 20, transcendentals=0),
        name="pack",
    )(place, ids, *masters)


def join_kernel(cuts, count, *refs):
    each = refs[count].shape[0] // count
    for at in range(count):
        for to, (start, rows) in enumerate(cuts):
            target = refs[count + to]
            if len(refs[at].shape) == 2:
                target[at] = refs[at][start : start + rows, :]
            else:
                target[at * each : (at + 1) * each] = refs[at][:, start : start + rows, :]


def join_call(blocks, *cuts):
    *head, rows, width = blocks[0].shape
    slots = len(blocks) * (head[0] if head else 1)
    cuts = cuts or ((0, rows),)
    return pl.pallas_call(
        functools.partial(join_kernel, cuts, len(blocks)),
        out_shape=[LIKE((slots, rows, width), HALF) for _, rows in cuts],
        compiler_params=params(SMALL_LIMIT),
        cost_estimate=pl.CostEstimate(flops=0, bytes_accessed=1 << 20, transcendentals=0),
        name="join",
    )(*blocks)


def block_sum(refs):
    total = refs[0][...].astype(FLOAT)
    for ref in refs[1:]:
        total = total + ref[...].astype(FLOAT)
    return total


def core_sum(kept, got):
    return [
        (kept[at : at + 4].astype(FLOAT) + got[at : at + 4].astype(FLOAT)).astype(HALF)
        for at in range(0, 16, 4)
    ]


def square_sum_kernel(rows, *refs):
    outs = refs[4 * len(rows) :]
    start = 0
    for at, count in enumerate(rows):
        total = block_sum(refs[4 * at : 4 * at + 4]).astype(HALF)
        for to in range(4):
            each = 4 // len(outs)
            if each == 1:
                outs[to][start : start + count, :] = total[to]
            else:
                outs[to // each][to % each, start : start + count, :] = total[to]
        start += count


def square_sum_call(*pieces, halves=True):
    rows = tuple(stacks[0].shape[1] for stacks in pieces)
    shape = (sum(rows), pieces[0][0].shape[2])
    return pl.pallas_call(
        functools.partial(square_sum_kernel, rows),
        out_shape=[LIKE((2, *shape), HALF)] * 2 if halves else [LIKE(shape, HALF)] * 4,
        compiler_params=params(SMALL_LIMIT),
        cost_estimate=pl.CostEstimate(flops=0, bytes_accessed=1 << 21, transcendentals=0),
        name="square_sum",
    )(*[stack for stacks in pieces for stack in stacks])


def pair_sum(kept, got):
    return [(kept[at].astype(FLOAT) + got[at].astype(FLOAT)).astype(HALF) for at in range(2)]


def swap(block, offset):
    return lax.ppermute(block, AXES, [(one, one ^ offset) for one in range(OWNERS)])


def swaps(block, offsets):
    return [swap(block, offset) for offset in offsets]


def slot_places(slot_refs):
    for at, offset in enumerate(ORDER):
        yield slot_refs[at // 4], at % 4, offset


def small_rows(slot_refs, start):
    total = None
    for slots in slot_refs:
        for at in range(slots.shape[0]):
            block = slots[at, start : start + 8, :].astype(FLOAT)
            total = block if total is None else total + block
    return total


def attend_kernel(place_ref, x_ref, *refs):
    slot_refs = refs[:8]
    joint_ref, probs_ref, mixed_ref, weight_ref, small_ref = refs[8:]
    head_size = mixed_ref.shape[1]
    place = place_ref[0]

    for slots, at, offset in slot_places(slot_refs):
        rows = owner_rows(offset, place, 16)
        for piece in range(3):
            weight_ref[0, rows, piece * head_size : (piece + 1) * head_size] = slots[
                at, piece * 16 : (piece + 1) * 16, :
            ]
    zeros = jnp.zeros((1, head_size), FLOAT)
    small = small_rows(slot_refs, 48)
    small_ref[...] = small
    shift = jnp.concatenate([small[0:1, :], zeros, small[1:2, :]], axis=1)
    joint_ref[0] = (product(x_ref[...], weight_ref[0], 1, 0) + shift).astype(HALF)
    keys = joint_ref[0, :CTX, head_size : 2 * head_size]
    values = joint_ref[0, :CTX, 2 * head_size :]
    values_turned = jnp.transpose(values)
    factor = head_size ** (-0.5) * 1.4426950408889634
    scores = product(keys, joint_ref[0, :, :head_size], 1, 1)
    top = jnp.max(scores, axis=0, keepdims=True)
    grown = jnp.exp2((scores - top) * factor)
    total = jnp.sum(grown, axis=0, keepdims=True)
    probs = (grown * (1.0 / total)).astype(HALF)
    probs_ref[0] = probs
    mixed_ref[...] = jnp.transpose(product(values_turned, probs, 1, 0)).astype(HALF)


def attend_call(place, x, slots):
    rows, width = x.shape
    head_size = width // HEADS
    return pl.pallas_call(
        attend_kernel,
        grid_spec=pltpu.PrefetchScalarGridSpec(
            num_scalar_prefetch=1,
            grid=(HEADS,),
            in_specs=[pl.BlockSpec((rows, width), lambda h, p: (0, 0))]
            + [pl.BlockSpec((part.shape[0], FIRST_ROWS, head_size), lambda h, p: (0, 0, h))
               for part in slots],
            out_specs=[
                pl.BlockSpec((1, rows, 3 * head_size), lambda h, p: (h, 0, 0)),
                pl.BlockSpec((1, CTX, rows), lambda h, p: (h, 0, 0)),
                pl.BlockSpec((rows, head_size), lambda h, p: (0, h)),
                pl.BlockSpec((1, width, 3 * head_size), lambda h, p: (h, 0, 0)),
                pl.BlockSpec((8, head_size), lambda h, p: (0, h)),
            ],
        ),
        out_shape=[
            LIKE((HEADS, rows, 3 * head_size), HALF),
            LIKE((HEADS, CTX, rows), HALF),
            LIKE((rows, HEADS * head_size), HALF),
            LIKE((HEADS, width, 3 * head_size), HALF),
            LIKE((8, width), FLOAT),
        ],
        compiler_params=params(),
        cost_estimate=pl.CostEstimate(
            flops=HEADS * (2 * rows * width * 3 * head_size + 4 * rows * CTX * head_size),
            bytes_accessed=HEADS * 4 * 1024 * 1024,
            transcendentals=HEADS * rows * CTX,
        ),
        name="attend",
    )(place, x, *slots)


def unpack_second(place, slot_refs, output_w, expand_w, shrink_w, vec_ref):
    width = output_w.shape[1]
    for slots, at, offset in slot_places(slot_refs):
        rows = owner_rows(offset, place, 16)
        output_w[rows, :] = slots[at, 0:16, :]
        expand_w[rows, :width] = slots[at, 16:32, :]
        expand_w[rows, width:] = slots[at, 32:48, :]
        shrink_w[owner_rows(offset, place, 32), :] = slots[at, 48:80, :]
    vec_ref[...] = small_rows(slot_refs, 80)


def row_mean(rows):
    return jnp.mean(rows, axis=-1, keepdims=True)


def normalize(rows):
    centred = rows - row_mean(rows)
    inv_std = lax.rsqrt(row_mean(centred * centred) + EPS)
    return (centred * inv_std, inv_std)


def forward_rows(x_ref, mixed_ref, vec_ref, output_w, expand_w, shrink_w):
    attn_out = product(mixed_ref[...], output_w[...], 1, 0) + vec_ref[2:3, :]
    unit_one, inv_one = normalize(x_ref[...].astype(FLOAT) + attn_out)
    first_norm = unit_one * vec_ref[0:1, :] + vec_ref[4:5, :]
    first_low = first_norm.astype(HALF)
    shift = jnp.concatenate([vec_ref[6:7, :], vec_ref[7:8, :]], axis=1)
    hidden = product(first_low, expand_w[...], 1, 0) + shift
    normal_cdf = 0.5 * (1.0 + lax.erf(hidden * ROOT_HALF))
    act_low = (hidden * normal_cdf).astype(HALF)
    slope = normal_cdf + hidden * (jnp.exp(-0.5 * hidden * hidden) * PDF_PEAK)
    branch = product(act_low, shrink_w[...], 1, 0) + vec_ref[3:4, :]
    unit_two, inv_two = normalize(first_norm + branch)
    result = unit_two * vec_ref[1:2, :] + vec_ref[5:6, :]
    return (unit_one, inv_one, first_low, act_low, slope, unit_two, inv_two, result)


def column_sum(rows):
    return jnp.sum(rows, axis=0, keepdims=True)


def backward_rows(grad_rows, mixed_ref, vec_ref, kept, output_w, expand_w, shrink_w,
                  grad_mixed_ref, grad_one_ref, grad_output, grad_expand, grad_shrink, sums):
    unit_one, inv_one, first_low, act_low, slope, unit_two, inv_two = kept
    width = grad_rows.shape[1]

    def layer_norm_back(rows, unit_rows, inv_std, gain):
        scaled = rows * gain
        return inv_std * (scaled - row_mean(scaled) - unit_rows * row_mean(scaled * unit_rows))

    grad_two = layer_norm_back(grad_rows, unit_two, inv_two, vec_ref[1:2, :])
    branch_low = grad_two.astype(HALF)
    grad_shrink[...] += product(act_low, branch_low, 0, 0)
    grad_hidden = (product(branch_low, shrink_w[...], 1, 1) * slope).astype(HALF)
    grad_expand[...] += product(first_low, grad_hidden, 0, 0)
    grad_first = grad_two + product(grad_hidden, expand_w[...], 1, 1)
    grad_one = layer_norm_back(grad_first, unit_one, inv_one, vec_ref[0:1, :])
    attn_low = grad_one.astype(HALF)
    grad_output[...] += product(mixed_ref[...], attn_low, 0, 0)
    grad_mixed_ref[...] = product(attn_low, output_w[...], 1, 1).astype(HALF)
    grad_one_ref[...] = grad_one
    sums[0:1, :] += column_sum(grad_first * unit_one)
    sums[1:2, :] += column_sum(grad_rows * unit_two)
    sums[2:3, :] += column_sum(attn_low.astype(FLOAT))
    sums[3:4, :] += column_sum(branch_low.astype(FLOAT))
    sums[4:5, :] += column_sum(grad_first)
    sums[5:6, :] += column_sum(grad_rows)
    hidden_sum = column_sum(grad_hidden.astype(FLOAT))
    sums[6:7, :] += hidden_sum[:, :width]
    sums[7:8, :] += hidden_sum[:, width:]


def pack_second(place, kept_ref, sent_ref, grad_output, grad_expand, grad_shrink, sums):
    width = grad_output.shape[1]
    small = sums[...].astype(HALF)
    for at, offset in enumerate(ORDER):
        slots_ref = kept_ref if at < 16 else sent_ref
        at = at % 16
        rows = owner_rows(offset, place, 16)
        slots_ref[at, 0:16, :] = grad_output[rows, :].astype(HALF)
        slots_ref[at, 16:32, :] = grad_expand[rows, :width].astype(HALF)
        slots_ref[at, 32:48, :] = grad_expand[rows, width:].astype(HALF)
        slots_ref[at, 48:80, :] = grad_shrink[owner_rows(offset, place, 32), :].astype(HALF)
        slots_ref[at, 80:88, :] = small


def dense_kernel(place_ref, x_ref, mixed_ref, *refs):
    slot_refs = refs[:8]
    (result_ref, unit_one_ref, inv_one_ref, act_ref, slope_ref, unit_two_ref, inv_two_ref, output_w,
     expand_w, shrink_w, vec_ref) = refs[8:]

    @pl.when(pl.program_id(0) == 0)
    def _():
        unpack_second(place_ref[0], slot_refs, output_w, expand_w, shrink_w, vec_ref)

    unit_one, inv_one, _, act_low, slope, unit_two, inv_two, result = forward_rows(
        x_ref, mixed_ref, vec_ref, output_w, expand_w, shrink_w
    )
    result_ref[...] = result.astype(HALF)
    unit_one_ref[...] = unit_one
    inv_one_ref[...] = inv_one
    act_ref[...] = act_low
    slope_ref[...] = slope
    unit_two_ref[...] = unit_two
    inv_two_ref[...] = inv_two


def grad_x_rows(grad_one_ref, grad_joint_ref, weight_ref):
    total = grad_one_ref[...]
    for head in range(weight_ref.shape[0]):
        total = total + product(grad_joint_ref[head], weight_ref[head], 1, 1)
    return total


def clear(*items):
    for item in items:
        item[...] = jnp.zeros_like(item)


def dense_back_kernel(place_ref, grad_one_next, grad_joint_next, weight_next, mixed_ref, *refs):
    (unit_one_ref, inv_one_ref, act_ref, slope_ref, unit_two_ref, inv_two_ref, output_w, expand_w,
     shrink_w, vec_ref, grad_mixed_ref, grad_one_ref, kept_ref, sent_ref, sums, grad_output,
     grad_expand, grad_shrink) = refs

    @pl.when(pl.program_id(0) == 0)
    def _():
        clear(sums, grad_output, grad_expand, grad_shrink)

    unit_one = unit_one_ref[...]
    first_low = (unit_one * vec_ref[0:1, :] + vec_ref[4:5, :]).astype(HALF)
    kept = (unit_one, inv_one_ref[...], first_low, act_ref[...], slope_ref[...], unit_two_ref[...],
            inv_two_ref[...])
    grad_rows = grad_x_rows(grad_one_next, grad_joint_next, weight_next)
    backward_rows(grad_rows, mixed_ref, vec_ref, kept, output_w, expand_w, shrink_w,
                  grad_mixed_ref, grad_one_ref, grad_output, grad_expand, grad_shrink, sums)

    @pl.when(pl.program_id(0) == pl.num_programs(0) - 1)
    def _():
        pack_second(place_ref[0], kept_ref, sent_ref, grad_output, grad_expand, grad_shrink, sums)


def dense_turn_kernel(place_ref, live_ref, ids_ref, x_ref, mixed_ref, *refs):
    slot_refs = refs[:8]
    (counts_ref, cot_ref, result_ref, grad_mixed_ref, grad_one_ref, kept_ref, sent_ref, output_w, expand_w,
     shrink_w, vec_ref, grad_output, grad_expand, grad_shrink, sums) = refs[8:]
    step = pl.program_id(0)

    @pl.when(step == 0)
    def _():
        unpack_second(place_ref[0], slot_refs, output_w, expand_w, shrink_w, vec_ref)
        clear(sums, grad_output, grad_expand, grad_shrink)

    *kept, result = forward_rows(x_ref, mixed_ref, vec_ref, output_w, expand_w, shrink_w)
    result_ref[...] = result.astype(HALF)
    counts = counts_ref[2:3, :]
    lanes = lax.broadcasted_iota(jnp.int32, counts.shape, 1)
    own_count = jnp.sum(jnp.where(lanes == ids_ref[0], counts, 0.0), axis=1, keepdims=True)
    row_weight = jnp.sum(counts, axis=1, keepdims=True) / (NDS * own_count)
    rows = cot_ref.shape[0]
    slot = lax.broadcasted_iota(jnp.int32, (rows, 1), 0) + step * rows
    grad_rows = cot_ref[...].astype(FLOAT) * jnp.where(slot < live_ref[0], row_weight, 0.0)
    backward_rows(grad_rows, mixed_ref, vec_ref, kept, output_w, expand_w, shrink_w,
                  grad_mixed_ref, grad_one_ref, grad_output, grad_expand, grad_shrink, sums)

    @pl.when(step == pl.num_programs(0) - 1)
    def _():
        pack_second(place_ref[0], kept_ref, sent_ref, grad_output, grad_expand, grad_shrink, sums)


def by_rows(width, block=ROW_BLOCK):
    return pl.BlockSpec((block, width), lambda i, *p: (i, 0))


def fixed(*shape):
    return pl.BlockSpec(shape, lambda i, *p: (0,) * len(shape))


def joint_rows(grad_joint, block=ROW_BLOCK):
    heads, _, width = grad_joint.shape
    return pl.BlockSpec((heads, block, width), lambda i, *p: (0, i, 0))


def weight_shapes(width):
    return [(width, width), (width, 2 * width), (2 * width, width)]


def dense_call(place, x, mixed, slots):
    rows, width = x.shape
    weights = weight_shapes(width)
    return pl.pallas_call(
        dense_kernel,
        grid_spec=pltpu.PrefetchScalarGridSpec(
            num_scalar_prefetch=1,
            grid=(rows // ROW_BLOCK,),
            in_specs=[by_rows(width)] * 2
            + [fixed(*part.shape) for part in slots],
            out_specs=[by_rows(width), by_rows(width), by_rows(1), by_rows(2 * width),
                       by_rows(2 * width), by_rows(width), by_rows(1)]
            + [fixed(*shape) for shape in weights]
            + [fixed(8, width)],
        ),
        out_shape=[LIKE((rows, width), HALF), LIKE((rows, width), FLOAT), LIKE((rows, 1), FLOAT),
                   LIKE((rows, 2 * width), HALF), LIKE((rows, 2 * width), FLOAT),
                   LIKE((rows, width), FLOAT), LIKE((rows, 1), FLOAT)]
        + [LIKE(shape, HALF) for shape in weights]
        + [LIKE((8, width), FLOAT)],
        compiler_params=params(),
        cost_estimate=pl.CostEstimate(
            flops=10 * rows * width * width, bytes_accessed=16 * 1024 * 1024,
            transcendentals=4 * rows * width,
        ),
        name="dense",
    )(place, x, mixed, *slots)


def dense_back_call(place, grad_one, grad_joint, weight, mixed, kept):
    rows, width = grad_one.shape
    weights = weight_shapes(width)
    some_rows = functools.partial(by_rows, block=BACK_BLOCK)
    return pl.pallas_call(
        dense_back_kernel,
        grid_spec=pltpu.PrefetchScalarGridSpec(
            num_scalar_prefetch=1,
            grid=(rows // BACK_BLOCK,),
            in_specs=[some_rows(width), joint_rows(grad_joint, BACK_BLOCK), fixed(*weight.shape), some_rows(width)]
            + [some_rows(width), some_rows(1), some_rows(2 * width), some_rows(2 * width), some_rows(width),
               some_rows(1)]
            + [fixed(*shape) for shape in weights]
            + [fixed(8, width)],
            out_specs=[some_rows(width), some_rows(width)] + [fixed(16, SECOND_ROWS, width)] * 2,
            scratch_shapes=[pltpu.VMEM((8, width), FLOAT)]
            + [pltpu.VMEM(shape, FLOAT) for shape in weights],
        ),
        out_shape=[LIKE((rows, width), HALF), LIKE((rows, width), FLOAT)]
        + [LIKE((16, SECOND_ROWS, width), HALF)] * 2,
        compiler_params=params(),
        cost_estimate=pl.CostEstimate(
            flops=26 * rows * width * width, bytes_accessed=20 * 1024 * 1024, transcendentals=0
        ),
        name="dense_back",
    )(place, grad_one, grad_joint, weight, mixed, *kept)


def dense_turn_call(place, live, ids, x, mixed, slots, small, cotangent):
    rows, width = x.shape
    weights = weight_shapes(width)
    return pl.pallas_call(
        dense_turn_kernel,
        grid_spec=pltpu.PrefetchScalarGridSpec(
            num_scalar_prefetch=3,
            grid=(rows // ROW_BLOCK,),
            in_specs=[by_rows(width)] * 2
            + [fixed(*part.shape) for part in slots]
            + [fixed(8, width), by_rows(width)],
            out_specs=[by_rows(width)] * 3 + [fixed(16, SECOND_ROWS, width)] * 2,
            scratch_shapes=[pltpu.VMEM(shape, HALF) for shape in weights]
            + [pltpu.VMEM((8, width), FLOAT)]
            + [pltpu.VMEM(shape, FLOAT) for shape in weights]
            + [pltpu.VMEM((8, width), FLOAT)],
        ),
        out_shape=[LIKE((rows, width), HALF), LIKE((rows, width), HALF), LIKE((rows, width), FLOAT)]
        + [LIKE((16, SECOND_ROWS, width), HALF)] * 2,
        compiler_params=params(),
        cost_estimate=pl.CostEstimate(
            flops=30 * rows * width * width, bytes_accessed=16 * 1024 * 1024,
            transcendentals=4 * rows * width,
        ),
        name="dense_turn",
    )(place, live, ids, x, mixed, *slots, small, cotangent)


def attend_back_kernel(place_ref, x_ref, joint_ref, probs_ref, grad_mixed_ref, *refs):
    kept_ref, sent_ref, grad_joint_ref, x_turned, grad_scores, small = refs[-6:]
    grad_joint = grad_joint_ref.at[0]
    rows = x_ref.shape[0]
    head_size = grad_mixed_ref.shape[1]
    place = place_ref[0]

    @pl.when(pl.program_id(0) == 0)
    def _():
        x_turned[...] = jnp.transpose(x_ref[...])
        clear(small)

    grad_joint[CTX:, head_size:] = jnp.zeros((rows - CTX, 2 * head_size), HALF)
    keys = joint_ref[0, :CTX, head_size : 2 * head_size]
    values = joint_ref[0, :CTX, 2 * head_size :]
    keys_turned = jnp.transpose(keys)
    factor = head_size ** (-0.5)
    grad_probs = product(values, grad_mixed_ref[...], 1, 1)
    probs = probs_ref[0].astype(FLOAT)
    level = column_sum(probs * grad_probs)
    grad_low = (probs * (grad_probs - level)).astype(HALF)
    grad_scores[...] = grad_low
    grad_joint[:, :head_size] = jnp.transpose(factor * product(keys_turned, grad_low, 1, 0)).astype(
        HALF
    )
    grad_joint[:CTX, head_size : 2 * head_size] = (
        factor * product(grad_scores[...], joint_ref[0, :, :head_size], 1, 0)
    ).astype(HALF)
    grad_joint[:CTX, 2 * head_size :] = product(probs_ref[0], grad_mixed_ref[...], 1, 0).astype(HALF)
    sums = column_sum(grad_joint[...].astype(FLOAT))
    small[0:1, :] = sums[:, :head_size]
    small[1:2, :] = sums[:, 2 * head_size :]
    small_low = small[...].astype(HALF)
    grad_low = product(x_turned[...], grad_joint[...], 1, 0).astype(HALF)
    holder = grad_scores
    holder[: grad_low.shape[0], : 3 * head_size] = grad_low
    for at, offset in enumerate(ORDER):
        slots_ref = kept_ref if at < 16 else sent_ref
        at = at % 16
        span = owner_rows(offset, place, 16)
        for piece in range(3):
            slots_ref[at, piece * 16 : (piece + 1) * 16, :] = holder[
                span, piece * head_size : (piece + 1) * head_size
            ]
        slots_ref[at, 48:56, :] = small_low


def attend_back_call(place, x, joint, probs, grad_mixed, base=0, heads=HEADS, before=()):
    rows, width = x.shape
    head_size = width // HEADS
    return pl.pallas_call(
        attend_back_kernel,
        grid_spec=pltpu.PrefetchScalarGridSpec(
            num_scalar_prefetch=1,
            grid=(heads,),
            in_specs=[
                pl.BlockSpec((rows, width), lambda h, p: (0, 0)),
                pl.BlockSpec((1, rows, 3 * head_size), lambda h, p: (h + base, 0, 0)),
                pl.BlockSpec((1, CTX, rows), lambda h, p: (h + base, 0, 0)),
                pl.BlockSpec((rows, head_size), lambda h, p: (0, h + base)),
            ]
            + [pl.BlockSpec(memory_space=pl.ANY)] * len(before),
            out_specs=[pl.BlockSpec((16, FIRST_ROWS, head_size), lambda h, p: (0, 0, h + base))] * 2
            + [pl.BlockSpec((1, rows, 3 * head_size), lambda h, p: (h + base, 0, 0))],
            scratch_shapes=[pltpu.VMEM((width, rows), HALF), pltpu.VMEM((CTX, rows), HALF),
                            pltpu.VMEM((8, head_size), FLOAT)],
        ),
        out_shape=[LIKE((16, FIRST_ROWS, width), HALF)] * 2
        + [LIKE((HEADS, rows, 3 * head_size), HALF)],
        input_output_aliases={5 + at: at for at in range(len(before))},
        compiler_params=params(),
        cost_estimate=pl.CostEstimate(
            flops=heads * (6 * rows * width * head_size + 8 * rows * CTX * head_size),
            bytes_accessed=heads * 4 * 1024 * 1024, transcendentals=0,
        ),
        name="attend_back",
    )(place, x, joint, probs, grad_mixed, *before)


def grad_x_kernel(grad_one_ref, grad_joint_ref, weight_ref, grad_x_ref):
    grad_x_ref[...] = grad_x_rows(grad_one_ref, grad_joint_ref, weight_ref)


def grad_x_call(grad_one, grad_joint, weight):
    rows, width = grad_one.shape
    return pl.pallas_call(
        grad_x_kernel,
        grid=(rows // ROW_BLOCK,),
        in_specs=[
            by_rows(width),
            joint_rows(grad_joint),
            fixed(*weight.shape),
        ],
        out_specs=by_rows(width),
        out_shape=LIKE((rows, width), FLOAT),
        compiler_params=params(),
        cost_estimate=pl.CostEstimate(
            flops=6 * rows * width * width, bytes_accessed=10 * 1024 * 1024, transcendentals=0
        ),
        name="grad_x",
    )(grad_one, grad_joint, weight)


def advance(master, moment, average, grad, momentum, step_rate, decay_now):
    new_moment = momentum * moment + grad
    new_master = master - step_rate * (grad + momentum * new_moment)
    new_average = decay_now * average + (1.0 - decay_now) * new_master
    return (new_moment, new_average, new_master, new_master.astype(HALF))


def stepper(rates_ref, state_refs, out_refs):
    rates = [rates_ref[at] for at in range(3)]

    def step(weight, where, grad):
        state = [ref[where] for ref in state_refs[3 * weight : 3 * weight + 3]]
        for ref, item in zip(out_refs[4 * weight : 4 * weight + 4], advance(*state, grad, *rates)):
            ref[where] = item

    return step


def second_step_kernel(rates_ref, *refs):
    middle, late = block_sum(refs[:2]), block_sum(refs[2:4])
    state_refs, out_refs, (first_ref, small_ref) = refs[4:13], refs[13:25], refs[25:]
    width = small_ref.shape[2]
    step = stepper(rates_ref, state_refs, out_refs)
    for layer, piece in enumerate((middle[FIRST_ROWS:], late)):
        step(0, (layer,), piece[0:16])
        step(1, (layer, slice(None), slice(0, width)), piece[16:32])
        step(1, (layer, slice(None), slice(width, 2 * width)), piece[32:48])
        step(2, (layer,), piece[48:80])
        small_ref[layer] = piece[80:88]
    first_ref[...] = middle[:FIRST_ROWS]


def step_shapes(masters):
    return [
        LIKE(master.shape, kind) for master in masters for kind in (FLOAT, FLOAT, FLOAT, HALF)
    ]


def step_call(kernel, rates, inputs, out_shape, name):
    return pl.pallas_call(
        kernel,
        in_specs=[pl.BlockSpec(memory_space=pltpu.SMEM)] * len(rates)
        + [pl.BlockSpec(memory_space=pltpu.VMEM)] * len(inputs),
        out_specs=[pl.BlockSpec(memory_space=pltpu.VMEM)] * len(out_shape),
        out_shape=out_shape,
        compiler_params=params(SMALL_LIMIT),
        cost_estimate=pl.CostEstimate(flops=0, bytes_accessed=1 << 22, transcendentals=0),
        name=name,
    )(*rates, *inputs)


def first_step_kernel(place_ref, rates_ref, small_ref, late_ref, *refs):
    blocks, state_refs, out_refs = refs[:4], refs[4:13], refs[13:]
    width = small_ref.shape[2]
    each = out_refs[4].shape[2]
    step = stepper(rates_ref, state_refs, out_refs)
    turn = width - place_ref[0] * each
    for layer, total in enumerate((block_sum(blocks), late_ref[...])):
        for piece in range(3):
            columns = slice(piece * width, (piece + 1) * width)
            step(0, (layer, slice(None), columns), total[piece * 16 : (piece + 1) * 16])
        own_first = pltpu.roll(total[48:56], turn, 1)[:, :each]
        own_second = pltpu.roll(small_ref[layer], turn, 1)[:, :each]
        step(1, (layer,), own_second[0:2])
        step(2, (layer, slice(0, 2)), own_first[0:2])
        step(2, (layer, slice(2, 8)), own_second[2:8])


def wide_to_rows(shard, width):
    return jnp.concatenate(
        [shard[:, at * width : (at + 1) * width] for at in range(shard.shape[1] // width)]
    )


def rows_to_wide(rows, pieces):
    each = rows.shape[0] // pieces
    return jnp.concatenate([rows[at * each : (at + 1) * each] for at in range(pieces)], axis=1)


def gather_rows(shards_by_part, small):
    width = small.shape[1]
    parts = []
    for shard in shards_by_part:
        whole = lax.all_gather(shard, AXES, axis=0, tiled=False)
        parts.append(whole.reshape(OWNERS, -1, width))
    smalls = jnp.broadcast_to(small[None] * (jnp.arange(OWNERS) == 0)[:, None, None].astype(HALF),
                              (OWNERS, *small.shape))
    slots = jnp.concatenate([*parts, smalls], axis=1)[np.array(ORDER)]
    return [slots[4 * at : 4 * at + 4] for at in range(8)]


def scatter_rows(kept, sent, parts):
    slots = jnp.concatenate([kept, sent])[np.argsort(np.array(ORDER))]
    everyone = lax.axis_size(AXES)
    own, start = [], 0
    for rows in parts:
        piece = slots[:, start : start + rows].reshape(everyone, -1, slots.shape[2])
        own.append(lax.psum_scatter(piece, AXES, scatter_dimension=0, tiled=False).astype(FLOAT))
        start += rows
    return own, lax.psum(slots[0, start:].astype(FLOAT), AXES)


def sync(*items):
    return lax.optimization_barrier(items)


def any_size(place, x, cotangent, dataset_ids, live, masters, moments, averages, rates):
    layers = masters[0].shape[0]
    width = x.shape[1]
    position = lax.axis_index(AXES)
    low = lambda item: item.astype(HALF)
    own = low(jnp.concatenate([masters[4], masters[5]], axis=1))
    wide = lax.all_gather(own, AXES, axis=2, tiled=True)
    onehot = (dataset_ids[0] == jnp.arange(width, dtype=jnp.int32)).astype(FLOAT)
    counts = low(lax.psum(onehot, AXES))[None]
    first, second = [], []
    for at in range(layers):
        pad = lambda rows: jnp.pad(rows, ((0, 8 - rows.shape[0]), (0, 0)))
        attend_w = masters[0][at]
        first.append(gather_rows(
            [low(attend_w[:, piece * width : (piece + 1) * width]) for piece in range(3)],
            pad(jnp.concatenate([wide[at, 2:4], counts])),
        ))
        expand_w = masters[2][at]
        second.append(gather_rows(
            [low(masters[1][at]), low(expand_w[:, :width]), low(expand_w[:, width:]),
             low(masters[3][at])],
            jnp.concatenate([wide[at, 0:2], wide[at, 4:10]]),
        ))
    current = x
    saved = []
    for at in range(layers):
        joint, probs, mixed, weight, small = attend_call(place, current, first[at])
        keep = (current, joint, probs, mixed, weight)
        if at + 1 < layers:
            current, *rest = dense_call(place, current, mixed, second[at])
            keep = (*keep, rest)
        saved.append(keep)
    counted = small
    first_grads, second_grads = [None] * layers, [None] * layers
    for at in reversed(range(layers)):
        start, joint, probs, mixed, weight = saved[at][:5]
        if at + 1 == layers:
            result, grad_mixed, grad_one, *slots = dense_turn_call(
                place, live, dataset_ids, start, mixed, second[at], counted, cotangent
            )
        else:
            grad_mixed, grad_one, *slots = dense_back_call(
                place, grad_one, grad_joint, saved[at + 1][4], mixed, saved[at][5]
            )
        second_grads[at] = slots
        *slots, grad_joint = attend_back_call(place, start, joint, probs, grad_mixed)
        first_grads[at] = slots
    grad_rows = grad_x_call(grad_one, grad_joint, weight)
    grads = [[] for _ in range(6)]
    for at in range(layers):
        kept, sent = first_grads[at]
        own, first_small = scatter_rows(kept, sent, (16, 16, 16))
        grads[0].append(jnp.concatenate(own, axis=1))
        own, small = scatter_rows(*second_grads[at], (16, 16, 16, 32))
        grads[1].append(own[0])
        grads[2].append(jnp.concatenate(own[1:3], axis=1))
        grads[3].append(own[3])
        rows = jnp.concatenate([small[0:2], first_small[0:2], small[2:8]])
        lanes = masters[4].shape[2]
        own_rows = lax.dynamic_slice(rows, (0, position * lanes), (10, lanes))
        grads[4].append(own_rows[:2])
        grads[5].append(own_rows[2:])
    outputs = []
    for master, moment, average, grad in zip(masters, moments, averages, grads):
        outputs.extend(
            advance(master, moment, average, jnp.stack(grad), rates[0], rates[1], rates[2])
        )
    return (result, grad_rows, *outputs)


def one_per_owner(place, x, cotangent, dataset_ids, live, masters, moments, averages, rates):
    width = x.shape[1]
    pair = HEADS // 2

    def to_core(stacks):
        return [swap(one, CORE) for one in stacks]

    def square(block):
        return swaps(block, SQUARE[1:])

    def square_back(stacks):
        return [swap(one, offset) for one, offset in zip(stacks[1:], SQUARE[1:])]

    def chain_back(blocks):
        return [swap(one, offset) for one, offset in zip(blocks[1:], CHAIN[1:])]

    near, following, late = pack_call(place, dataset_ids, masters)
    (first_own,) = join_call([near, *swaps(near, CHAIN[1:])])

    first_own, following, late = sync(first_own, following, late)
    first_near = [first_own, *square(first_own)]
    (following_two,) = join_call([following, swap(following, CHAIN[1])])
    (late_two,) = join_call([late, swap(late, CHAIN[1])])
    (second_own,) = join_call([following_two, swap(following_two, CHAIN[2])])
    first_far = to_core(first_near)

    first_far, second_own, x, late_two = sync(first_far, second_own, x, late_two)
    second_near = [second_own, *square(second_own)]
    late_got = swap(late_two, CHAIN[2])
    joint, probs, mixed, weight, _ = attend_call(place, x, [*first_near, *first_far])

    mixed, second_near, late_two, late_got = sync(mixed, second_near, late_two, late_got)
    third_own, late_own = join_call(
        [late_two, late_got], (0, FIRST_ROWS), (FIRST_ROWS, SECOND_ROWS)
    )
    second_far = to_core(second_near)
    second_far, third_own, mixed = sync(second_far, third_own, mixed)
    third_near = [third_own, *square(third_own)]
    third_far = [swap(third_own, CORE)]
    middle, *dense_kept = dense_call(place, x, mixed, [*second_near, *second_far])

    middle, third_near, third_far, late_own = sync(middle, third_near, third_far, late_own)
    third_far += to_core(third_near[1:])
    third_far, late_own, middle = sync(third_far, late_own, middle)
    late_near = [late_own, *square(late_own)]
    late_far = [swap(late_own, CORE)]
    late_joint, late_probs, late_mixed, late_weight, small = attend_call(
        place, middle, [*third_near, *third_far]
    )

    late_mixed, late_near, late_far = sync(late_mixed, late_near, late_far)
    late_far += to_core(late_near[1:])
    result, grad_mixed, grad_one, kept, sent = dense_turn_call(
        place, live, dataset_ids, middle, late_mixed, [*late_near, *late_far], small, cotangent
    )

    sent, grad_mixed = sync(sent, grad_mixed)
    got = swap(sent, CORE)
    next_kept, next_sent, grad_joint = attend_back_call(
        place, middle, late_joint, late_probs, grad_mixed
    )

    got, next_sent, grad_joint = sync(got, next_sent, grad_joint)
    late_stacks = core_sum(kept, got)
    late_stacks, next_sent, grad_joint = sync(late_stacks, next_sent, grad_joint)
    late_got = square_back(late_stacks)
    got = swap(next_sent, CORE)
    grad_mixed, grad_one, kept, sent = dense_back_call(
        place, grad_one, grad_joint, late_weight, mixed, dense_kept
    )

    got, late_got, sent, grad_mixed = sync(got, late_got, sent, grad_mixed)
    first_stacks = core_sum(next_kept, got)
    late_kept, late_sent = square_sum_call([late_stacks[0], *late_got])
    first_stacks, late_kept, late_sent, sent, grad_mixed = sync(
        first_stacks, late_kept, late_sent, sent, grad_mixed
    )
    first_got = square_back(first_stacks)
    got = swap(sent, CORE)
    late_got = swap(late_sent, CHAIN[2])
    before = attend_back_call(place, x, joint, probs, grad_mixed, 0, pair)

    got, first_got, late_got, before = sync(got, first_got, late_got, before)
    second_stacks = core_sum(kept, got)
    late_own, late_sent = pair_sum(late_kept, late_got)
    second_stacks, before, late_sent = sync(second_stacks, before, late_sent)
    second_got = square_back(second_stacks)
    late_got = swap(late_sent, CHAIN[1])
    kept, sent, grad_joint = attend_back_call(
        place, x, joint, probs, grad_mixed, pair, HEADS - pair, before
    )

    second_got, sent, grad_joint, late_got = sync(second_got, sent, grad_joint, late_got)
    got = swap(sent, CORE)
    middle_kept, middle_sent = square_sum_call(
        [first_stacks[0], *first_got], [second_stacks[0], *second_got]
    )
    got, middle_sent = sync(got, middle_sent)
    stacks = core_sum(kept, got)
    stacks, middle_sent, grad_joint = sync(stacks, middle_sent, grad_joint)
    got = square_back(stacks)
    middle_got = swap(middle_sent, CHAIN[2])
    grad_rows = grad_x_call(grad_one, grad_joint, weight)

    middle_got, grad_rows = sync(middle_got, grad_rows)
    middle_own, middle_sent = pair_sum(middle_kept, middle_got)
    middle_got = swap(middle_sent, CHAIN[1])

    def state_of(*which):
        return [item for at in which for item in (masters[at], moments[at], averages[at])]

    last_blocks = square_sum_call([stacks[0], *got], halves=False)
    last_got = chain_back(last_blocks)
    *stepped, late_first, small = step_call(
        second_step_kernel,
        [rates],
        [middle_own, middle_got, late_own, late_got, *state_of(1, 2, 3)],
        [*step_shapes(masters[1:4]), LIKE((FIRST_ROWS, width), FLOAT),
         LIKE((2, 8, width), FLOAT)],
        "second_step",
    )
    rest = step_call(
        first_step_kernel,
        [place, rates],
        [small, late_first, last_blocks[0], *last_got, *state_of(0, 4, 5)],
        step_shapes((masters[0], masters[4], masters[5])),
        "first_step",
    )
    return (result, grad_rows, *rest[:4], *stepped, *rest[4:])


def shards(
    tokens,
    cotangent,
    dataset_ids,
    query_counts,
    learn_rate,
    momentum_coef,
    average_decay,
    step_count,
    *state,
):
    masters, moments, averages = state[0::3], state[1::3], state[2::3]
    position = lax.axis_index(AXES)
    direct = lax.axis_size(AXES) == OWNERS
    place = (position if direct else jnp.zeros_like(position)).astype(jnp.int32).reshape(1)
    step_value = step_count[0].astype(FLOAT)
    decay_now = average_decay[0] * (1.0 + step_value) / (4.0 + step_value)
    rates = jnp.stack([momentum_coef[0], learn_rate[0], decay_now])
    run = one_per_owner if direct else any_size
    result, grad_rows, *outputs = run(
        place, tokens[0], cotangent[0], dataset_ids, query_counts + CTX, masters, moments, averages,
        rates,
    )
    return (result[None], grad_rows[None], *outputs)


def solution(mesh):
    rows = P(AXES, None, None)
    weight = P(None, AXES, None)
    vector = P(None, None, AXES)
    scalar = P()
    return jax.shard_map(
        shards,
        mesh=mesh,
        in_specs=(rows, rows, P(AXES), P(AXES), *[scalar] * 4, *[weight] * 12, *[vector] * 6),
        out_specs=(rows, rows, *[weight] * 16, *[vector] * 8),
        check_vma=False,
    )
```

```python
import functools

import jax
import jax.numpy as jnp
import numpy as np
from jax import lax
from jax.experimental import pallas as pl
from jax.experimental.pallas import tpu as pltpu
from jax.sharding import PartitionSpec as P

HEADS = 4
CTX = 896
NDS = 8
EPS = 1e-05
OWNERS = 32
AXES = ("dp", "fsdp")

CHAIN = (0, 4, 2, 6)
SQUARE = (0, 1, 16, 17)
CORE = 8
ORDER = tuple(core ^ side ^ link for core in (0, CORE) for side in SQUARE for link in CHAIN)

FIRST_ROWS = 56
SECOND_ROWS = 88

ROW_BLOCK = 512
BACK_BLOCK = 256
ROOT_HALF = 0.7071067811865476
PDF_PEAK = 0.3989422804014327
VMEM_LIMIT = 60 * 1024 * 1024
SMALL_LIMIT = 12 * 1024 * 1024
FLOAT = jnp.float32
HALF = jnp.bfloat16
LIKE = jax.ShapeDtypeStruct


def product(left, right, left_dim, right_dim):
    return lax.dot_general(
        left, right, (((left_dim,), (right_dim,)), ((), ())), preferred_element_type=FLOAT
    )


def owner_rows(offset, place, rows):
    return pl.ds(pl.multiple_of((offset ^ place) * rows, rows), rows)


def params(limit=VMEM_LIMIT):
    return pltpu.CompilerParams(vmem_limit_bytes=limit)


def pack_kernel(place_ref, ids_ref, attend_ref, output_ref, expand_ref, shrink_ref, gains_ref,
                bias_ref, *outs):
    *outs, small = outs
    width = small.shape[1]
    each = gains_ref.shape[2]
    lane = lax.broadcasted_iota(jnp.int32, (each, width), 1)
    own = lax.broadcasted_iota(jnp.int32, (each, width), 0) + place_ref[0] * each
    pick = (lane == own).astype(HALF)
    lanes = lax.broadcasted_iota(jnp.int32, (1, width), 1)

    for layer in range(attend_ref.shape[0]):
        first, top, second = (outs[0], 0, outs[1]) if layer == 0 else (outs[1], SECOND_ROWS, outs[2])
        gains = product(gains_ref[layer].astype(HALF), pick, 1, 0)
        biases = product(bias_ref[layer].astype(HALF), pick, 1, 0)
        for piece in range(3):
            first[top + piece * 16 : top + (piece + 1) * 16, :] = attend_ref[
                layer, :, piece * width : (piece + 1) * width
            ].astype(HALF)
        small[...] = jnp.zeros_like(small)
        small[0:2, :] = biases[0:2, :]
        small[2:3, :] = (lanes == ids_ref[0]).astype(FLOAT)
        first[top + 48 : top + 56, :] = small[...].astype(HALF)
        second[0:16, :] = output_ref[layer].astype(HALF)
        for piece in range(2):
            second[(piece + 1) * 16 : (piece + 2) * 16, :] = expand_ref[
                layer, :, piece * width : (piece + 1) * width
            ].astype(HALF)
        second[48:80, :] = shrink_ref[layer].astype(HALF)
        small[0:2, :] = gains
        small[2:8, :] = biases[2:8, :]
        second[80:88, :] = small[...].astype(HALF)


def pack_call(place, ids, masters):
    width = masters[1].shape[2]
    rows = (FIRST_ROWS, SECOND_ROWS + FIRST_ROWS, SECOND_ROWS)
    return pl.pallas_call(
        pack_kernel,
        in_specs=[pl.BlockSpec(memory_space=pltpu.SMEM)] * 2
        + [pl.BlockSpec(memory_space=pltpu.VMEM)] * 6,
        out_specs=[pl.BlockSpec(memory_space=pltpu.VMEM)] * len(rows),
        out_shape=[LIKE((count, width), HALF) for count in rows],
        scratch_shapes=[pltpu.VMEM((8, width), FLOAT)],
        compiler_params=params(),
        cost_estimate=pl.CostEstimate(flops=0, bytes_accessed=1 << 20, transcendentals=0),
        name="pack",
    )(place, ids, *masters)


def join_kernel(cuts, count, *refs):
    each = refs[count].shape[0] // count
    for at in range(count):
        for to, (start, rows) in enumerate(cuts):
            target = refs[count + to]
            if len(refs[at].shape) == 2:
                target[at] = refs[at][start : start + rows, :]
            else:
                target[at * each : (at + 1) * each] = refs[at][:, start : start + rows, :]


def join_call(blocks, *cuts):
    *head, rows, width = blocks[0].shape
    slots = len(blocks) * (head[0] if head else 1)
    cuts = cuts or ((0, rows),)
    return pl.pallas_call(
        functools.partial(join_kernel, cuts, len(blocks)),
        out_shape=[LIKE((slots, rows, width), HALF) for _, rows in cuts],
        compiler_params=params(SMALL_LIMIT),
        cost_estimate=pl.CostEstimate(flops=0, bytes_accessed=1 << 20, transcendentals=0),
        name="join",
    )(*blocks)


def block_sum(refs):
    total = refs[0][...].astype(FLOAT)
    for ref in refs[1:]:
        total = total + ref[...].astype(FLOAT)
    return total


def core_sum(kept, got):
    return [
        (kept[at : at + 4].astype(FLOAT) + got[at : at + 4].astype(FLOAT)).astype(HALF)
        for at in range(0, 16, 4)
    ]


def square_sum_kernel(rows, *refs):
    outs = refs[4 * len(rows) :]
    start = 0
    for at, count in enumerate(rows):
        total = block_sum(refs[4 * at : 4 * at + 4]).astype(HALF)
        for to in range(4):
            each = 4 // len(outs)
            if each == 1:
                outs[to][start : start + count, :] = total[to]
            else:
                outs[to // each][to % each, start : start + count, :] = total[to]
        start += count


def square_sum_call(*pieces, halves=True):
    rows = tuple(stacks[0].shape[1] for stacks in pieces)
    shape = (sum(rows), pieces[0][0].shape[2])
    return pl.pallas_call(
        functools.partial(square_sum_kernel, rows),
        out_shape=[LIKE((2, *shape), HALF)] * 2 if halves else [LIKE(shape, HALF)] * 4,
        compiler_params=params(SMALL_LIMIT),
        cost_estimate=pl.CostEstimate(flops=0, bytes_accessed=1 << 21, transcendentals=0),
        name="square_sum",
    )(*[stack for stacks in pieces for stack in stacks])


def pair_sum(kept, got):
    return [(kept[at].astype(FLOAT) + got[at].astype(FLOAT)).astype(HALF) for at in range(2)]


def swap(block, offset):
    return lax.ppermute(block, AXES, [(one, one ^ offset) for one in range(OWNERS)])


def swaps(block, offsets):
    return [swap(block, offset) for offset in offsets]


def slot_places(slot_refs):
    for at, offset in enumerate(ORDER):
        yield slot_refs[at // 4], at % 4, offset


def small_rows(slot_refs, start):
    total = None
    for slots in slot_refs:
        for at in range(slots.shape[0]):
            block = slots[at, start : start + 8, :].astype(FLOAT)
            total = block if total is None else total + block
    return total


def attend_kernel(place_ref, x_ref, *refs):
    slot_refs = refs[:8]
    joint_ref, probs_ref, mixed_ref, weight_ref, small_ref = refs[8:]
    count = joint_ref.shape[0]
    head_size = joint_ref.shape[2] // 3
    place = place_ref[0]

    for slots, at, offset in slot_places(slot_refs):
        rows = owner_rows(offset, place, 16)
        for piece in range(3):
            for head in range(count):
                weight_ref[head, rows, piece * head_size : (piece + 1) * head_size] = slots[
                    at, piece * 16 : (piece + 1) * 16, head * head_size : (head + 1) * head_size
                ]
    zeros = jnp.zeros((1, head_size), FLOAT)
    small = small_rows(slot_refs, 48)
    small_ref[...] = small
    factor = head_size ** (-0.5) * 1.4426950408889634
    weights = jnp.concatenate([weight_ref[head] for head in range(count)], axis=1)
    wide = product(x_ref[...], weights, 1, 0)
    for head in range(count):
        own = slice(head * head_size, (head + 1) * head_size)
        shift = jnp.concatenate([small[0:1, own], zeros, small[1:2, own]], axis=1)
        part = wide[:, 3 * head * head_size : 3 * (head + 1) * head_size]
        joint_ref[head] = (part + shift).astype(HALF)
    scores = []
    for head in range(count):
        keys = joint_ref[head, :CTX, head_size : 2 * head_size]
        scores.append(product(keys, joint_ref[head, :, :head_size], 1, 1))
    for head in range(count):
        values_turned = jnp.transpose(joint_ref[head, :CTX, 2 * head_size :])
        top = jnp.max(scores[head], axis=0, keepdims=True)
        grown = jnp.exp2((scores[head] - top) * factor)
        total = jnp.sum(grown, axis=0, keepdims=True)
        probs = (grown * (1.0 / total)).astype(HALF)
        probs_ref[head] = probs
        mixed_ref[:, head * head_size : (head + 1) * head_size] = jnp.transpose(
            product(values_turned, probs, 1, 0)
        ).astype(HALF)


def attend_call(place, x, slots):
    rows, width = x.shape
    head_size = width // HEADS
    return pl.pallas_call(
        attend_kernel,
        grid_spec=pltpu.PrefetchScalarGridSpec(
            num_scalar_prefetch=1,
            grid=(HEADS // 2,),
            in_specs=[pl.BlockSpec((rows, width), lambda h, p: (0, 0))]
            + [pl.BlockSpec((part.shape[0], FIRST_ROWS, 2 * head_size), lambda h, p: (0, 0, h))
               for part in slots],
            out_specs=[
                pl.BlockSpec((2, rows, 3 * head_size), lambda h, p: (h, 0, 0)),
                pl.BlockSpec((2, CTX, rows), lambda h, p: (h, 0, 0)),
                pl.BlockSpec((rows, 2 * head_size), lambda h, p: (0, h)),
                pl.BlockSpec((2, width, 3 * head_size), lambda h, p: (h, 0, 0)),
                pl.BlockSpec((8, 2 * head_size), lambda h, p: (0, h)),
            ],
        ),
        out_shape=[
            LIKE((HEADS, rows, 3 * head_size), HALF),
            LIKE((HEADS, CTX, rows), HALF),
            LIKE((rows, HEADS * head_size), HALF),
            LIKE((HEADS, width, 3 * head_size), HALF),
            LIKE((8, width), FLOAT),
        ],
        compiler_params=params(),
        cost_estimate=pl.CostEstimate(
            flops=HEADS * (2 * rows * width * 3 * head_size + 4 * rows * CTX * head_size),
            bytes_accessed=HEADS * 4 * 1024 * 1024,
            transcendentals=HEADS * rows * CTX,
        ),
        name="attend",
    )(place, x, *slots)


def unpack_second(place, slot_refs, output_w, expand_w, shrink_w, vec_ref):
    width = output_w.shape[1]
    for slots, at, offset in slot_places(slot_refs):
        rows = owner_rows(offset, place, 16)
        output_w[rows, :] = slots[at, 0:16, :]
        expand_w[rows, :width] = slots[at, 16:32, :]
        expand_w[rows, width:] = slots[at, 32:48, :]
        shrink_w[owner_rows(offset, place, 32), :] = slots[at, 48:80, :]
    vec_ref[...] = small_rows(slot_refs, 80)


def row_mean(rows):
    return jnp.mean(rows, axis=-1, keepdims=True)


def normalize(rows):
    centred = rows - row_mean(rows)
    inv_std = lax.rsqrt(row_mean(centred * centred) + EPS)
    return (centred * inv_std, inv_std)


def forward_rows(x_ref, mixed_ref, vec_ref, output_w, expand_w, shrink_w):
    attn_out = product(mixed_ref[...], output_w[...], 1, 0) + vec_ref[2:3, :]
    unit_one, inv_one = normalize(x_ref[...].astype(FLOAT) + attn_out)
    first_norm = unit_one * vec_ref[0:1, :] + vec_ref[4:5, :]
    first_low = first_norm.astype(HALF)
    shift = jnp.concatenate([vec_ref[6:7, :], vec_ref[7:8, :]], axis=1)
    hidden = product(first_low, expand_w[...], 1, 0) + shift
    normal_cdf = 0.5 * (1.0 + lax.erf(hidden * ROOT_HALF))
    act_low = (hidden * normal_cdf).astype(HALF)
    slope = normal_cdf + hidden * (jnp.exp(-0.5 * hidden * hidden) * PDF_PEAK)
    branch = product(act_low, shrink_w[...], 1, 0) + vec_ref[3:4, :]
    unit_two, inv_two = normalize(first_norm + branch)
    result = unit_two * vec_ref[1:2, :] + vec_ref[5:6, :]
    return (unit_one, inv_one, first_low, act_low, slope, unit_two, inv_two, result)


def column_sum(rows):
    return jnp.sum(rows, axis=0, keepdims=True)


def backward_rows(grad_rows, mixed_ref, vec_ref, kept, output_w, expand_w, shrink_w,
                  grad_mixed_ref, grad_one_ref, grad_output, grad_expand, grad_shrink, sums):
    unit_one, inv_one, first_low, act_low, slope, unit_two, inv_two = kept
    width = grad_rows.shape[1]

    def layer_norm_back(rows, unit_rows, inv_std, gain):
        scaled = rows * gain
        return inv_std * (scaled - row_mean(scaled) - unit_rows * row_mean(scaled * unit_rows))

    grad_two = layer_norm_back(grad_rows, unit_two, inv_two, vec_ref[1:2, :])
    branch_low = grad_two.astype(HALF)
    grad_shrink[...] += product(act_low, branch_low, 0, 0)
    grad_hidden = (product(branch_low, shrink_w[...], 1, 1) * slope).astype(HALF)
    grad_expand[...] += product(first_low, grad_hidden, 0, 0)
    grad_first = grad_two + product(grad_hidden, expand_w[...], 1, 1)
    grad_one = layer_norm_back(grad_first, unit_one, inv_one, vec_ref[0:1, :])
    attn_low = grad_one.astype(HALF)
    grad_output[...] += product(mixed_ref[...], attn_low, 0, 0)
    grad_mixed_ref[...] = product(attn_low, output_w[...], 1, 1).astype(HALF)
    grad_one_ref[...] = grad_one
    sums[0:1, :] += column_sum(grad_first * unit_one)
    sums[1:2, :] += column_sum(grad_rows * unit_two)
    sums[2:3, :] += column_sum(attn_low.astype(FLOAT))
    sums[3:4, :] += column_sum(branch_low.astype(FLOAT))
    sums[4:5, :] += column_sum(grad_first)
    sums[5:6, :] += column_sum(grad_rows)
    hidden_sum = column_sum(grad_hidden.astype(FLOAT))
    sums[6:7, :] += hidden_sum[:, :width]
    sums[7:8, :] += hidden_sum[:, width:]


def pack_second(place, kept_ref, sent_ref, grad_output, grad_expand, grad_shrink, sums):
    width = grad_output.shape[1]
    small = sums[...].astype(HALF)
    for at, offset in enumerate(ORDER):
        slots_ref = kept_ref if at < 16 else sent_ref
        at = at % 16
        rows = owner_rows(offset, place, 16)
        slots_ref[at, 0:16, :] = grad_output[rows, :].astype(HALF)
        slots_ref[at, 16:32, :] = grad_expand[rows, :width].astype(HALF)
        slots_ref[at, 32:48, :] = grad_expand[rows, width:].astype(HALF)
        slots_ref[at, 48:80, :] = grad_shrink[owner_rows(offset, place, 32), :].astype(HALF)
        slots_ref[at, 80:88, :] = small


def dense_kernel(place_ref, x_ref, mixed_ref, *refs):
    slot_refs = refs[:8]
    (result_ref, unit_one_ref, inv_one_ref, act_ref, slope_ref, unit_two_ref, inv_two_ref, output_w,
     expand_w, shrink_w, vec_ref) = refs[8:]

    @pl.when(pl.program_id(0) == 0)
    def _():
        unpack_second(place_ref[0], slot_refs, output_w, expand_w, shrink_w, vec_ref)

    unit_one, inv_one, _, act_low, slope, unit_two, inv_two, result = forward_rows(
        x_ref, mixed_ref, vec_ref, output_w, expand_w, shrink_w
    )
    result_ref[...] = result.astype(HALF)
    unit_one_ref[...] = unit_one
    inv_one_ref[...] = inv_one
    act_ref[...] = act_low
    slope_ref[...] = slope
    unit_two_ref[...] = unit_two
    inv_two_ref[...] = inv_two


def grad_x_rows(grad_one_ref, grad_joint_ref, weight_ref):
    total = grad_one_ref[...]
    for head in range(weight_ref.shape[0]):
        total = total + product(grad_joint_ref[head], weight_ref[head], 1, 1)
    return total


def clear(*items):
    for item in items:
        item[...] = jnp.zeros_like(item)


def dense_back_kernel(place_ref, grad_one_next, grad_joint_next, weight_next, mixed_ref, *refs):
    (unit_one_ref, inv_one_ref, act_ref, slope_ref, unit_two_ref, inv_two_ref, output_w, expand_w,
     shrink_w, vec_ref, grad_mixed_ref, grad_one_ref, kept_ref, sent_ref, sums, grad_output,
     grad_expand, grad_shrink) = refs

    @pl.when(pl.program_id(0) == 0)
    def _():
        clear(sums, grad_output, grad_expand, grad_shrink)

    unit_one = unit_one_ref[...]
    first_low = (unit_one * vec_ref[0:1, :] + vec_ref[4:5, :]).astype(HALF)
    kept = (unit_one, inv_one_ref[...], first_low, act_ref[...], slope_ref[...], unit_two_ref[...],
            inv_two_ref[...])
    grad_rows = grad_x_rows(grad_one_next, grad_joint_next, weight_next)
    backward_rows(grad_rows, mixed_ref, vec_ref, kept, output_w, expand_w, shrink_w,
                  grad_mixed_ref, grad_one_ref, grad_output, grad_expand, grad_shrink, sums)

    @pl.when(pl.program_id(0) == pl.num_programs(0) - 1)
    def _():
        pack_second(place_ref[0], kept_ref, sent_ref, grad_output, grad_expand, grad_shrink, sums)


def dense_turn_kernel(place_ref, live_ref, ids_ref, x_ref, mixed_ref, *refs):
    slot_refs = refs[:8]
    (counts_ref, cot_ref, result_ref, grad_mixed_ref, grad_one_ref, kept_ref, sent_ref, output_w, expand_w,
     shrink_w, vec_ref, grad_output, grad_expand, grad_shrink, sums) = refs[8:]
    step = pl.program_id(0)

    @pl.when(step == 0)
    def _():
        unpack_second(place_ref[0], slot_refs, output_w, expand_w, shrink_w, vec_ref)
        clear(sums, grad_output, grad_expand, grad_shrink)

    *kept, result = forward_rows(x_ref, mixed_ref, vec_ref, output_w, expand_w, shrink_w)
    result_ref[...] = result.astype(HALF)
    counts = counts_ref[2:3, :]
    lanes = lax.broadcasted_iota(jnp.int32, counts.shape, 1)
    own_count = jnp.sum(jnp.where(lanes == ids_ref[0], counts, 0.0), axis=1, keepdims=True)
    row_weight = jnp.sum(counts, axis=1, keepdims=True) / (NDS * own_count)
    rows = cot_ref.shape[0]
    slot = lax.broadcasted_iota(jnp.int32, (rows, 1), 0) + step * rows
    grad_rows = cot_ref[...].astype(FLOAT) * jnp.where(slot < live_ref[0], row_weight, 0.0)
    backward_rows(grad_rows, mixed_ref, vec_ref, kept, output_w, expand_w, shrink_w,
                  grad_mixed_ref, grad_one_ref, grad_output, grad_expand, grad_shrink, sums)

    @pl.when(step == pl.num_programs(0) - 1)
    def _():
        pack_second(place_ref[0], kept_ref, sent_ref, grad_output, grad_expand, grad_shrink, sums)


def by_rows(width, block=ROW_BLOCK):
    return pl.BlockSpec((block, width), lambda i, *p: (i, 0))


def fixed(*shape):
    return pl.BlockSpec(shape, lambda i, *p: (0,) * len(shape))


def joint_rows(grad_joint, block=ROW_BLOCK):
    heads, _, width = grad_joint.shape
    return pl.BlockSpec((heads, block, width), lambda i, *p: (0, i, 0))


def weight_shapes(width):
    return [(width, width), (width, 2 * width), (2 * width, width)]


def dense_call(place, x, mixed, slots):
    rows, width = x.shape
    weights = weight_shapes(width)
    return pl.pallas_call(
        dense_kernel,
        grid_spec=pltpu.PrefetchScalarGridSpec(
            num_scalar_prefetch=1,
            grid=(rows // ROW_BLOCK,),
            in_specs=[by_rows(width)] * 2
            + [fixed(*part.shape) for part in slots],
            out_specs=[by_rows(width), by_rows(width), by_rows(1), by_rows(2 * width),
                       by_rows(2 * width), by_rows(width), by_rows(1)]
            + [fixed(*shape) for shape in weights]
            + [fixed(8, width)],
        ),
        out_shape=[LIKE((rows, width), HALF), LIKE((rows, width), FLOAT), LIKE((rows, 1), FLOAT),
                   LIKE((rows, 2 * width), HALF), LIKE((rows, 2 * width), FLOAT),
                   LIKE((rows, width), FLOAT), LIKE((rows, 1), FLOAT)]
        + [LIKE(shape, HALF) for shape in weights]
        + [LIKE((8, width), FLOAT)],
        compiler_params=params(),
        cost_estimate=pl.CostEstimate(
            flops=10 * rows * width * width, bytes_accessed=16 * 1024 * 1024,
            transcendentals=4 * rows * width,
        ),
        name="dense",
    )(place, x, mixed, *slots)


def dense_back_call(place, grad_one, grad_joint, weight, mixed, kept):
    rows, width = grad_one.shape
    weights = weight_shapes(width)
    some_rows = functools.partial(by_rows, block=BACK_BLOCK)
    return pl.pallas_call(
        dense_back_kernel,
        grid_spec=pltpu.PrefetchScalarGridSpec(
            num_scalar_prefetch=1,
            grid=(rows // BACK_BLOCK,),
            in_specs=[some_rows(width), joint_rows(grad_joint, BACK_BLOCK), fixed(*weight.shape), some_rows(width)]
            + [some_rows(width), some_rows(1), some_rows(2 * width), some_rows(2 * width), some_rows(width),
               some_rows(1)]
            + [fixed(*shape) for shape in weights]
            + [fixed(8, width)],
            out_specs=[some_rows(width), some_rows(width)] + [fixed(16, SECOND_ROWS, width)] * 2,
            scratch_shapes=[pltpu.VMEM((8, width), FLOAT)]
            + [pltpu.VMEM(shape, FLOAT) for shape in weights],
        ),
        out_shape=[LIKE((rows, width), HALF), LIKE((rows, width), FLOAT)]
        + [LIKE((16, SECOND_ROWS, width), HALF)] * 2,
        compiler_params=params(),
        cost_estimate=pl.CostEstimate(
            flops=26 * rows * width * width, bytes_accessed=20 * 1024 * 1024, transcendentals=0
        ),
        name="dense_back",
    )(place, grad_one, grad_joint, weight, mixed, *kept)


def dense_turn_call(place, live, ids, x, mixed, slots, small, cotangent):
    rows, width = x.shape
    weights = weight_shapes(width)
    return pl.pallas_call(
        dense_turn_kernel,
        grid_spec=pltpu.PrefetchScalarGridSpec(
            num_scalar_prefetch=3,
            grid=(rows // ROW_BLOCK,),
            in_specs=[by_rows(width)] * 2
            + [fixed(*part.shape) for part in slots]
            + [fixed(8, width), by_rows(width)],
            out_specs=[by_rows(width)] * 3 + [fixed(16, SECOND_ROWS, width)] * 2,
            scratch_shapes=[pltpu.VMEM(shape, HALF) for shape in weights]
            + [pltpu.VMEM((8, width), FLOAT)]
            + [pltpu.VMEM(shape, FLOAT) for shape in weights]
            + [pltpu.VMEM((8, width), FLOAT)],
        ),
        out_shape=[LIKE((rows, width), HALF), LIKE((rows, width), HALF), LIKE((rows, width), FLOAT)]
        + [LIKE((16, SECOND_ROWS, width), HALF)] * 2,
        compiler_params=params(),
        cost_estimate=pl.CostEstimate(
            flops=30 * rows * width * width, bytes_accessed=16 * 1024 * 1024,
            transcendentals=4 * rows * width,
        ),
        name="dense_turn",
    )(place, live, ids, x, mixed, *slots, small, cotangent)


def attend_back_kernel(place_ref, x_ref, joint_ref, probs_ref, grad_mixed_ref, *refs):
    kept_ref, sent_ref, grad_joint_ref, grad_scores, small = refs[-5:]
    grad_joint = grad_joint_ref.at[0]
    rows = x_ref.shape[0]
    head_size = grad_mixed_ref.shape[1]
    place = place_ref[0]

    @pl.when(pl.program_id(0) == 0)
    def _():
        clear(small)

    grad_joint[CTX:, head_size:] = jnp.zeros((rows - CTX, 2 * head_size), HALF)
    keys = joint_ref[0, :CTX, head_size : 2 * head_size]
    values = joint_ref[0, :CTX, 2 * head_size :]
    keys_turned = jnp.transpose(keys)
    factor = head_size ** (-0.5)
    grad_probs = product(values, grad_mixed_ref[...], 1, 1)
    probs = probs_ref[0].astype(FLOAT)
    level = column_sum(probs * grad_probs)
    grad_low = (probs * (grad_probs - level)).astype(HALF)
    grad_scores[...] = grad_low
    grad_joint[:, :head_size] = jnp.transpose(factor * product(keys_turned, grad_low, 1, 0)).astype(
        HALF
    )
    grad_joint[:CTX, head_size : 2 * head_size] = (
        factor * product(grad_scores[...], joint_ref[0, :, :head_size], 1, 0)
    ).astype(HALF)
    grad_joint[:CTX, 2 * head_size :] = product(probs_ref[0], grad_mixed_ref[...], 1, 0).astype(HALF)
    sums = column_sum(grad_joint[...].astype(FLOAT))
    small[0:1, :] = sums[:, :head_size]
    small[1:2, :] = sums[:, 2 * head_size :]
    small_low = small[...].astype(HALF)
    grad_low = product(x_ref[...], grad_joint[...], 0, 0).astype(HALF)
    holder = grad_scores
    holder[: grad_low.shape[0], : 3 * head_size] = grad_low
    for at, offset in enumerate(ORDER):
        slots_ref = kept_ref if at < 16 else sent_ref
        at = at % 16
        span = owner_rows(offset, place, 16)
        for piece in range(3):
            slots_ref[at, piece * 16 : (piece + 1) * 16, :] = holder[
                span, piece * head_size : (piece + 1) * head_size
            ]
        slots_ref[at, 48:56, :] = small_low


def attend_back_call(place, x, joint, probs, grad_mixed, base=0, heads=HEADS, before=()):
    rows, width = x.shape
    head_size = width // HEADS
    return pl.pallas_call(
        attend_back_kernel,
        grid_spec=pltpu.PrefetchScalarGridSpec(
            num_scalar_prefetch=1,
            grid=(heads,),
            in_specs=[
                pl.BlockSpec((rows, width), lambda h, p: (0, 0)),
                pl.BlockSpec((1, rows, 3 * head_size), lambda h, p: (h + base, 0, 0)),
                pl.BlockSpec((1, CTX, rows), lambda h, p: (h + base, 0, 0)),
                pl.BlockSpec((rows, head_size), lambda h, p: (0, h + base)),
            ]
            + [pl.BlockSpec(memory_space=pl.ANY)] * len(before),
            out_specs=[pl.BlockSpec((16, FIRST_ROWS, head_size), lambda h, p: (0, 0, h + base))] * 2
            + [pl.BlockSpec((1, rows, 3 * head_size), lambda h, p: (h + base, 0, 0))],
            scratch_shapes=[pltpu.VMEM((CTX, rows), HALF), pltpu.VMEM((8, head_size), FLOAT)],
        ),
        out_shape=[LIKE((16, FIRST_ROWS, width), HALF)] * 2
        + [LIKE((HEADS, rows, 3 * head_size), HALF)],
        input_output_aliases={5 + at: at for at in range(len(before))},
        compiler_params=params(),
        cost_estimate=pl.CostEstimate(
            flops=heads * (6 * rows * width * head_size + 8 * rows * CTX * head_size),
            bytes_accessed=heads * 4 * 1024 * 1024, transcendentals=0,
        ),
        name="attend_back",
    )(place, x, joint, probs, grad_mixed, *before)


def grad_x_kernel(grad_one_ref, grad_joint_ref, weight_ref, grad_x_ref):
    grad_x_ref[...] = grad_x_rows(grad_one_ref, grad_joint_ref, weight_ref)


def grad_x_call(grad_one, grad_joint, weight):
    rows, width = grad_one.shape
    return pl.pallas_call(
        grad_x_kernel,
        grid=(rows // ROW_BLOCK,),
        in_specs=[
            by_rows(width),
            joint_rows(grad_joint),
            fixed(*weight.shape),
        ],
        out_specs=by_rows(width),
        out_shape=LIKE((rows, width), FLOAT),
        compiler_params=params(),
        cost_estimate=pl.CostEstimate(
            flops=6 * rows * width * width, bytes_accessed=10 * 1024 * 1024, transcendentals=0
        ),
        name="grad_x",
    )(grad_one, grad_joint, weight)


def advance(master, moment, average, grad, momentum, step_rate, decay_now):
    new_moment = momentum * moment + grad
    new_master = master - step_rate * (grad + momentum * new_moment)
    new_average = decay_now * average + (1.0 - decay_now) * new_master
    return (new_moment, new_average, new_master, new_master.astype(HALF))


def stepper(rates_ref, state_refs, out_refs):
    rates = [rates_ref[at] for at in range(3)]

    def step(weight, where, grad):
        state = [ref[where] for ref in state_refs[3 * weight : 3 * weight + 3]]
        for ref, item in zip(out_refs[4 * weight : 4 * weight + 4], advance(*state, grad, *rates)):
            ref[where] = item

    return step


def second_step_kernel(rates_ref, *refs):
    middle, late = block_sum(refs[:2]), block_sum(refs[2:4])
    state_refs, out_refs, (first_ref, small_ref) = refs[4:13], refs[13:25], refs[25:]
    width = small_ref.shape[2]
    step = stepper(rates_ref, state_refs, out_refs)
    for layer, piece in enumerate((middle[FIRST_ROWS:], late)):
        step(0, (layer,), piece[0:16])
        step(1, (layer, slice(None), slice(0, width)), piece[16:32])
        step(1, (layer, slice(None), slice(width, 2 * width)), piece[32:48])
        step(2, (layer,), piece[48:80])
        small_ref[layer] = piece[80:88]
    first_ref[...] = middle[:FIRST_ROWS]


def step_shapes(masters):
    return [
        LIKE(master.shape, kind) for master in masters for kind in (FLOAT, FLOAT, FLOAT, HALF)
    ]


def step_call(kernel, rates, inputs, out_shape, name):
    return pl.pallas_call(
        kernel,
        in_specs=[pl.BlockSpec(memory_space=pltpu.SMEM)] * len(rates)
        + [pl.BlockSpec(memory_space=pltpu.VMEM)] * len(inputs),
        out_specs=[pl.BlockSpec(memory_space=pltpu.VMEM)] * len(out_shape),
        out_shape=out_shape,
        compiler_params=params(SMALL_LIMIT),
        cost_estimate=pl.CostEstimate(flops=0, bytes_accessed=1 << 22, transcendentals=0),
        name=name,
    )(*rates, *inputs)


def first_step_kernel(place_ref, rates_ref, small_ref, late_ref, *refs):
    blocks, state_refs, out_refs = refs[:4], refs[4:13], refs[13:]
    width = small_ref.shape[2]
    each = out_refs[4].shape[2]
    step = stepper(rates_ref, state_refs, out_refs)
    turn = width - place_ref[0] * each
    for layer, total in enumerate((block_sum(blocks), late_ref[...])):
        for piece in range(3):
            columns = slice(piece * width, (piece + 1) * width)
            step(0, (layer, slice(None), columns), total[piece * 16 : (piece + 1) * 16])
        own_first = pltpu.roll(total[48:56], turn, 1)[:, :each]
        own_second = pltpu.roll(small_ref[layer], turn, 1)[:, :each]
        step(1, (layer,), own_second[0:2])
        step(2, (layer, slice(0, 2)), own_first[0:2])
        step(2, (layer, slice(2, 8)), own_second[2:8])


def wide_to_rows(shard, width):
    return jnp.concatenate(
        [shard[:, at * width : (at + 1) * width] for at in range(shard.shape[1] // width)]
    )


def rows_to_wide(rows, pieces):
    each = rows.shape[0] // pieces
    return jnp.concatenate([rows[at * each : (at + 1) * each] for at in range(pieces)], axis=1)


def gather_rows(shards_by_part, small):
    width = small.shape[1]
    parts = []
    for shard in shards_by_part:
        whole = lax.all_gather(shard, AXES, axis=0, tiled=False)
        parts.append(whole.reshape(OWNERS, -1, width))
    smalls = jnp.broadcast_to(small[None] * (jnp.arange(OWNERS) == 0)[:, None, None].astype(HALF),
                              (OWNERS, *small.shape))
    slots = jnp.concatenate([*parts, smalls], axis=1)[np.array(ORDER)]
    return [slots[4 * at : 4 * at + 4] for at in range(8)]


def scatter_rows(kept, sent, parts):
    slots = jnp.concatenate([kept, sent])[np.argsort(np.array(ORDER))]
    everyone = lax.axis_size(AXES)
    own, start = [], 0
    for rows in parts:
        piece = slots[:, start : start + rows].reshape(everyone, -1, slots.shape[2])
        own.append(lax.psum_scatter(piece, AXES, scatter_dimension=0, tiled=False).astype(FLOAT))
        start += rows
    return own, lax.psum(slots[0, start:].astype(FLOAT), AXES)


def sync(*items):
    return lax.optimization_barrier(items)


def any_size(place, x, cotangent, dataset_ids, live, masters, moments, averages, rates):
    layers = masters[0].shape[0]
    width = x.shape[1]
    position = lax.axis_index(AXES)
    low = lambda item: item.astype(HALF)
    own = low(jnp.concatenate([masters[4], masters[5]], axis=1))
    wide = lax.all_gather(own, AXES, axis=2, tiled=True)
    onehot = (dataset_ids[0] == jnp.arange(width, dtype=jnp.int32)).astype(FLOAT)
    counts = low(lax.psum(onehot, AXES))[None]
    first, second = [], []
    for at in range(layers):
        pad = lambda rows: jnp.pad(rows, ((0, 8 - rows.shape[0]), (0, 0)))
        attend_w = masters[0][at]
        first.append(gather_rows(
            [low(attend_w[:, piece * width : (piece + 1) * width]) for piece in range(3)],
            pad(jnp.concatenate([wide[at, 2:4], counts])),
        ))
        expand_w = masters[2][at]
        second.append(gather_rows(
            [low(masters[1][at]), low(expand_w[:, :width]), low(expand_w[:, width:]),
             low(masters[3][at])],
            jnp.concatenate([wide[at, 0:2], wide[at, 4:10]]),
        ))
    current = x
    saved = []
    for at in range(layers):
        joint, probs, mixed, weight, small = attend_call(place, current, first[at])
        keep = (current, joint, probs, mixed, weight)
        if at + 1 < layers:
            current, *rest = dense_call(place, current, mixed, second[at])
            keep = (*keep, rest)
        saved.append(keep)
    counted = small
    first_grads, second_grads = [None] * layers, [None] * layers
    for at in reversed(range(layers)):
        start, joint, probs, mixed, weight = saved[at][:5]
        if at + 1 == layers:
            result, grad_mixed, grad_one, *slots = dense_turn_call(
                place, live, dataset_ids, start, mixed, second[at], counted, cotangent
            )
        else:
            grad_mixed, grad_one, *slots = dense_back_call(
                place, grad_one, grad_joint, saved[at + 1][4], mixed, saved[at][5]
            )
        second_grads[at] = slots
        *slots, grad_joint = attend_back_call(place, start, joint, probs, grad_mixed)
        first_grads[at] = slots
    grad_rows = grad_x_call(grad_one, grad_joint, weight)
    grads = [[] for _ in range(6)]
    for at in range(layers):
        kept, sent = first_grads[at]
        own, first_small = scatter_rows(kept, sent, (16, 16, 16))
        grads[0].append(jnp.concatenate(own, axis=1))
        own, small = scatter_rows(*second_grads[at], (16, 16, 16, 32))
        grads[1].append(own[0])
        grads[2].append(jnp.concatenate(own[1:3], axis=1))
        grads[3].append(own[3])
        rows = jnp.concatenate([small[0:2], first_small[0:2], small[2:8]])
        lanes = masters[4].shape[2]
        own_rows = lax.dynamic_slice(rows, (0, position * lanes), (10, lanes))
        grads[4].append(own_rows[:2])
        grads[5].append(own_rows[2:])
    outputs = []
    for master, moment, average, grad in zip(masters, moments, averages, grads):
        outputs.extend(
            advance(master, moment, average, jnp.stack(grad), rates[0], rates[1], rates[2])
        )
    return (result, grad_rows, *outputs)


def one_per_owner(place, x, cotangent, dataset_ids, live, masters, moments, averages, rates):
    width = x.shape[1]
    pair = HEADS // 2

    def to_core(stacks):
        return [swap(one, CORE) for one in stacks]

    def square(block):
        return swaps(block, SQUARE[1:])

    def square_back(stacks):
        return [swap(one, offset) for one, offset in zip(stacks[1:], SQUARE[1:])]

    def chain_back(blocks):
        return [swap(one, offset) for one, offset in zip(blocks[1:], CHAIN[1:])]

    first, following, late = pack_call(place, dataset_ids, masters)
    (first_own,) = join_call([first, *swaps(first, CHAIN[1:])])

    first_own, following = sync(first_own, following)
    first_near = [first_own, *square(first_own)]
    (following_two,) = join_call([following, swap(following, CHAIN[1])])
    second_own, third_own = join_call(
        [following_two, swap(following_two, CHAIN[2])],
        (0, SECOND_ROWS),
        (SECOND_ROWS, FIRST_ROWS),
    )
    first_far = to_core(first_near)

    first_far, second_own, third_own, x, late = sync(first_far, second_own, third_own, x, late)
    second_near = [second_own, *square(second_own)]
    second_far = [swap(second_own, CORE)]
    late_got = swap(late, CHAIN[1])
    joint, probs, mixed, weight, _ = attend_call(place, x, [*first_near, *first_far])

    mixed, second_near, second_far, third_own, late, late_got = sync(
        mixed, second_near, second_far, third_own, late, late_got
    )
    (late_two,) = join_call([late, late_got])
    second_far += to_core(second_near[1:])
    second_far, third_own, late_two, mixed = sync(second_far, third_own, late_two, mixed)
    third_near = [third_own, *square(third_own)]
    third_far = [swap(third_own, CORE)]
    late_got = swap(late_two, CHAIN[2])
    middle, *dense_kept = dense_call(place, x, mixed, [*second_near, *second_far])

    middle, third_near, third_far, late_two, late_got = sync(
        middle, third_near, third_far, late_two, late_got
    )
    third_far += to_core(third_near[1:])
    (late_own,) = join_call([late_two, late_got])
    third_far, late_own, middle = sync(third_far, late_own, middle)
    late_near = [late_own, *square(late_own)]
    late_far = [swap(late_own, CORE)]
    late_joint, late_probs, late_mixed, late_weight, small = attend_call(
        place, middle, [*third_near, *third_far]
    )

    late_mixed, late_near, late_far = sync(late_mixed, late_near, late_far)
    late_far += to_core(late_near[1:])
    result, grad_mixed, grad_one, kept, sent = dense_turn_call(
        place, live, dataset_ids, middle, late_mixed, [*late_near, *late_far], small, cotangent
    )

    sent, grad_mixed = sync(sent, grad_mixed)
    got = swap(sent, CORE)
    next_kept, next_sent, grad_joint = attend_back_call(
        place, middle, late_joint, late_probs, grad_mixed
    )

    got, next_sent, grad_joint = sync(got, next_sent, grad_joint)
    late_stacks = core_sum(kept, got)
    late_stacks, next_sent, grad_joint = sync(late_stacks, next_sent, grad_joint)
    late_got = square_back(late_stacks)
    got = swap(next_sent, CORE)
    grad_mixed, grad_one, kept, sent = dense_back_call(
        place, grad_one, grad_joint, late_weight, mixed, dense_kept
    )

    got, late_got, sent, grad_mixed = sync(got, late_got, sent, grad_mixed)
    first_stacks = core_sum(next_kept, got)
    late_kept, late_sent = square_sum_call([late_stacks[0], *late_got])
    first_stacks, late_kept, late_sent, sent, grad_mixed = sync(
        first_stacks, late_kept, late_sent, sent, grad_mixed
    )
    first_got = square_back(first_stacks)
    got = swap(sent, CORE)
    late_got = swap(late_sent, CHAIN[2])
    before = attend_back_call(place, x, joint, probs, grad_mixed, 0, pair)

    got, first_got, late_got, before = sync(got, first_got, late_got, before)
    second_stacks = core_sum(kept, got)
    late_own, late_sent = pair_sum(late_kept, late_got)
    second_stacks, before, late_sent = sync(second_stacks, before, late_sent)
    second_got = square_back(second_stacks)
    late_got = swap(late_sent, CHAIN[1])
    kept, sent, grad_joint = attend_back_call(
        place, x, joint, probs, grad_mixed, pair, HEADS - pair, before
    )

    second_got, sent, grad_joint, late_got = sync(second_got, sent, grad_joint, late_got)
    got = swap(sent, CORE)
    middle_kept, middle_sent = square_sum_call(
        [first_stacks[0], *first_got], [second_stacks[0], *second_got]
    )
    got, middle_sent = sync(got, middle_sent)
    stacks = core_sum(kept, got)
    stacks, middle_sent, grad_joint = sync(stacks, middle_sent, grad_joint)
    got = square_back(stacks)
    middle_got = swap(middle_sent, CHAIN[2])
    grad_rows = grad_x_call(grad_one, grad_joint, weight)

    middle_got, grad_rows = sync(middle_got, grad_rows)
    middle_own, middle_sent = pair_sum(middle_kept, middle_got)
    middle_got = swap(middle_sent, CHAIN[1])

    def state_of(*which):
        return [item for at in which for item in (masters[at], moments[at], averages[at])]

    last_blocks = square_sum_call([stacks[0], *got], halves=False)
    last_got = chain_back(last_blocks)
    *stepped, late_first, small = step_call(
        second_step_kernel,
        [rates],
        [middle_own, middle_got, late_own, late_got, *state_of(1, 2, 3)],
        [*step_shapes(masters[1:4]), LIKE((FIRST_ROWS, width), FLOAT),
         LIKE((2, 8, width), FLOAT)],
        "second_step",
    )
    rest = step_call(
        first_step_kernel,
        [place, rates],
        [small, late_first, last_blocks[0], *last_got, *state_of(0, 4, 5)],
        step_shapes((masters[0], masters[4], masters[5])),
        "first_step",
    )
    return (result, grad_rows, *rest[:4], *stepped, *rest[4:])


def shards(
    tokens,
    cotangent,
    dataset_ids,
    query_counts,
    learn_rate,
    momentum_coef,
    average_decay,
    step_count,
    *state,
):
    masters, moments, averages = state[0::3], state[1::3], state[2::3]
    position = lax.axis_index(AXES)
    direct = lax.axis_size(AXES) == OWNERS
    place = (position if direct else jnp.zeros_like(position)).astype(jnp.int32).reshape(1)
    step_value = step_count[0].astype(FLOAT)
    decay_now = average_decay[0] * (1.0 + step_value) / (4.0 + step_value)
    rates = jnp.stack([momentum_coef[0], learn_rate[0], decay_now])
    run = one_per_owner if direct else any_size
    result, grad_rows, *outputs = run(
        place, tokens[0], cotangent[0], dataset_ids, query_counts + CTX, masters, moments, averages,
        rates,
    )
    return (result[None], grad_rows[None], *outputs)


def solution(mesh):
    rows = P(AXES, None, None)
    weight = P(None, AXES, None)
    vector = P(None, None, AXES)
    scalar = P()
    return jax.shard_map(
        shards,
        mesh=mesh,
        in_specs=(rows, rows, P(AXES), P(AXES), *[scalar] * 4, *[weight] * 12, *[vector] * 6),
        out_specs=(rows, rows, *[weight] * 16, *[vector] * 8),
        check_vma=False,
    )
```

```python
import functools

import jax
import jax.numpy as jnp
import numpy as np
from jax import lax
from jax.experimental import pallas as pl
from jax.experimental.pallas import tpu as pltpu
from jax.sharding import PartitionSpec as P

HEADS = 4
CTX = 896
NDS = 8
EPS = 1e-05
OWNERS = 32
AXES = ("dp", "fsdp")

CHAIN = (0, 4, 2, 6)
SQUARE = (0, 1, 16, 17)
CORE = 8
ORDER = tuple(core ^ side ^ link for core in (0, CORE) for side in SQUARE for link in CHAIN)

FIRST_ROWS = 56
SECOND_ROWS = 88

ROW_BLOCK = 512
BACK_BLOCK = 256
ROOT_HALF = 0.7071067811865476
PDF_PEAK = 0.3989422804014327
VMEM_LIMIT = 60 * 1024 * 1024
SMALL_LIMIT = 12 * 1024 * 1024
FLOAT = jnp.float32
HALF = jnp.bfloat16
LIKE = jax.ShapeDtypeStruct


def product(left, right, left_dim, right_dim):
    return lax.dot_general(
        left, right, (((left_dim,), (right_dim,)), ((), ())), preferred_element_type=FLOAT
    )


def owner_rows(offset, place, rows):
    return pl.ds(pl.multiple_of((offset ^ place) * rows, rows), rows)


def params(limit=VMEM_LIMIT):
    return pltpu.CompilerParams(vmem_limit_bytes=limit)


def pack_kernel(place_ref, ids_ref, attend_ref, output_ref, expand_ref, shrink_ref, gains_ref,
                bias_ref, *outs):
    *outs, small = outs
    width = small.shape[1]
    each = gains_ref.shape[2]
    lane = lax.broadcasted_iota(jnp.int32, (each, width), 1)
    own = lax.broadcasted_iota(jnp.int32, (each, width), 0) + place_ref[0] * each
    pick = (lane == own).astype(HALF)
    lanes = lax.broadcasted_iota(jnp.int32, (1, width), 1)

    for layer in range(attend_ref.shape[0]):
        first, top, second = (outs[0], 0, outs[1]) if layer == 0 else (outs[1], SECOND_ROWS, outs[2])
        gains = product(gains_ref[layer].astype(HALF), pick, 1, 0)
        biases = product(bias_ref[layer].astype(HALF), pick, 1, 0)
        for piece in range(3):
            first[top + piece * 16 : top + (piece + 1) * 16, :] = attend_ref[
                layer, :, piece * width : (piece + 1) * width
            ].astype(HALF)
        small[...] = jnp.zeros_like(small)
        small[0:2, :] = biases[0:2, :]
        small[2:3, :] = (lanes == ids_ref[0]).astype(FLOAT)
        first[top + 48 : top + 56, :] = small[...].astype(HALF)
        second[0:16, :] = output_ref[layer].astype(HALF)
        for piece in range(2):
            second[(piece + 1) * 16 : (piece + 2) * 16, :] = expand_ref[
                layer, :, piece * width : (piece + 1) * width
            ].astype(HALF)
        second[48:80, :] = shrink_ref[layer].astype(HALF)
        small[0:2, :] = gains
        small[2:8, :] = biases[2:8, :]
        second[80:88, :] = small[...].astype(HALF)


def pack_call(place, ids, masters):
    width = masters[1].shape[2]
    rows = (FIRST_ROWS, SECOND_ROWS + FIRST_ROWS, SECOND_ROWS)
    return pl.pallas_call(
        pack_kernel,
        in_specs=[pl.BlockSpec(memory_space=pltpu.SMEM)] * 2
        + [pl.BlockSpec(memory_space=pltpu.VMEM)] * 6,
        out_specs=[pl.BlockSpec(memory_space=pltpu.VMEM)] * len(rows),
        out_shape=[LIKE((count, width), HALF) for count in rows],
        scratch_shapes=[pltpu.VMEM((8, width), FLOAT)],
        compiler_params=params(),
        cost_estimate=pl.CostEstimate(flops=0, bytes_accessed=1 << 20, transcendentals=0),
        name="pack",
    )(place, ids, *masters)


def join_kernel(cuts, count, *refs):
    each = refs[count].shape[0] // count
    for at in range(count):
        for to, (start, rows) in enumerate(cuts):
            target = refs[count + to]
            if len(refs[at].shape) == 2:
                target[at] = refs[at][start : start + rows, :]
            else:
                target[at * each : (at + 1) * each] = refs[at][:, start : start + rows, :]


def join_call(blocks, *cuts):
    *head, rows, width = blocks[0].shape
    slots = len(blocks) * (head[0] if head else 1)
    cuts = cuts or ((0, rows),)
    return pl.pallas_call(
        functools.partial(join_kernel, cuts, len(blocks)),
        out_shape=[LIKE((slots, rows, width), HALF) for _, rows in cuts],
        compiler_params=params(SMALL_LIMIT),
        cost_estimate=pl.CostEstimate(flops=0, bytes_accessed=1 << 20, transcendentals=0),
        name="join",
    )(*blocks)


def block_sum(refs):
    total = refs[0][...].astype(FLOAT)
    for ref in refs[1:]:
        total = total + ref[...].astype(FLOAT)
    return total


def core_sum(kept, got):
    return [
        (kept[at : at + 4].astype(FLOAT) + got[at : at + 4].astype(FLOAT)).astype(HALF)
        for at in range(0, 16, 4)
    ]


def core_sums_kernel(*refs):
    *sources, one, two, three, four = refs
    for to, out in enumerate((one, two, three, four)):
        start = 0
        for at in range(0, len(sources), 2):
            kept, got = (ref[4 * to : 4 * to + 4].astype(FLOAT) for ref in sources[at : at + 2])
            out[:, start : start + kept.shape[1], :] = (kept + got).astype(HALF)
            start += kept.shape[1]


def core_sums_call(*pieces):
    rows = sum(piece.shape[1] for piece in pieces[::2])
    return pl.pallas_call(
        core_sums_kernel,
        out_shape=[LIKE((4, rows, pieces[0].shape[2]), HALF)] * 4,
        compiler_params=params(SMALL_LIMIT),
        cost_estimate=pl.CostEstimate(flops=0, bytes_accessed=1 << 22, transcendentals=0),
        name="core_sums",
    )(*pieces)


def square_sum_kernel(rows, *refs):
    outs = refs[4 * len(rows) :]
    start = 0
    for at, count in enumerate(rows):
        total = block_sum(refs[4 * at : 4 * at + 4]).astype(HALF)
        for to in range(4):
            each = 4 // len(outs)
            if each == 1:
                outs[to][start : start + count, :] = total[to]
            else:
                outs[to // each][to % each, start : start + count, :] = total[to]
        start += count


def square_sum_call(*pieces, halves=True):
    rows = tuple(stacks[0].shape[1] for stacks in pieces)
    shape = (sum(rows), pieces[0][0].shape[2])
    return pl.pallas_call(
        functools.partial(square_sum_kernel, rows),
        out_shape=[LIKE((2, *shape), HALF)] * 2 if halves else [LIKE(shape, HALF)] * 4,
        compiler_params=params(SMALL_LIMIT),
        cost_estimate=pl.CostEstimate(flops=0, bytes_accessed=1 << 21, transcendentals=0),
        name="square_sum",
    )(*[stack for stacks in pieces for stack in stacks])


def pair_sum(kept, got):
    return [(kept[at].astype(FLOAT) + got[at].astype(FLOAT)).astype(HALF) for at in range(2)]


def swap(block, offset):
    return lax.ppermute(block, AXES, [(one, one ^ offset) for one in range(OWNERS)])


def swaps(block, offsets):
    return [swap(block, offset) for offset in offsets]


def slot_places(slot_refs):
    for at, offset in enumerate(ORDER):
        yield slot_refs[at // 4], at % 4, offset


def small_rows(slot_refs, start):
    total = None
    for slots in slot_refs:
        for at in range(slots.shape[0]):
            block = slots[at, start : start + 8, :].astype(FLOAT)
            total = block if total is None else total + block
    return total


def attend_kernel(place_ref, x_ref, *refs):
    slot_refs = refs[:8]
    joint_ref, probs_ref, mixed_ref, weight_ref, small_ref = refs[8:]
    count = joint_ref.shape[0]
    head_size = joint_ref.shape[2] // 3
    place = place_ref[0]

    for slots, at, offset in slot_places(slot_refs):
        rows = owner_rows(offset, place, 16)
        for piece in range(3):
            for head in range(count):
                weight_ref[head, rows, piece * head_size : (piece + 1) * head_size] = slots[
                    at, piece * 16 : (piece + 1) * 16, head * head_size : (head + 1) * head_size
                ]
    zeros = jnp.zeros((1, head_size), FLOAT)
    small = small_rows(slot_refs, 48)
    small_ref[...] = small
    factor = head_size ** (-0.5) * 1.4426950408889634
    weights = jnp.concatenate([weight_ref[head] for head in range(count)], axis=1)
    wide = product(x_ref[...], weights, 1, 0)
    for head in range(count):
        own = slice(head * head_size, (head + 1) * head_size)
        shift = jnp.concatenate([small[0:1, own], zeros, small[1:2, own]], axis=1)
        part = wide[:, 3 * head * head_size : 3 * (head + 1) * head_size]
        joint_ref[head] = (part + shift).astype(HALF)
    scores = []
    for head in range(count):
        keys = joint_ref[head, :CTX, head_size : 2 * head_size]
        scores.append(product(keys, joint_ref[head, :, :head_size], 1, 1))
    for head in range(count):
        values_turned = jnp.transpose(joint_ref[head, :CTX, 2 * head_size :])
        top = jnp.max(scores[head], axis=0, keepdims=True)
        grown = jnp.exp2((scores[head] - top) * factor)
        total = jnp.sum(grown, axis=0, keepdims=True)
        probs = (grown * (1.0 / total)).astype(HALF)
        probs_ref[head] = probs
        mixed_ref[:, head * head_size : (head + 1) * head_size] = jnp.transpose(
            product(values_turned, probs, 1, 0)
        ).astype(HALF)


def attend_call(place, x, slots):
    rows, width = x.shape
    head_size = width // HEADS
    return pl.pallas_call(
        attend_kernel,
        grid_spec=pltpu.PrefetchScalarGridSpec(
            num_scalar_prefetch=1,
            grid=(HEADS // 2,),
            in_specs=[pl.BlockSpec((rows, width), lambda h, p: (0, 0))]
            + [pl.BlockSpec((part.shape[0], FIRST_ROWS, 2 * head_size), lambda h, p: (0, 0, h))
               for part in slots],
            out_specs=[
                pl.BlockSpec((2, rows, 3 * head_size), lambda h, p: (h, 0, 0)),
                pl.BlockSpec((2, CTX, rows), lambda h, p: (h, 0, 0)),
                pl.BlockSpec((rows, 2 * head_size), lambda h, p: (0, h)),
                pl.BlockSpec((2, width, 3 * head_size), lambda h, p: (h, 0, 0)),
                pl.BlockSpec((8, 2 * head_size), lambda h, p: (0, h)),
            ],
        ),
        out_shape=[
            LIKE((HEADS, rows, 3 * head_size), HALF),
            LIKE((HEADS, CTX, rows), HALF),
            LIKE((rows, HEADS * head_size), HALF),
            LIKE((HEADS, width, 3 * head_size), HALF),
            LIKE((8, width), FLOAT),
        ],
        compiler_params=params(),
        cost_estimate=pl.CostEstimate(
            flops=HEADS * (2 * rows * width * 3 * head_size + 4 * rows * CTX * head_size),
            bytes_accessed=HEADS * 4 * 1024 * 1024,
            transcendentals=HEADS * rows * CTX,
        ),
        name="attend",
    )(place, x, *slots)


def unpack_second(place, slot_refs, output_w, expand_w, shrink_w, vec_ref):
    width = output_w.shape[1]
    for slots, at, offset in slot_places(slot_refs):
        rows = owner_rows(offset, place, 16)
        output_w[rows, :] = slots[at, 0:16, :]
        expand_w[rows, :width] = slots[at, 16:32, :]
        expand_w[rows, width:] = slots[at, 32:48, :]
        shrink_w[owner_rows(offset, place, 32), :] = slots[at, 48:80, :]
    vec_ref[...] = small_rows(slot_refs, 80)


def row_mean(rows):
    return jnp.mean(rows, axis=-1, keepdims=True)


def normalize(rows):
    centred = rows - row_mean(rows)
    inv_std = lax.rsqrt(row_mean(centred * centred) + EPS)
    return (centred * inv_std, inv_std)


def forward_rows(x_ref, mixed_ref, vec_ref, output_w, expand_w, shrink_w):
    attn_out = product(mixed_ref[...], output_w[...], 1, 0) + vec_ref[2:3, :]
    unit_one, inv_one = normalize(x_ref[...].astype(FLOAT) + attn_out)
    first_norm = unit_one * vec_ref[0:1, :] + vec_ref[4:5, :]
    first_low = first_norm.astype(HALF)
    shift = jnp.concatenate([vec_ref[6:7, :], vec_ref[7:8, :]], axis=1)
    hidden = product(first_low, expand_w[...], 1, 0) + shift
    normal_cdf = 0.5 * (1.0 + lax.erf(hidden * ROOT_HALF))
    act_low = (hidden * normal_cdf).astype(HALF)
    slope = normal_cdf + hidden * (jnp.exp(-0.5 * hidden * hidden) * PDF_PEAK)
    branch = product(act_low, shrink_w[...], 1, 0) + vec_ref[3:4, :]
    unit_two, inv_two = normalize(first_norm + branch)
    result = unit_two * vec_ref[1:2, :] + vec_ref[5:6, :]
    return (unit_one, inv_one, first_low, act_low, slope, unit_two, inv_two, result)


def column_sum(rows):
    return jnp.sum(rows, axis=0, keepdims=True)


def backward_rows(grad_rows, mixed_ref, vec_ref, kept, output_w, expand_w, shrink_w,
                  grad_mixed_ref, grad_one_ref, grad_output, grad_expand, grad_shrink, sums):
    unit_one, inv_one, first_low, act_low, slope, unit_two, inv_two = kept
    width = grad_rows.shape[1]

    def layer_norm_back(rows, unit_rows, inv_std, gain):
        scaled = rows * gain
        return inv_std * (scaled - row_mean(scaled) - unit_rows * row_mean(scaled * unit_rows))

    grad_two = layer_norm_back(grad_rows, unit_two, inv_two, vec_ref[1:2, :])
    branch_low = grad_two.astype(HALF)
    grad_shrink[...] += product(act_low, branch_low, 0, 0)
    grad_hidden = (product(branch_low, shrink_w[...], 1, 1) * slope).astype(HALF)
    grad_expand[...] += product(first_low, grad_hidden, 0, 0)
    grad_first = grad_two + product(grad_hidden, expand_w[...], 1, 1)
    grad_one = layer_norm_back(grad_first, unit_one, inv_one, vec_ref[0:1, :])
    attn_low = grad_one.astype(HALF)
    grad_output[...] += product(mixed_ref[...], attn_low, 0, 0)
    grad_mixed_ref[...] = product(attn_low, output_w[...], 1, 1).astype(HALF)
    grad_one_ref[...] = grad_one
    sums[0:1, :] += column_sum(grad_first * unit_one)
    sums[1:2, :] += column_sum(grad_rows * unit_two)
    sums[2:3, :] += column_sum(attn_low.astype(FLOAT))
    sums[3:4, :] += column_sum(branch_low.astype(FLOAT))
    sums[4:5, :] += column_sum(grad_first)
    sums[5:6, :] += column_sum(grad_rows)
    hidden_sum = column_sum(grad_hidden.astype(FLOAT))
    sums[6:7, :] += hidden_sum[:, :width]
    sums[7:8, :] += hidden_sum[:, width:]


def pack_second(place, kept_ref, sent_ref, grad_output, grad_expand, grad_shrink, sums):
    width = grad_output.shape[1]
    small = sums[...].astype(HALF)
    for at, offset in enumerate(ORDER):
        slots_ref = kept_ref if at < 16 else sent_ref
        at = at % 16
        rows = owner_rows(offset, place, 16)
        slots_ref[at, 0:16, :] = grad_output[rows, :].astype(HALF)
        slots_ref[at, 16:32, :] = grad_expand[rows, :width].astype(HALF)
        slots_ref[at, 32:48, :] = grad_expand[rows, width:].astype(HALF)
        slots_ref[at, 48:80, :] = grad_shrink[owner_rows(offset, place, 32), :].astype(HALF)
        slots_ref[at, 80:88, :] = small


def dense_kernel(place_ref, x_ref, mixed_ref, *refs):
    slot_refs = refs[:8]
    (result_ref, unit_one_ref, inv_one_ref, act_ref, slope_ref, unit_two_ref, inv_two_ref, output_w,
     expand_w, shrink_w, vec_ref) = refs[8:]

    @pl.when(pl.program_id(0) == 0)
    def _():
        unpack_second(place_ref[0], slot_refs, output_w, expand_w, shrink_w, vec_ref)

    unit_one, inv_one, _, act_low, slope, unit_two, inv_two, result = forward_rows(
        x_ref, mixed_ref, vec_ref, output_w, expand_w, shrink_w
    )
    result_ref[...] = result.astype(HALF)
    unit_one_ref[...] = unit_one
    inv_one_ref[...] = inv_one
    act_ref[...] = act_low
    slope_ref[...] = slope
    unit_two_ref[...] = unit_two
    inv_two_ref[...] = inv_two


def grad_x_rows(grad_one_ref, grad_joint_ref, weight_ref):
    total = grad_one_ref[...]
    for head in range(weight_ref.shape[0]):
        total = total + product(grad_joint_ref[head], weight_ref[head], 1, 1)
    return total


def clear(*items):
    for item in items:
        item[...] = jnp.zeros_like(item)


def dense_back_kernel(place_ref, grad_one_next, grad_joint_next, weight_next, mixed_ref, *refs):
    (unit_one_ref, inv_one_ref, act_ref, slope_ref, unit_two_ref, inv_two_ref, output_w, expand_w,
     shrink_w, vec_ref, grad_mixed_ref, grad_one_ref, kept_ref, sent_ref, sums, grad_output,
     grad_expand, grad_shrink) = refs

    @pl.when(pl.program_id(0) == 0)
    def _():
        clear(sums, grad_output, grad_expand, grad_shrink)

    unit_one = unit_one_ref[...]
    first_low = (unit_one * vec_ref[0:1, :] + vec_ref[4:5, :]).astype(HALF)
    kept = (unit_one, inv_one_ref[...], first_low, act_ref[...], slope_ref[...], unit_two_ref[...],
            inv_two_ref[...])
    grad_rows = grad_x_rows(grad_one_next, grad_joint_next, weight_next)
    backward_rows(grad_rows, mixed_ref, vec_ref, kept, output_w, expand_w, shrink_w,
                  grad_mixed_ref, grad_one_ref, grad_output, grad_expand, grad_shrink, sums)

    @pl.when(pl.program_id(0) == pl.num_programs(0) - 1)
    def _():
        pack_second(place_ref[0], kept_ref, sent_ref, grad_output, grad_expand, grad_shrink, sums)


def dense_turn_kernel(place_ref, live_ref, ids_ref, x_ref, mixed_ref, *refs):
    slot_refs = refs[:8]
    (counts_ref, cot_ref, result_ref, grad_mixed_ref, grad_one_ref, kept_ref, sent_ref, output_w, expand_w,
     shrink_w, vec_ref, grad_output, grad_expand, grad_shrink, sums) = refs[8:]
    step = pl.program_id(0)

    @pl.when(step == 0)
    def _():
        unpack_second(place_ref[0], slot_refs, output_w, expand_w, shrink_w, vec_ref)
        clear(sums, grad_output, grad_expand, grad_shrink)

    *kept, result = forward_rows(x_ref, mixed_ref, vec_ref, output_w, expand_w, shrink_w)
    result_ref[...] = result.astype(HALF)
    counts = counts_ref[2:3, :]
    lanes = lax.broadcasted_iota(jnp.int32, counts.shape, 1)
    own_count = jnp.sum(jnp.where(lanes == ids_ref[0], counts, 0.0), axis=1, keepdims=True)
    row_weight = jnp.sum(counts, axis=1, keepdims=True) / (NDS * own_count)
    rows = cot_ref.shape[0]
    slot = lax.broadcasted_iota(jnp.int32, (rows, 1), 0) + step * rows
    grad_rows = cot_ref[...].astype(FLOAT) * jnp.where(slot < live_ref[0], row_weight, 0.0)
    backward_rows(grad_rows, mixed_ref, vec_ref, kept, output_w, expand_w, shrink_w,
                  grad_mixed_ref, grad_one_ref, grad_output, grad_expand, grad_shrink, sums)

    @pl.when(step == pl.num_programs(0) - 1)
    def _():
        pack_second(place_ref[0], kept_ref, sent_ref, grad_output, grad_expand, grad_shrink, sums)


def by_rows(width, block=ROW_BLOCK):
    return pl.BlockSpec((block, width), lambda i, *p: (i, 0))


def fixed(*shape):
    return pl.BlockSpec(shape, lambda i, *p: (0,) * len(shape))


def joint_rows(grad_joint, block=ROW_BLOCK):
    heads, _, width = grad_joint.shape
    return pl.BlockSpec((heads, block, width), lambda i, *p: (0, i, 0))


def weight_shapes(width):
    return [(width, width), (width, 2 * width), (2 * width, width)]


def dense_call(place, x, mixed, slots):
    rows, width = x.shape
    weights = weight_shapes(width)
    return pl.pallas_call(
        dense_kernel,
        grid_spec=pltpu.PrefetchScalarGridSpec(
            num_scalar_prefetch=1,
            grid=(rows // ROW_BLOCK,),
            in_specs=[by_rows(width)] * 2
            + [fixed(*part.shape) for part in slots],
            out_specs=[by_rows(width), by_rows(width), by_rows(1), by_rows(2 * width),
                       by_rows(2 * width), by_rows(width), by_rows(1)]
            + [fixed(*shape) for shape in weights]
            + [fixed(8, width)],
        ),
        out_shape=[LIKE((rows, width), HALF), LIKE((rows, width), FLOAT), LIKE((rows, 1), FLOAT),
                   LIKE((rows, 2 * width), HALF), LIKE((rows, 2 * width), FLOAT),
                   LIKE((rows, width), FLOAT), LIKE((rows, 1), FLOAT)]
        + [LIKE(shape, HALF) for shape in weights]
        + [LIKE((8, width), FLOAT)],
        compiler_params=params(),
        cost_estimate=pl.CostEstimate(
            flops=10 * rows * width * width, bytes_accessed=16 * 1024 * 1024,
            transcendentals=4 * rows * width,
        ),
        name="dense",
    )(place, x, mixed, *slots)


def dense_back_call(place, grad_one, grad_joint, weight, mixed, kept):
    rows, width = grad_one.shape
    weights = weight_shapes(width)
    some_rows = functools.partial(by_rows, block=BACK_BLOCK)
    return pl.pallas_call(
        dense_back_kernel,
        grid_spec=pltpu.PrefetchScalarGridSpec(
            num_scalar_prefetch=1,
            grid=(rows // BACK_BLOCK,),
            in_specs=[some_rows(width), joint_rows(grad_joint, BACK_BLOCK), fixed(*weight.shape), some_rows(width)]
            + [some_rows(width), some_rows(1), some_rows(2 * width), some_rows(2 * width), some_rows(width),
               some_rows(1)]
            + [fixed(*shape) for shape in weights]
            + [fixed(8, width)],
            out_specs=[some_rows(width), some_rows(width)] + [fixed(16, SECOND_ROWS, width)] * 2,
            scratch_shapes=[pltpu.VMEM((8, width), FLOAT)]
            + [pltpu.VMEM(shape, FLOAT) for shape in weights],
        ),
        out_shape=[LIKE((rows, width), HALF), LIKE((rows, width), FLOAT)]
        + [LIKE((16, SECOND_ROWS, width), HALF)] * 2,
        compiler_params=params(),
        cost_estimate=pl.CostEstimate(
            flops=26 * rows * width * width, bytes_accessed=20 * 1024 * 1024, transcendentals=0
        ),
        name="dense_back",
    )(place, grad_one, grad_joint, weight, mixed, *kept)


def dense_turn_call(place, live, ids, x, mixed, slots, small, cotangent):
    rows, width = x.shape
    weights = weight_shapes(width)
    return pl.pallas_call(
        dense_turn_kernel,
        grid_spec=pltpu.PrefetchScalarGridSpec(
            num_scalar_prefetch=3,
            grid=(rows // ROW_BLOCK,),
            in_specs=[by_rows(width)] * 2
            + [fixed(*part.shape) for part in slots]
            + [fixed(8, width), by_rows(width)],
            out_specs=[by_rows(width)] * 3 + [fixed(16, SECOND_ROWS, width)] * 2,
            scratch_shapes=[pltpu.VMEM(shape, HALF) for shape in weights]
            + [pltpu.VMEM((8, width), FLOAT)]
            + [pltpu.VMEM(shape, FLOAT) for shape in weights]
            + [pltpu.VMEM((8, width), FLOAT)],
        ),
        out_shape=[LIKE((rows, width), HALF), LIKE((rows, width), HALF), LIKE((rows, width), FLOAT)]
        + [LIKE((16, SECOND_ROWS, width), HALF)] * 2,
        compiler_params=params(),
        cost_estimate=pl.CostEstimate(
            flops=30 * rows * width * width, bytes_accessed=16 * 1024 * 1024,
            transcendentals=4 * rows * width,
        ),
        name="dense_turn",
    )(place, live, ids, x, mixed, *slots, small, cotangent)


def attend_back_kernel(place_ref, x_ref, joint_ref, probs_ref, grad_mixed_ref, kept_ref, sent_ref,
                       grad_joint_ref, grad_scores, small):
    grad_joint = grad_joint_ref.at[0]
    rows = x_ref.shape[0]
    head_size = grad_mixed_ref.shape[1]
    place = place_ref[0]

    @pl.when(pl.program_id(0) == 0)
    def _():
        clear(small)

    grad_joint[CTX:, head_size:] = jnp.zeros((rows - CTX, 2 * head_size), HALF)
    keys = joint_ref[0, :CTX, head_size : 2 * head_size]
    values = joint_ref[0, :CTX, 2 * head_size :]
    keys_turned = jnp.transpose(keys)
    factor = head_size ** (-0.5)
    grad_probs = product(values, grad_mixed_ref[...], 1, 1)
    probs = probs_ref[0].astype(FLOAT)
    level = column_sum(probs * grad_probs)
    grad_low = (probs * (grad_probs - level)).astype(HALF)
    grad_scores[...] = grad_low
    grad_joint[:, :head_size] = jnp.transpose(factor * product(keys_turned, grad_low, 1, 0)).astype(
        HALF
    )
    grad_joint[:CTX, head_size : 2 * head_size] = (
        factor * product(grad_scores[...], joint_ref[0, :, :head_size], 1, 0)
    ).astype(HALF)
    grad_joint[:CTX, 2 * head_size :] = product(probs_ref[0], grad_mixed_ref[...], 1, 0).astype(HALF)
    sums = column_sum(grad_joint[...].astype(FLOAT))
    small[0:1, :] = sums[:, :head_size]
    small[1:2, :] = sums[:, 2 * head_size :]
    small_low = small[...].astype(HALF)
    grad_low = product(x_ref[...], grad_joint[...], 0, 0).astype(HALF)
    holder = grad_scores
    holder[: grad_low.shape[0], : 3 * head_size] = grad_low
    for at, offset in enumerate(ORDER):
        slots_ref = kept_ref if at < 16 else sent_ref
        at = at % 16
        span = owner_rows(offset, place, 16)
        for piece in range(3):
            slots_ref[at, piece * 16 : (piece + 1) * 16, :] = holder[
                span, piece * head_size : (piece + 1) * head_size
            ]
        slots_ref[at, 48:56, :] = small_low


def attend_back_call(place, x, joint, probs, grad_mixed):
    rows, width = x.shape
    head_size = width // HEADS
    return pl.pallas_call(
        attend_back_kernel,
        grid_spec=pltpu.PrefetchScalarGridSpec(
            num_scalar_prefetch=1,
            grid=(HEADS,),
            in_specs=[
                pl.BlockSpec((rows, width), lambda h, p: (0, 0)),
                pl.BlockSpec((1, rows, 3 * head_size), lambda h, p: (h, 0, 0)),
                pl.BlockSpec((1, CTX, rows), lambda h, p: (h, 0, 0)),
                pl.BlockSpec((rows, head_size), lambda h, p: (0, h)),
            ],
            out_specs=[pl.BlockSpec((16, FIRST_ROWS, head_size), lambda h, p: (0, 0, h))] * 2
            + [pl.BlockSpec((1, rows, 3 * head_size), lambda h, p: (h, 0, 0))],
            scratch_shapes=[pltpu.VMEM((CTX, rows), HALF), pltpu.VMEM((8, head_size), FLOAT)],
        ),
        out_shape=[LIKE((16, FIRST_ROWS, width), HALF)] * 2
        + [LIKE((HEADS, rows, 3 * head_size), HALF)],
        compiler_params=params(),
        cost_estimate=pl.CostEstimate(
            flops=HEADS * (6 * rows * width * head_size + 8 * rows * CTX * head_size),
            bytes_accessed=HEADS * 4 * 1024 * 1024, transcendentals=0,
        ),
        name="attend_back",
    )(place, x, joint, probs, grad_mixed)


def grad_x_kernel(grad_one_ref, grad_joint_ref, weight_ref, grad_x_ref):
    grad_x_ref[...] = grad_x_rows(grad_one_ref, grad_joint_ref, weight_ref)


def grad_x_call(grad_one, grad_joint, weight):
    rows, width = grad_one.shape
    return pl.pallas_call(
        grad_x_kernel,
        grid=(rows // ROW_BLOCK,),
        in_specs=[
            by_rows(width),
            joint_rows(grad_joint),
            fixed(*weight.shape),
        ],
        out_specs=by_rows(width),
        out_shape=LIKE((rows, width), FLOAT),
        compiler_params=params(),
        cost_estimate=pl.CostEstimate(
            flops=6 * rows * width * width, bytes_accessed=10 * 1024 * 1024, transcendentals=0
        ),
        name="grad_x",
    )(grad_one, grad_joint, weight)


def advance(master, moment, average, grad, momentum, step_rate, decay_now):
    new_moment = momentum * moment + grad
    new_master = master - step_rate * (grad + momentum * new_moment)
    new_average = decay_now * average + (1.0 - decay_now) * new_master
    return (new_moment, new_average, new_master, new_master.astype(HALF))


def stepper(rates_ref, state_refs, out_refs):
    rates = [rates_ref[at] for at in range(3)]

    def step(weight, where, grad):
        state = [ref[where] for ref in state_refs[3 * weight : 3 * weight + 3]]
        for ref, item in zip(out_refs[4 * weight : 4 * weight + 4], advance(*state, grad, *rates)):
            ref[where] = item

    return step


def second_step_kernel(rates_ref, *refs):
    middle, late = block_sum(refs[:2]), block_sum(refs[2:4])
    state_refs, out_refs, (first_ref, small_ref) = refs[4:13], refs[13:25], refs[25:]
    width = small_ref.shape[2]
    step = stepper(rates_ref, state_refs, out_refs)
    for layer, piece in enumerate((middle[FIRST_ROWS:], late)):
        step(0, (layer,), piece[0:16])
        step(1, (layer, slice(None), slice(0, width)), piece[16:32])
        step(1, (layer, slice(None), slice(width, 2 * width)), piece[32:48])
        step(2, (layer,), piece[48:80])
        small_ref[layer] = piece[80:88]
    first_ref[...] = middle[:FIRST_ROWS]


def step_shapes(masters):
    return [
        LIKE(master.shape, kind) for master in masters for kind in (FLOAT, FLOAT, FLOAT, HALF)
    ]


def step_call(kernel, rates, inputs, out_shape, name):
    return pl.pallas_call(
        kernel,
        in_specs=[pl.BlockSpec(memory_space=pltpu.SMEM)] * len(rates)
        + [pl.BlockSpec(memory_space=pltpu.VMEM)] * len(inputs),
        out_specs=[pl.BlockSpec(memory_space=pltpu.VMEM)] * len(out_shape),
        out_shape=out_shape,
        compiler_params=params(SMALL_LIMIT),
        cost_estimate=pl.CostEstimate(flops=0, bytes_accessed=1 << 22, transcendentals=0),
        name=name,
    )(*rates, *inputs)


def first_step_kernel(place_ref, rates_ref, small_ref, late_ref, *refs):
    blocks, state_refs, out_refs = refs[:4], refs[4:13], refs[13:]
    width = small_ref.shape[2]
    each = out_refs[4].shape[2]
    step = stepper(rates_ref, state_refs, out_refs)
    turn = width - place_ref[0] * each
    for layer, total in enumerate((block_sum(blocks), late_ref[...])):
        for piece in range(3):
            columns = slice(piece * width, (piece + 1) * width)
            step(0, (layer, slice(None), columns), total[piece * 16 : (piece + 1) * 16])
        own_first = pltpu.roll(total[48:56], turn, 1)[:, :each]
        own_second = pltpu.roll(small_ref[layer], turn, 1)[:, :each]
        step(1, (layer,), own_second[0:2])
        step(2, (layer, slice(0, 2)), own_first[0:2])
        step(2, (layer, slice(2, 8)), own_second[2:8])


def wide_to_rows(shard, width):
    return jnp.concatenate(
        [shard[:, at * width : (at + 1) * width] for at in range(shard.shape[1] // width)]
    )


def rows_to_wide(rows, pieces):
    each = rows.shape[0] // pieces
    return jnp.concatenate([rows[at * each : (at + 1) * each] for at in range(pieces)], axis=1)


def gather_rows(shards_by_part, small):
    width = small.shape[1]
    parts = []
    for shard in shards_by_part:
        whole = lax.all_gather(shard, AXES, axis=0, tiled=False)
        parts.append(whole.reshape(OWNERS, -1, width))
    smalls = jnp.broadcast_to(small[None] * (jnp.arange(OWNERS) == 0)[:, None, None].astype(HALF),
                              (OWNERS, *small.shape))
    slots = jnp.concatenate([*parts, smalls], axis=1)[np.array(ORDER)]
    return [slots[4 * at : 4 * at + 4] for at in range(8)]


def scatter_rows(kept, sent, parts):
    slots = jnp.concatenate([kept, sent])[np.argsort(np.array(ORDER))]
    everyone = lax.axis_size(AXES)
    own, start = [], 0
    for rows in parts:
        piece = slots[:, start : start + rows].reshape(everyone, -1, slots.shape[2])
        own.append(lax.psum_scatter(piece, AXES, scatter_dimension=0, tiled=False).astype(FLOAT))
        start += rows
    return own, lax.psum(slots[0, start:].astype(FLOAT), AXES)


def sync(*items):
    return lax.optimization_barrier(items)


def any_size(place, x, cotangent, dataset_ids, live, masters, moments, averages, rates):
    layers = masters[0].shape[0]
    width = x.shape[1]
    position = lax.axis_index(AXES)
    low = lambda item: item.astype(HALF)
    own = low(jnp.concatenate([masters[4], masters[5]], axis=1))
    wide = lax.all_gather(own, AXES, axis=2, tiled=True)
    onehot = (dataset_ids[0] == jnp.arange(width, dtype=jnp.int32)).astype(FLOAT)
    counts = low(lax.psum(onehot, AXES))[None]
    first, second = [], []
    for at in range(layers):
        pad = lambda rows: jnp.pad(rows, ((0, 8 - rows.shape[0]), (0, 0)))
        attend_w = masters[0][at]
        first.append(gather_rows(
            [low(attend_w[:, piece * width : (piece + 1) * width]) for piece in range(3)],
            pad(jnp.concatenate([wide[at, 2:4], counts])),
        ))
        expand_w = masters[2][at]
        second.append(gather_rows(
            [low(masters[1][at]), low(expand_w[:, :width]), low(expand_w[:, width:]),
             low(masters[3][at])],
            jnp.concatenate([wide[at, 0:2], wide[at, 4:10]]),
        ))
    current = x
    saved = []
    for at in range(layers):
        joint, probs, mixed, weight, small = attend_call(place, current, first[at])
        keep = (current, joint, probs, mixed, weight)
        if at + 1 < layers:
            current, *rest = dense_call(place, current, mixed, second[at])
            keep = (*keep, rest)
        saved.append(keep)
    counted = small
    first_grads, second_grads = [None] * layers, [None] * layers
    for at in reversed(range(layers)):
        start, joint, probs, mixed, weight = saved[at][:5]
        if at + 1 == layers:
            result, grad_mixed, grad_one, *slots = dense_turn_call(
                place, live, dataset_ids, start, mixed, second[at], counted, cotangent
            )
        else:
            grad_mixed, grad_one, *slots = dense_back_call(
                place, grad_one, grad_joint, saved[at + 1][4], mixed, saved[at][5]
            )
        second_grads[at] = slots
        *slots, grad_joint = attend_back_call(place, start, joint, probs, grad_mixed)
        first_grads[at] = slots
    grad_rows = grad_x_call(grad_one, grad_joint, weight)
    grads = [[] for _ in range(6)]
    for at in range(layers):
        kept, sent = first_grads[at]
        own, first_small = scatter_rows(kept, sent, (16, 16, 16))
        grads[0].append(jnp.concatenate(own, axis=1))
        own, small = scatter_rows(*second_grads[at], (16, 16, 16, 32))
        grads[1].append(own[0])
        grads[2].append(jnp.concatenate(own[1:3], axis=1))
        grads[3].append(own[3])
        rows = jnp.concatenate([small[0:2], first_small[0:2], small[2:8]])
        lanes = masters[4].shape[2]
        own_rows = lax.dynamic_slice(rows, (0, position * lanes), (10, lanes))
        grads[4].append(own_rows[:2])
        grads[5].append(own_rows[2:])
    outputs = []
    for master, moment, average, grad in zip(masters, moments, averages, grads):
        outputs.extend(
            advance(master, moment, average, jnp.stack(grad), rates[0], rates[1], rates[2])
        )
    return (result, grad_rows, *outputs)


def one_per_owner(place, x, cotangent, dataset_ids, live, masters, moments, averages, rates):
    width = x.shape[1]

    def to_core(stacks):
        return [swap(one, CORE) for one in stacks]

    def square(block):
        return swaps(block, SQUARE[1:])

    def square_back(stacks):
        return [swap(one, offset) for one, offset in zip(stacks[1:], SQUARE[1:])]

    def chain_back(blocks):
        return [swap(one, offset) for one, offset in zip(blocks[1:], CHAIN[1:])]

    first, following, late = pack_call(place, dataset_ids, masters)
    (first_own,) = join_call([first, *swaps(first, CHAIN[1:])])

    first_own, following = sync(first_own, following)
    first_near = [first_own, *square(first_own)]
    (following_two,) = join_call([following, swap(following, CHAIN[1])])
    second_own, third_own = join_call(
        [following_two, swap(following_two, CHAIN[2])],
        (0, SECOND_ROWS),
        (SECOND_ROWS, FIRST_ROWS),
    )
    first_far = to_core(first_near)

    first_far, second_own, third_own, x, late = sync(first_far, second_own, third_own, x, late)
    second_near = [second_own, *square(second_own)]
    second_far = [swap(second_own, CORE)]
    late_got = swap(late, CHAIN[1])
    joint, probs, mixed, weight, _ = attend_call(place, x, [*first_near, *first_far])

    mixed, second_near, second_far, third_own, late, late_got = sync(
        mixed, second_near, second_far, third_own, late, late_got
    )
    (late_two,) = join_call([late, late_got])
    second_far += to_core(second_near[1:])
    second_far, third_own, late_two, mixed = sync(second_far, third_own, late_two, mixed)
    third_near = [third_own, *square(third_own)]
    third_far = [swap(third_own, CORE)]
    late_got = swap(late_two, CHAIN[2])
    middle, *dense_kept = dense_call(place, x, mixed, [*second_near, *second_far])

    middle, third_near, third_far, late_two, late_got = sync(
        middle, third_near, third_far, late_two, late_got
    )
    third_far += to_core(third_near[1:])
    (late_own,) = join_call([late_two, late_got])
    third_far, late_own, middle = sync(third_far, late_own, middle)
    late_near = [late_own, *square(late_own)]
    late_far = [swap(late_own, CORE)]
    late_joint, late_probs, late_mixed, late_weight, small = attend_call(
        place, middle, [*third_near, *third_far]
    )

    late_mixed, late_near, late_far = sync(late_mixed, late_near, late_far)
    late_far += to_core(late_near[1:])
    result, grad_mixed, grad_one, kept, sent = dense_turn_call(
        place, live, dataset_ids, middle, late_mixed, [*late_near, *late_far], small, cotangent
    )

    sent, grad_mixed = sync(sent, grad_mixed)
    got = swap(sent, CORE)
    next_kept, next_sent, grad_joint = attend_back_call(
        place, middle, late_joint, late_probs, grad_mixed
    )

    got, next_sent, grad_joint = sync(got, next_sent, grad_joint)
    late_stacks = core_sum(kept, got)
    late_stacks, next_sent, grad_joint = sync(late_stacks, next_sent, grad_joint)
    late_got = square_back(late_stacks)
    got = swap(next_sent, CORE)
    grad_mixed, grad_one, kept, sent = dense_back_call(
        place, grad_one, grad_joint, late_weight, mixed, dense_kept
    )

    got, late_got, sent, grad_mixed = sync(got, late_got, sent, grad_mixed)
    late_kept, late_sent = square_sum_call([late_stacks[0], *late_got])
    stacks = core_sums_call(next_kept, got, kept, swap(sent, CORE))
    stacks, late_kept, late_sent, grad_mixed = sync(stacks, late_kept, late_sent, grad_mixed)
    middle_got = square_back(stacks)
    late_got = swap(late_sent, CHAIN[2])
    kept, sent, grad_joint = attend_back_call(place, x, joint, probs, grad_mixed)
    grad_rows = grad_x_call(grad_one, grad_joint, weight)

    middle_got, late_got, sent, grad_rows = sync(middle_got, late_got, sent, grad_rows)
    got = swap(sent, CORE)
    late_own, late_sent = pair_sum(late_kept, late_got)
    middle_kept, middle_sent = square_sum_call([stacks[0], *middle_got])
    got, middle_sent, late_sent = sync(got, middle_sent, late_sent)
    stacks = core_sum(kept, got)
    stacks, middle_sent, late_sent = sync(stacks, middle_sent, late_sent)
    got = square_back(stacks)
    middle_got = swap(middle_sent, CHAIN[2])
    late_got = swap(late_sent, CHAIN[1])
    middle_got, late_got = sync(middle_got, late_got)
    middle_own, middle_sent = pair_sum(middle_kept, middle_got)
    middle_got = swap(middle_sent, CHAIN[1])

    def state_of(*which):
        return [item for at in which for item in (masters[at], moments[at], averages[at])]

    last_blocks = square_sum_call([stacks[0], *got], halves=False)
    last_got = chain_back(last_blocks)
    *stepped, late_first, small = step_call(
        second_step_kernel,
        [rates],
        [middle_own, middle_got, late_own, late_got, *state_of(1, 2, 3)],
        [*step_shapes(masters[1:4]), LIKE((FIRST_ROWS, width), FLOAT),
         LIKE((2, 8, width), FLOAT)],
        "second_step",
    )
    rest = step_call(
        first_step_kernel,
        [place, rates],
        [small, late_first, last_blocks[0], *last_got, *state_of(0, 4, 5)],
        step_shapes((masters[0], masters[4], masters[5])),
        "first_step",
    )
    return (result, grad_rows, *rest[:4], *stepped, *rest[4:])


def shards(
    tokens,
    cotangent,
    dataset_ids,
    query_counts,
    learn_rate,
    momentum_coef,
    average_decay,
    step_count,
    *state,
):
    masters, moments, averages = state[0::3], state[1::3], state[2::3]
    position = lax.axis_index(AXES)
    direct = lax.axis_size(AXES) == OWNERS
    place = (position if direct else jnp.zeros_like(position)).astype(jnp.int32).reshape(1)
    step_value = step_count[0].astype(FLOAT)
    decay_now = average_decay[0] * (1.0 + step_value) / (4.0 + step_value)
    rates = jnp.stack([momentum_coef[0], learn_rate[0], decay_now])
    run = one_per_owner if direct else any_size
    result, grad_rows, *outputs = run(
        place, tokens[0], cotangent[0], dataset_ids, query_counts + CTX, masters, moments, averages,
        rates,
    )
    return (result[None], grad_rows[None], *outputs)


def solution(mesh):
    rows = P(AXES, None, None)
    weight = P(None, AXES, None)
    vector = P(None, None, AXES)
    scalar = P()
    return jax.shard_map(
        shards,
        mesh=mesh,
        in_specs=(rows, rows, P(AXES), P(AXES), *[scalar] * 4, *[weight] * 12, *[vector] * 6),
        out_specs=(rows, rows, *[weight] * 16, *[vector] * 8),
        check_vma=False,
    )
```

```python
import functools

import jax
import jax.numpy as jnp
import numpy as np
from jax import lax
from jax.experimental import pallas as pl
from jax.experimental.pallas import tpu as pltpu
from jax.sharding import PartitionSpec as P

HEADS = 4
CTX = 896
NDS = 8
EPS = 1e-05
OWNERS = 32
AXES = ("dp", "fsdp")

CHAIN = (0, 4, 2, 6)
SQUARE = (0, 1, 16, 17)
CORE = 8
ORDER = tuple(core ^ side ^ link for core in (0, CORE) for side in SQUARE for link in CHAIN)

FIRST_ROWS = 56
SECOND_ROWS = 88

ROW_BLOCK = 512
BACK_BLOCK = 256
ROOT_HALF = 0.7071067811865476
PDF_PEAK = 0.3989422804014327
VMEM_LIMIT = 60 * 1024 * 1024
SMALL_LIMIT = 12 * 1024 * 1024
FLOAT = jnp.float32
HALF = jnp.bfloat16
LIKE = jax.ShapeDtypeStruct


def product(left, right, left_dim, right_dim):
    return lax.dot_general(
        left, right, (((left_dim,), (right_dim,)), ((), ())), preferred_element_type=FLOAT
    )


def owner_rows(offset, place, rows):
    return pl.ds(pl.multiple_of((offset ^ place) * rows, rows), rows)


def params(limit=VMEM_LIMIT):
    return pltpu.CompilerParams(vmem_limit_bytes=limit)


def pack_kernel(place_ref, ids_ref, attend_ref, output_ref, expand_ref, shrink_ref, gains_ref,
                bias_ref, *outs):
    *outs, small = outs
    width = small.shape[1]
    each = gains_ref.shape[2]
    lane = lax.broadcasted_iota(jnp.int32, (each, width), 1)
    own = lax.broadcasted_iota(jnp.int32, (each, width), 0) + place_ref[0] * each
    pick = (lane == own).astype(HALF)
    lanes = lax.broadcasted_iota(jnp.int32, (1, width), 1)

    for layer in range(attend_ref.shape[0]):
        first, top, second = (outs[0], 0, outs[1]) if layer == 0 else (outs[1], SECOND_ROWS, outs[2])
        gains = product(gains_ref[layer].astype(HALF), pick, 1, 0)
        biases = product(bias_ref[layer].astype(HALF), pick, 1, 0)
        for piece in range(3):
            first[top + piece * 16 : top + (piece + 1) * 16, :] = attend_ref[
                layer, :, piece * width : (piece + 1) * width
            ].astype(HALF)
        small[...] = jnp.zeros_like(small)
        small[0:2, :] = biases[0:2, :]
        small[2:3, :] = (lanes == ids_ref[0]).astype(FLOAT)
        first[top + 48 : top + 56, :] = small[...].astype(HALF)
        second[0:16, :] = output_ref[layer].astype(HALF)
        for piece in range(2):
            second[(piece + 1) * 16 : (piece + 2) * 16, :] = expand_ref[
                layer, :, piece * width : (piece + 1) * width
            ].astype(HALF)
        second[48:80, :] = shrink_ref[layer].astype(HALF)
        small[0:2, :] = gains
        small[2:8, :] = biases[2:8, :]
        second[80:88, :] = small[...].astype(HALF)


def pack_call(place, ids, masters):
    width = masters[1].shape[2]
    rows = (FIRST_ROWS, SECOND_ROWS + FIRST_ROWS, SECOND_ROWS)
    return pl.pallas_call(
        pack_kernel,
        in_specs=[pl.BlockSpec(memory_space=pltpu.SMEM)] * 2
        + [pl.BlockSpec(memory_space=pltpu.VMEM)] * 6,
        out_specs=[pl.BlockSpec(memory_space=pltpu.VMEM)] * len(rows),
        out_shape=[LIKE((count, width), HALF) for count in rows],
        scratch_shapes=[pltpu.VMEM((8, width), FLOAT)],
        compiler_params=params(),
        cost_estimate=pl.CostEstimate(flops=0, bytes_accessed=1 << 20, transcendentals=0),
        name="pack",
    )(place, ids, *masters)


def join_kernel(cuts, count, *refs):
    each = refs[count].shape[0] // count
    for at in range(count):
        for to, (start, rows) in enumerate(cuts):
            target = refs[count + to]
            if len(refs[at].shape) == 2:
                target[at] = refs[at][start : start + rows, :]
            else:
                target[at * each : (at + 1) * each] = refs[at][:, start : start + rows, :]


def join_call(blocks, *cuts):
    *head, rows, width = blocks[0].shape
    slots = len(blocks) * (head[0] if head else 1)
    cuts = cuts or ((0, rows),)
    return pl.pallas_call(
        functools.partial(join_kernel, cuts, len(blocks)),
        out_shape=[LIKE((slots, rows, width), HALF) for _, rows in cuts],
        compiler_params=params(SMALL_LIMIT),
        cost_estimate=pl.CostEstimate(flops=0, bytes_accessed=1 << 20, transcendentals=0),
        name="join",
    )(*blocks)


def block_sum(refs):
    total = refs[0][...].astype(FLOAT)
    for ref in refs[1:]:
        total = total + ref[...].astype(FLOAT)
    return total


def core_sum(kept, got):
    return [
        (kept[at : at + 4].astype(FLOAT) + got[at : at + 4].astype(FLOAT)).astype(HALF)
        for at in range(0, 16, 4)
    ]


def core_sums_kernel(*refs):
    *sources, one, two, three, four = refs
    for to, out in enumerate((one, two, three, four)):
        start = 0
        for at in range(0, len(sources), 2):
            kept, got = (ref[4 * to : 4 * to + 4].astype(FLOAT) for ref in sources[at : at + 2])
            out[:, start : start + kept.shape[1], :] = (kept + got).astype(HALF)
            start += kept.shape[1]


def core_sums_call(*pieces):
    rows = sum(piece.shape[1] for piece in pieces[::2])
    return pl.pallas_call(
        core_sums_kernel,
        out_shape=[LIKE((4, rows, pieces[0].shape[2]), HALF)] * 4,
        compiler_params=params(SMALL_LIMIT),
        cost_estimate=pl.CostEstimate(flops=0, bytes_accessed=1 << 22, transcendentals=0),
        name="core_sums",
    )(*pieces)


def square_sum_kernel(rows, *refs):
    outs = refs[4 * len(rows) :]
    start = 0
    for at, count in enumerate(rows):
        total = block_sum(refs[4 * at : 4 * at + 4]).astype(HALF)
        for to in range(4):
            each = 4 // len(outs)
            if each == 1:
                outs[to][start : start + count, :] = total[to]
            else:
                outs[to // each][to % each, start : start + count, :] = total[to]
        start += count


def square_sum_call(*pieces, halves=True):
    rows = tuple(stacks[0].shape[1] for stacks in pieces)
    shape = (sum(rows), pieces[0][0].shape[2])
    return pl.pallas_call(
        functools.partial(square_sum_kernel, rows),
        out_shape=[LIKE((2, *shape), HALF)] * 2 if halves else [LIKE(shape, HALF)] * 4,
        compiler_params=params(SMALL_LIMIT),
        cost_estimate=pl.CostEstimate(flops=0, bytes_accessed=1 << 21, transcendentals=0),
        name="square_sum",
    )(*[stack for stacks in pieces for stack in stacks])


def pair_sum(kept, got):
    return [(kept[at].astype(FLOAT) + got[at].astype(FLOAT)).astype(HALF) for at in range(2)]


def swap(block, offset):
    return lax.ppermute(block, AXES, [(one, one ^ offset) for one in range(OWNERS)])


def swaps(block, offsets):
    return [swap(block, offset) for offset in offsets]


def slot_places(slot_refs):
    for at, offset in enumerate(ORDER):
        yield slot_refs[at // 4], at % 4, offset


def small_rows(slot_refs, start):
    total = None
    for slots in slot_refs:
        for at in range(slots.shape[0]):
            block = slots[at, start : start + 8, :].astype(FLOAT)
            total = block if total is None else total + block
    return total


def attend_kernel(place_ref, x_ref, *refs):
    slot_refs = refs[:8]
    joint_ref, probs_ref, mixed_ref, weight_ref, small_ref = refs[8:]
    count = joint_ref.shape[0]
    head_size = joint_ref.shape[2] // 3
    place = place_ref[0]

    for slots, at, offset in slot_places(slot_refs):
        rows = owner_rows(offset, place, 16)
        for piece in range(3):
            for head in range(count):
                weight_ref[head, rows, piece * head_size : (piece + 1) * head_size] = slots[
                    at, piece * 16 : (piece + 1) * 16, head * head_size : (head + 1) * head_size
                ]
    zeros = jnp.zeros((1, head_size), FLOAT)
    small = small_rows(slot_refs, 48)
    small_ref[...] = small
    factor = head_size ** (-0.5) * 1.4426950408889634
    weights = jnp.concatenate([weight_ref[head] for head in range(count)], axis=1)
    wide = product(x_ref[...], weights, 1, 0)
    for head in range(count):
        own = slice(head * head_size, (head + 1) * head_size)
        shift = jnp.concatenate([small[0:1, own], zeros, small[1:2, own]], axis=1)
        part = wide[:, 3 * head * head_size : 3 * (head + 1) * head_size]
        joint_ref[head] = (part + shift).astype(HALF)
    scores = []
    for head in range(count):
        keys = joint_ref[head, :CTX, head_size : 2 * head_size]
        scores.append(product(keys, joint_ref[head, :, :head_size], 1, 1))
    for head in range(count):
        values_turned = jnp.transpose(joint_ref[head, :CTX, 2 * head_size :])
        top = jnp.max(scores[head], axis=0, keepdims=True)
        grown = jnp.exp2((scores[head] - top) * factor)
        total = jnp.sum(grown, axis=0, keepdims=True)
        probs = (grown * (1.0 / total)).astype(HALF)
        probs_ref[head] = probs
        mixed_ref[:, head * head_size : (head + 1) * head_size] = jnp.transpose(
            product(values_turned, probs, 1, 0)
        ).astype(HALF)


def attend_call(place, x, slots):
    rows, width = x.shape
    head_size = width // HEADS
    return pl.pallas_call(
        attend_kernel,
        grid_spec=pltpu.PrefetchScalarGridSpec(
            num_scalar_prefetch=1,
            grid=(HEADS // 2,),
            in_specs=[pl.BlockSpec((rows, width), lambda h, p: (0, 0))]
            + [pl.BlockSpec((part.shape[0], FIRST_ROWS, 2 * head_size), lambda h, p: (0, 0, h))
               for part in slots],
            out_specs=[
                pl.BlockSpec((2, rows, 3 * head_size), lambda h, p: (h, 0, 0)),
                pl.BlockSpec((2, CTX, rows), lambda h, p: (h, 0, 0)),
                pl.BlockSpec((rows, 2 * head_size), lambda h, p: (0, h)),
                pl.BlockSpec((2, width, 3 * head_size), lambda h, p: (h, 0, 0)),
                pl.BlockSpec((8, 2 * head_size), lambda h, p: (0, h)),
            ],
        ),
        out_shape=[
            LIKE((HEADS, rows, 3 * head_size), HALF),
            LIKE((HEADS, CTX, rows), HALF),
            LIKE((rows, HEADS * head_size), HALF),
            LIKE((HEADS, width, 3 * head_size), HALF),
            LIKE((8, width), FLOAT),
        ],
        compiler_params=params(),
        cost_estimate=pl.CostEstimate(
            flops=HEADS * (2 * rows * width * 3 * head_size + 4 * rows * CTX * head_size),
            bytes_accessed=HEADS * 4 * 1024 * 1024,
            transcendentals=HEADS * rows * CTX,
        ),
        name="attend",
    )(place, x, *slots)


def unpack_second(place, slot_refs, output_w, expand_w, shrink_w, vec_ref):
    width = output_w.shape[1]
    for slots, at, offset in slot_places(slot_refs):
        rows = owner_rows(offset, place, 16)
        output_w[rows, :] = slots[at, 0:16, :]
        expand_w[rows, :width] = slots[at, 16:32, :]
        expand_w[rows, width:] = slots[at, 32:48, :]
        shrink_w[owner_rows(offset, place, 32), :] = slots[at, 48:80, :]
    vec_ref[...] = small_rows(slot_refs, 80)


def row_mean(rows):
    return jnp.mean(rows, axis=-1, keepdims=True)


def normalize(rows):
    centred = rows - row_mean(rows)
    inv_std = lax.rsqrt(row_mean(centred * centred) + EPS)
    return (centred * inv_std, inv_std)


def forward_rows(x_ref, mixed_ref, vec_ref, output_w, expand_w, shrink_w):
    attn_out = product(mixed_ref[...], output_w[...], 1, 0) + vec_ref[2:3, :]
    unit_one, inv_one = normalize(x_ref[...].astype(FLOAT) + attn_out)
    first_norm = unit_one * vec_ref[0:1, :] + vec_ref[4:5, :]
    first_low = first_norm.astype(HALF)
    shift = jnp.concatenate([vec_ref[6:7, :], vec_ref[7:8, :]], axis=1)
    hidden = product(first_low, expand_w[...], 1, 0) + shift
    normal_cdf = 0.5 * (1.0 + lax.erf(hidden * ROOT_HALF))
    act_low = (hidden * normal_cdf).astype(HALF)
    slope = normal_cdf + hidden * (jnp.exp(-0.5 * hidden * hidden) * PDF_PEAK)
    branch = product(act_low, shrink_w[...], 1, 0) + vec_ref[3:4, :]
    unit_two, inv_two = normalize(first_norm + branch)
    result = unit_two * vec_ref[1:2, :] + vec_ref[5:6, :]
    return (unit_one, inv_one, first_low, act_low, slope, unit_two, inv_two, result)


def column_sum(rows):
    return jnp.sum(rows, axis=0, keepdims=True)


def backward_rows(grad_rows, mixed_ref, vec_ref, kept, output_w, expand_w, shrink_w,
                  grad_mixed_ref, grad_one_ref, grad_output, grad_expand, grad_shrink, sums):
    unit_one, inv_one, first_low, act_low, slope, unit_two, inv_two = kept
    width = grad_rows.shape[1]

    def layer_norm_back(rows, unit_rows, inv_std, gain):
        scaled = rows * gain
        return inv_std * (scaled - row_mean(scaled) - unit_rows * row_mean(scaled * unit_rows))

    grad_two = layer_norm_back(grad_rows, unit_two, inv_two, vec_ref[1:2, :])
    branch_low = grad_two.astype(HALF)
    grad_shrink[...] += product(act_low, branch_low, 0, 0)
    grad_hidden = (product(branch_low, shrink_w[...], 1, 1) * slope).astype(HALF)
    grad_expand[...] += product(first_low, grad_hidden, 0, 0)
    grad_first = grad_two + product(grad_hidden, expand_w[...], 1, 1)
    grad_one = layer_norm_back(grad_first, unit_one, inv_one, vec_ref[0:1, :])
    attn_low = grad_one.astype(HALF)
    grad_output[...] += product(mixed_ref[...], attn_low, 0, 0)
    grad_mixed_ref[...] = product(attn_low, output_w[...], 1, 1).astype(HALF)
    grad_one_ref[...] = grad_one
    sums[0:1, :] += column_sum(grad_first * unit_one)
    sums[1:2, :] += column_sum(grad_rows * unit_two)
    sums[2:3, :] += column_sum(attn_low.astype(FLOAT))
    sums[3:4, :] += column_sum(branch_low.astype(FLOAT))
    sums[4:5, :] += column_sum(grad_first)
    sums[5:6, :] += column_sum(grad_rows)
    hidden_sum = column_sum(grad_hidden.astype(FLOAT))
    sums[6:7, :] += hidden_sum[:, :width]
    sums[7:8, :] += hidden_sum[:, width:]


def pack_second(place, kept_ref, sent_ref, grad_output, grad_expand, grad_shrink, sums):
    width = grad_output.shape[1]
    small = sums[...].astype(HALF)
    for at, offset in enumerate(ORDER):
        slots_ref = kept_ref if at < 16 else sent_ref
        at = at % 16
        rows = owner_rows(offset, place, 16)
        slots_ref[at, 0:16, :] = grad_output[rows, :].astype(HALF)
        slots_ref[at, 16:32, :] = grad_expand[rows, :width].astype(HALF)
        slots_ref[at, 32:48, :] = grad_expand[rows, width:].astype(HALF)
        slots_ref[at, 48:80, :] = grad_shrink[owner_rows(offset, place, 32), :].astype(HALF)
        slots_ref[at, 80:88, :] = small


def dense_kernel(place_ref, x_ref, mixed_ref, *refs):
    slot_refs = refs[:8]
    (result_ref, unit_one_ref, inv_one_ref, act_ref, slope_ref, unit_two_ref, inv_two_ref, output_w,
     expand_w, shrink_w, vec_ref) = refs[8:]

    @pl.when(pl.program_id(0) == 0)
    def _():
        unpack_second(place_ref[0], slot_refs, output_w, expand_w, shrink_w, vec_ref)

    unit_one, inv_one, _, act_low, slope, unit_two, inv_two, result = forward_rows(
        x_ref, mixed_ref, vec_ref, output_w, expand_w, shrink_w
    )
    result_ref[...] = result.astype(HALF)
    unit_one_ref[...] = unit_one
    inv_one_ref[...] = inv_one
    act_ref[...] = act_low
    slope_ref[...] = slope
    unit_two_ref[...] = unit_two
    inv_two_ref[...] = inv_two


def grad_x_rows(grad_one_ref, grad_joint_ref, weight_ref):
    total = grad_one_ref[...]
    for head in range(weight_ref.shape[0]):
        total = total + product(grad_joint_ref[head], weight_ref[head], 1, 1)
    return total


def clear(*items):
    for item in items:
        item[...] = jnp.zeros_like(item)


def dense_back_kernel(place_ref, grad_one_next, grad_joint_next, weight_next, mixed_ref, *refs):
    (unit_one_ref, inv_one_ref, act_ref, slope_ref, unit_two_ref, inv_two_ref, output_w, expand_w,
     shrink_w, vec_ref, grad_mixed_ref, grad_one_ref, kept_ref, sent_ref, sums, grad_output,
     grad_expand, grad_shrink) = refs

    @pl.when(pl.program_id(0) == 0)
    def _():
        clear(sums, grad_output, grad_expand, grad_shrink)

    unit_one = unit_one_ref[...]
    first_low = (unit_one * vec_ref[0:1, :] + vec_ref[4:5, :]).astype(HALF)
    kept = (unit_one, inv_one_ref[...], first_low, act_ref[...], slope_ref[...], unit_two_ref[...],
            inv_two_ref[...])
    grad_rows = grad_x_rows(grad_one_next, grad_joint_next, weight_next)
    backward_rows(grad_rows, mixed_ref, vec_ref, kept, output_w, expand_w, shrink_w,
                  grad_mixed_ref, grad_one_ref, grad_output, grad_expand, grad_shrink, sums)

    @pl.when(pl.program_id(0) == pl.num_programs(0) - 1)
    def _():
        pack_second(place_ref[0], kept_ref, sent_ref, grad_output, grad_expand, grad_shrink, sums)


def dense_turn_kernel(place_ref, live_ref, ids_ref, x_ref, mixed_ref, *refs):
    slot_refs = refs[:8]
    (counts_ref, cot_ref, result_ref, grad_mixed_ref, grad_one_ref, kept_ref, sent_ref, output_w, expand_w,
     shrink_w, vec_ref, grad_output, grad_expand, grad_shrink, sums) = refs[8:]
    step = pl.program_id(0)

    @pl.when(step == 0)
    def _():
        unpack_second(place_ref[0], slot_refs, output_w, expand_w, shrink_w, vec_ref)
        clear(sums, grad_output, grad_expand, grad_shrink)

    *kept, result = forward_rows(x_ref, mixed_ref, vec_ref, output_w, expand_w, shrink_w)
    result_ref[...] = result.astype(HALF)
    counts = counts_ref[2:3, :]
    lanes = lax.broadcasted_iota(jnp.int32, counts.shape, 1)
    own_count = jnp.sum(jnp.where(lanes == ids_ref[0], counts, 0.0), axis=1, keepdims=True)
    row_weight = jnp.sum(counts, axis=1, keepdims=True) / (NDS * own_count)
    rows = cot_ref.shape[0]
    slot = lax.broadcasted_iota(jnp.int32, (rows, 1), 0) + step * rows
    grad_rows = cot_ref[...].astype(FLOAT) * jnp.where(slot < live_ref[0], row_weight, 0.0)
    backward_rows(grad_rows, mixed_ref, vec_ref, kept, output_w, expand_w, shrink_w,
                  grad_mixed_ref, grad_one_ref, grad_output, grad_expand, grad_shrink, sums)

    @pl.when(step == pl.num_programs(0) - 1)
    def _():
        pack_second(place_ref[0], kept_ref, sent_ref, grad_output, grad_expand, grad_shrink, sums)


def by_rows(width, block=ROW_BLOCK):
    return pl.BlockSpec((block, width), lambda i, *p: (i, 0))


def fixed(*shape):
    return pl.BlockSpec(shape, lambda i, *p: (0,) * len(shape))


def joint_rows(grad_joint, block=ROW_BLOCK):
    heads, _, width = grad_joint.shape
    return pl.BlockSpec((heads, block, width), lambda i, *p: (0, i, 0))


def weight_shapes(width):
    return [(width, width), (width, 2 * width), (2 * width, width)]


def dense_call(place, x, mixed, slots):
    rows, width = x.shape
    weights = weight_shapes(width)
    return pl.pallas_call(
        dense_kernel,
        grid_spec=pltpu.PrefetchScalarGridSpec(
            num_scalar_prefetch=1,
            grid=(rows // ROW_BLOCK,),
            in_specs=[by_rows(width)] * 2
            + [fixed(*part.shape) for part in slots],
            out_specs=[by_rows(width), by_rows(width), by_rows(1), by_rows(2 * width),
                       by_rows(2 * width), by_rows(width), by_rows(1)]
            + [fixed(*shape) for shape in weights]
            + [fixed(8, width)],
        ),
        out_shape=[LIKE((rows, width), HALF), LIKE((rows, width), FLOAT), LIKE((rows, 1), FLOAT),
                   LIKE((rows, 2 * width), HALF), LIKE((rows, 2 * width), FLOAT),
                   LIKE((rows, width), FLOAT), LIKE((rows, 1), FLOAT)]
        + [LIKE(shape, HALF) for shape in weights]
        + [LIKE((8, width), FLOAT)],
        compiler_params=params(),
        cost_estimate=pl.CostEstimate(
            flops=10 * rows * width * width, bytes_accessed=16 * 1024 * 1024,
            transcendentals=4 * rows * width,
        ),
        name="dense",
    )(place, x, mixed, *slots)


def dense_back_call(place, grad_one, grad_joint, weight, mixed, kept):
    rows, width = grad_one.shape
    weights = weight_shapes(width)
    some_rows = functools.partial(by_rows, block=BACK_BLOCK)
    return pl.pallas_call(
        dense_back_kernel,
        grid_spec=pltpu.PrefetchScalarGridSpec(
            num_scalar_prefetch=1,
            grid=(rows // BACK_BLOCK,),
            in_specs=[some_rows(width), joint_rows(grad_joint, BACK_BLOCK), fixed(*weight.shape), some_rows(width)]
            + [some_rows(width), some_rows(1), some_rows(2 * width), some_rows(2 * width), some_rows(width),
               some_rows(1)]
            + [fixed(*shape) for shape in weights]
            + [fixed(8, width)],
            out_specs=[some_rows(width), some_rows(width)] + [fixed(16, SECOND_ROWS, width)] * 2,
            scratch_shapes=[pltpu.VMEM((8, width), FLOAT)]
            + [pltpu.VMEM(shape, FLOAT) for shape in weights],
        ),
        out_shape=[LIKE((rows, width), HALF), LIKE((rows, width), FLOAT)]
        + [LIKE((16, SECOND_ROWS, width), HALF)] * 2,
        compiler_params=params(),
        cost_estimate=pl.CostEstimate(
            flops=26 * rows * width * width, bytes_accessed=20 * 1024 * 1024, transcendentals=0
        ),
        name="dense_back",
    )(place, grad_one, grad_joint, weight, mixed, *kept)


def dense_turn_call(place, live, ids, x, mixed, slots, small, cotangent):
    rows, width = x.shape
    weights = weight_shapes(width)
    return pl.pallas_call(
        dense_turn_kernel,
        grid_spec=pltpu.PrefetchScalarGridSpec(
            num_scalar_prefetch=3,
            grid=(rows // ROW_BLOCK,),
            in_specs=[by_rows(width)] * 2
            + [fixed(*part.shape) for part in slots]
            + [fixed(8, width), by_rows(width)],
            out_specs=[by_rows(width)] * 3 + [fixed(16, SECOND_ROWS, width)] * 2,
            scratch_shapes=[pltpu.VMEM(shape, HALF) for shape in weights]
            + [pltpu.VMEM((8, width), FLOAT)]
            + [pltpu.VMEM(shape, FLOAT) for shape in weights]
            + [pltpu.VMEM((8, width), FLOAT)],
        ),
        out_shape=[LIKE((rows, width), HALF), LIKE((rows, width), HALF), LIKE((rows, width), FLOAT)]
        + [LIKE((16, SECOND_ROWS, width), HALF)] * 2,
        compiler_params=params(),
        cost_estimate=pl.CostEstimate(
            flops=30 * rows * width * width, bytes_accessed=16 * 1024 * 1024,
            transcendentals=4 * rows * width,
        ),
        name="dense_turn",
    )(place, live, ids, x, mixed, *slots, small, cotangent)


def attend_back_kernel(place_ref, x_ref, joint_ref, probs_ref, grad_mixed_ref, kept_ref, sent_ref,
                       grad_joint_ref, grad_scores, small):
    grad_joint = grad_joint_ref.at[0]
    rows = x_ref.shape[0]
    head_size = grad_mixed_ref.shape[1]
    place = place_ref[0]

    @pl.when(pl.program_id(0) == 0)
    def _():
        clear(small)

    grad_joint[CTX:, head_size:] = jnp.zeros((rows - CTX, 2 * head_size), HALF)
    keys = joint_ref[0, :CTX, head_size : 2 * head_size]
    values = joint_ref[0, :CTX, 2 * head_size :]
    keys_turned = jnp.transpose(keys)
    factor = head_size ** (-0.5)
    grad_probs = product(values, grad_mixed_ref[...], 1, 1)
    probs = probs_ref[0].astype(FLOAT)
    level = column_sum(probs * grad_probs)
    grad_low = (probs * (grad_probs - level)).astype(HALF)
    grad_scores[...] = grad_low
    grad_joint[:, :head_size] = jnp.transpose(factor * product(keys_turned, grad_low, 1, 0)).astype(
        HALF
    )
    grad_joint[:CTX, head_size : 2 * head_size] = (
        factor * product(grad_scores[...], joint_ref[0, :, :head_size], 1, 0)
    ).astype(HALF)
    grad_joint[:CTX, 2 * head_size :] = product(probs_ref[0], grad_mixed_ref[...], 1, 0).astype(HALF)
    sums = column_sum(grad_joint[...].astype(FLOAT))
    small[0:1, :] = sums[:, :head_size]
    small[1:2, :] = sums[:, 2 * head_size :]
    small_low = small[...].astype(HALF)
    grad_low = product(x_ref[...], grad_joint[...], 0, 0).astype(HALF)
    holder = grad_scores
    holder[: grad_low.shape[0], : 3 * head_size] = grad_low
    for at, offset in enumerate(ORDER):
        slots_ref = kept_ref if at < 16 else sent_ref
        at = at % 16
        span = owner_rows(offset, place, 16)
        for piece in range(3):
            slots_ref[at, piece * 16 : (piece + 1) * 16, :] = holder[
                span, piece * head_size : (piece + 1) * head_size
            ]
        slots_ref[at, 48:56, :] = small_low


def attend_back_call(place, x, joint, probs, grad_mixed):
    rows, width = x.shape
    head_size = width // HEADS
    return pl.pallas_call(
        attend_back_kernel,
        grid_spec=pltpu.PrefetchScalarGridSpec(
            num_scalar_prefetch=1,
            grid=(HEADS,),
            in_specs=[
                pl.BlockSpec((rows, width), lambda h, p: (0, 0)),
                pl.BlockSpec((1, rows, 3 * head_size), lambda h, p: (h, 0, 0)),
                pl.BlockSpec((1, CTX, rows), lambda h, p: (h, 0, 0)),
                pl.BlockSpec((rows, head_size), lambda h, p: (0, h)),
            ],
            out_specs=[pl.BlockSpec((16, FIRST_ROWS, head_size), lambda h, p: (0, 0, h))] * 2
            + [pl.BlockSpec((1, rows, 3 * head_size), lambda h, p: (h, 0, 0))],
            scratch_shapes=[pltpu.VMEM((CTX, rows), HALF), pltpu.VMEM((8, head_size), FLOAT)],
        ),
        out_shape=[LIKE((16, FIRST_ROWS, width), HALF)] * 2
        + [LIKE((HEADS, rows, 3 * head_size), HALF)],
        compiler_params=params(),
        cost_estimate=pl.CostEstimate(
            flops=HEADS * (6 * rows * width * head_size + 8 * rows * CTX * head_size),
            bytes_accessed=HEADS * 4 * 1024 * 1024, transcendentals=0,
        ),
        name="attend_back",
    )(place, x, joint, probs, grad_mixed)


def grad_x_kernel(grad_one_ref, grad_joint_ref, weight_ref, grad_x_ref):
    grad_x_ref[...] = grad_x_rows(grad_one_ref, grad_joint_ref, weight_ref)


def grad_x_call(grad_one, grad_joint, weight):
    rows, width = grad_one.shape
    return pl.pallas_call(
        grad_x_kernel,
        grid=(rows // ROW_BLOCK,),
        in_specs=[
            by_rows(width),
            joint_rows(grad_joint),
            fixed(*weight.shape),
        ],
        out_specs=by_rows(width),
        out_shape=LIKE((rows, width), FLOAT),
        compiler_params=params(),
        cost_estimate=pl.CostEstimate(
            flops=6 * rows * width * width, bytes_accessed=10 * 1024 * 1024, transcendentals=0
        ),
        name="grad_x",
    )(grad_one, grad_joint, weight)


def advance(master, moment, average, grad, momentum, step_rate, decay_now):
    new_moment = momentum * moment + grad
    new_master = master - step_rate * (grad + momentum * new_moment)
    new_average = decay_now * average + (1.0 - decay_now) * new_master
    return (new_moment, new_average, new_master, new_master.astype(HALF))


def stepper(rates_ref, state_refs, out_refs):
    rates = [rates_ref[at] for at in range(3)]

    def step(weight, where, grad):
        state = [ref[where] for ref in state_refs[3 * weight : 3 * weight + 3]]
        for ref, item in zip(out_refs[4 * weight : 4 * weight + 4], advance(*state, grad, *rates)):
            ref[where] = item

    return step


def second_step_kernel(rates_ref, *refs):
    middle, late = block_sum(refs[:2]), block_sum(refs[2:4])
    state_refs, out_refs, (first_ref, small_ref) = refs[4:13], refs[13:25], refs[25:]
    width = small_ref.shape[2]
    step = stepper(rates_ref, state_refs, out_refs)
    for layer, piece in enumerate((middle[FIRST_ROWS:], late)):
        step(0, (layer,), piece[0:16])
        step(1, (layer, slice(None), slice(0, width)), piece[16:32])
        step(1, (layer, slice(None), slice(width, 2 * width)), piece[32:48])
        step(2, (layer,), piece[48:80])
        small_ref[layer] = piece[80:88]
    first_ref[...] = middle[:FIRST_ROWS]


def step_shapes(masters):
    return [
        LIKE(master.shape, kind) for master in masters for kind in (FLOAT, FLOAT, FLOAT, HALF)
    ]


def step_call(kernel, rates, inputs, out_shape, name):
    return pl.pallas_call(
        kernel,
        in_specs=[pl.BlockSpec(memory_space=pltpu.SMEM)] * len(rates)
        + [pl.BlockSpec(memory_space=pltpu.VMEM)] * len(inputs),
        out_specs=[pl.BlockSpec(memory_space=pltpu.VMEM)] * len(out_shape),
        out_shape=out_shape,
        compiler_params=params(SMALL_LIMIT),
        cost_estimate=pl.CostEstimate(flops=0, bytes_accessed=1 << 22, transcendentals=0),
        name=name,
    )(*rates, *inputs)


def first_step_kernel(place_ref, rates_ref, small_ref, late_ref, *refs):
    blocks, state_refs, out_refs = refs[:4], refs[4:13], refs[13:]
    width = small_ref.shape[2]
    each = out_refs[4].shape[2]
    step = stepper(rates_ref, state_refs, out_refs)
    turn = width - place_ref[0] * each
    for layer, total in enumerate((block_sum(blocks), late_ref[...])):
        for piece in range(3):
            columns = slice(piece * width, (piece + 1) * width)
            step(0, (layer, slice(None), columns), total[piece * 16 : (piece + 1) * 16])
        own_first = pltpu.roll(total[48:56], turn, 1)[:, :each]
        own_second = pltpu.roll(small_ref[layer], turn, 1)[:, :each]
        step(1, (layer,), own_second[0:2])
        step(2, (layer, slice(0, 2)), own_first[0:2])
        step(2, (layer, slice(2, 8)), own_second[2:8])


def wide_to_rows(shard, width):
    return jnp.concatenate(
        [shard[:, at * width : (at + 1) * width] for at in range(shard.shape[1] // width)]
    )


def rows_to_wide(rows, pieces):
    each = rows.shape[0] // pieces
    return jnp.concatenate([rows[at * each : (at + 1) * each] for at in range(pieces)], axis=1)


def gather_rows(shards_by_part, small):
    width = small.shape[1]
    parts = []
    for shard in shards_by_part:
        whole = lax.all_gather(shard, AXES, axis=0, tiled=False)
        parts.append(whole.reshape(OWNERS, -1, width))
    smalls = jnp.broadcast_to(small[None] * (jnp.arange(OWNERS) == 0)[:, None, None].astype(HALF),
                              (OWNERS, *small.shape))
    slots = jnp.concatenate([*parts, smalls], axis=1)[np.array(ORDER)]
    return [slots[4 * at : 4 * at + 4] for at in range(8)]


def scatter_rows(kept, sent, parts):
    slots = jnp.concatenate([kept, sent])[np.argsort(np.array(ORDER))]
    everyone = lax.axis_size(AXES)
    own, start = [], 0
    for rows in parts:
        piece = slots[:, start : start + rows].reshape(everyone, -1, slots.shape[2])
        own.append(lax.psum_scatter(piece, AXES, scatter_dimension=0, tiled=False).astype(FLOAT))
        start += rows
    return own, lax.psum(slots[0, start:].astype(FLOAT), AXES)


def sync(*items):
    return lax.optimization_barrier(items)


def any_size(place, x, cotangent, dataset_ids, live, masters, moments, averages, rates):
    layers = masters[0].shape[0]
    width = x.shape[1]
    position = lax.axis_index(AXES)
    low = lambda item: item.astype(HALF)
    own = low(jnp.concatenate([masters[4], masters[5]], axis=1))
    wide = lax.all_gather(own, AXES, axis=2, tiled=True)
    onehot = (dataset_ids[0] == jnp.arange(width, dtype=jnp.int32)).astype(FLOAT)
    counts = low(lax.psum(onehot, AXES))[None]
    first, second = [], []
    for at in range(layers):
        pad = lambda rows: jnp.pad(rows, ((0, 8 - rows.shape[0]), (0, 0)))
        attend_w = masters[0][at]
        first.append(gather_rows(
            [low(attend_w[:, piece * width : (piece + 1) * width]) for piece in range(3)],
            pad(jnp.concatenate([wide[at, 2:4], counts])),
        ))
        expand_w = masters[2][at]
        second.append(gather_rows(
            [low(masters[1][at]), low(expand_w[:, :width]), low(expand_w[:, width:]),
             low(masters[3][at])],
            jnp.concatenate([wide[at, 0:2], wide[at, 4:10]]),
        ))
    current = x
    saved = []
    for at in range(layers):
        joint, probs, mixed, weight, small = attend_call(place, current, first[at])
        keep = (current, joint, probs, mixed, weight)
        if at + 1 < layers:
            current, *rest = dense_call(place, current, mixed, second[at])
            keep = (*keep, rest)
        saved.append(keep)
    counted = small
    first_grads, second_grads = [None] * layers, [None] * layers
    for at in reversed(range(layers)):
        start, joint, probs, mixed, weight = saved[at][:5]
        if at + 1 == layers:
            result, grad_mixed, grad_one, *slots = dense_turn_call(
                place, live, dataset_ids, start, mixed, second[at], counted, cotangent
            )
        else:
            grad_mixed, grad_one, *slots = dense_back_call(
                place, grad_one, grad_joint, saved[at + 1][4], mixed, saved[at][5]
            )
        second_grads[at] = slots
        *slots, grad_joint = attend_back_call(place, start, joint, probs, grad_mixed)
        first_grads[at] = slots
    grad_rows = grad_x_call(grad_one, grad_joint, weight)
    grads = [[] for _ in range(6)]
    for at in range(layers):
        kept, sent = first_grads[at]
        own, first_small = scatter_rows(kept, sent, (16, 16, 16))
        grads[0].append(jnp.concatenate(own, axis=1))
        own, small = scatter_rows(*second_grads[at], (16, 16, 16, 32))
        grads[1].append(own[0])
        grads[2].append(jnp.concatenate(own[1:3], axis=1))
        grads[3].append(own[3])
        rows = jnp.concatenate([small[0:2], first_small[0:2], small[2:8]])
        lanes = masters[4].shape[2]
        own_rows = lax.dynamic_slice(rows, (0, position * lanes), (10, lanes))
        grads[4].append(own_rows[:2])
        grads[5].append(own_rows[2:])
    outputs = []
    for master, moment, average, grad in zip(masters, moments, averages, grads):
        outputs.extend(
            advance(master, moment, average, jnp.stack(grad), rates[0], rates[1], rates[2])
        )
    return (result, grad_rows, *outputs)


def one_per_owner(place, x, cotangent, dataset_ids, live, masters, moments, averages, rates):
    width = x.shape[1]

    def to_core(stacks):
        return [swap(one, CORE) for one in stacks]

    def square(block):
        return swaps(block, SQUARE[1:])

    def square_back(stacks):
        return [swap(one, offset) for one, offset in zip(stacks[1:], SQUARE[1:])]

    def chain_back(blocks):
        return [swap(one, offset) for one, offset in zip(blocks[1:], CHAIN[1:])]

    first, following, late = pack_call(place, dataset_ids, masters)
    (first_own,) = join_call([first, *swaps(first, CHAIN[1:])])

    first_own, following = sync(first_own, following)
    first_near = [first_own, *square(first_own)]
    (following_two,) = join_call([following, swap(following, CHAIN[1])])
    second_own, third_own = join_call(
        [following_two, swap(following_two, CHAIN[2])],
        (0, SECOND_ROWS),
        (SECOND_ROWS, FIRST_ROWS),
    )
    first_far = to_core(first_near)

    first_far, second_own, third_own, x, late = sync(first_far, second_own, third_own, x, late)
    second_near = [second_own, *square(second_own)]
    second_far = [swap(second_own, CORE)]
    late_got = swap(late, CHAIN[1])
    joint, probs, mixed, weight, _ = attend_call(place, x, [*first_near, *first_far])

    mixed, second_near, second_far, third_own, late, late_got = sync(
        mixed, second_near, second_far, third_own, late, late_got
    )
    (late_two,) = join_call([late, late_got])
    second_far += to_core(second_near[1:])
    second_far, third_own, late_two, mixed = sync(second_far, third_own, late_two, mixed)
    third_near = [third_own, *square(third_own)]
    third_far = [swap(third_own, CORE)]
    late_got = swap(late_two, CHAIN[2])
    middle, *dense_kept = dense_call(place, x, mixed, [*second_near, *second_far])

    middle, third_near, third_far, late_two, late_got = sync(
        middle, third_near, third_far, late_two, late_got
    )
    third_far += to_core(third_near[1:])
    (late_own,) = join_call([late_two, late_got])
    third_far, late_own, middle = sync(third_far, late_own, middle)
    late_near = [late_own, *square(late_own)]
    late_far = [swap(late_own, CORE)]
    late_joint, late_probs, late_mixed, late_weight, small = attend_call(
        place, middle, [*third_near, *third_far]
    )

    late_mixed, late_near, late_far = sync(late_mixed, late_near, late_far)
    late_far += to_core(late_near[1:])
    result, grad_mixed, grad_one, kept, sent = dense_turn_call(
        place, live, dataset_ids, middle, late_mixed, [*late_near, *late_far], small, cotangent
    )

    sent, grad_mixed = sync(sent, grad_mixed)
    got = swap(sent, CORE)
    next_kept, next_sent, grad_joint = attend_back_call(
        place, middle, late_joint, late_probs, grad_mixed
    )

    got, next_sent, grad_joint = sync(got, next_sent, grad_joint)
    late_stacks = core_sum(kept, got)
    late_stacks, next_sent, grad_joint = sync(late_stacks, next_sent, grad_joint)
    late_got = square_back(late_stacks)
    got = swap(next_sent, CORE)
    grad_mixed, grad_one, kept, sent = dense_back_call(
        place, grad_one, grad_joint, late_weight, mixed, dense_kept
    )

    got, late_got, sent, grad_mixed = sync(got, late_got, sent, grad_mixed)
    late_kept, late_sent = square_sum_call([late_stacks[0], *late_got])
    stacks = core_sums_call(next_kept, got, kept, swap(sent, CORE))
    stacks, late_kept, late_sent, grad_mixed = sync(stacks, late_kept, late_sent, grad_mixed)
    middle_got = square_back(stacks)
    late_got = swap(late_sent, CHAIN[2])
    kept, sent, grad_joint = attend_back_call(place, x, joint, probs, grad_mixed)
    grad_rows = grad_x_call(grad_one, grad_joint, weight)

    middle_got, late_got, sent, grad_rows = sync(middle_got, late_got, sent, grad_rows)
    got = swap(sent, CORE)
    late_own, late_sent = pair_sum(late_kept, late_got)
    middle_kept, middle_sent = square_sum_call([stacks[0], *middle_got])
    middle_got = swap(middle_sent, CHAIN[2])
    late_got = swap(late_sent, CHAIN[1])
    stacks = core_sum(kept, got)
    got = square_back(stacks)
    middle_got, late_got, got[0] = sync(middle_got, late_got, got[0])
    middle_own, middle_sent = pair_sum(middle_kept, middle_got)
    middle_got = swap(middle_sent, CHAIN[1])

    def state_of(*which):
        return [item for at in which for item in (masters[at], moments[at], averages[at])]

    last_blocks = square_sum_call([stacks[0], *got], halves=False)
    last_got = chain_back(last_blocks)
    *stepped, late_first, small = step_call(
        second_step_kernel,
        [rates],
        [middle_own, middle_got, late_own, late_got, *state_of(1, 2, 3)],
        [*step_shapes(masters[1:4]), LIKE((FIRST_ROWS, width), FLOAT),
         LIKE((2, 8, width), FLOAT)],
        "second_step",
    )
    rest = step_call(
        first_step_kernel,
        [place, rates],
        [small, late_first, last_blocks[0], *last_got, *state_of(0, 4, 5)],
        step_shapes((masters[0], masters[4], masters[5])),
        "first_step",
    )
    return (result, grad_rows, *rest[:4], *stepped, *rest[4:])


def shards(
    tokens,
    cotangent,
    dataset_ids,
    query_counts,
    learn_rate,
    momentum_coef,
    average_decay,
    step_count,
    *state,
):
    masters, moments, averages = state[0::3], state[1::3], state[2::3]
    position = lax.axis_index(AXES)
    direct = lax.axis_size(AXES) == OWNERS
    place = (position if direct else jnp.zeros_like(position)).astype(jnp.int32).reshape(1)
    step_value = step_count[0].astype(FLOAT)
    decay_now = average_decay[0] * (1.0 + step_value) / (4.0 + step_value)
    rates = jnp.stack([momentum_coef[0], learn_rate[0], decay_now])
    run = one_per_owner if direct else any_size
    result, grad_rows, *outputs = run(
        place, tokens[0], cotangent[0], dataset_ids, query_counts + CTX, masters, moments, averages,
        rates,
    )
    return (result[None], grad_rows[None], *outputs)


def solution(mesh):
    rows = P(AXES, None, None)
    weight = P(None, AXES, None)
    vector = P(None, None, AXES)
    scalar = P()
    return jax.shard_map(
        shards,
        mesh=mesh,
        in_specs=(rows, rows, P(AXES), P(AXES), *[scalar] * 4, *[weight] * 12, *[vector] * 6),
        out_specs=(rows, rows, *[weight] * 16, *[vector] * 8),
        check_vma=False,
    )
```
